768 devices in a mesh: dom: 64 (over y, z_hi, x), band: 12 (over z_lo, core).
Axes of the slice: x: 4, y: 8, z: 12 (z_hi: 2, z_lo: 6; z = z_hi * 6 + z_lo), core: 2. Of those that a mesh axis runs over, the one named last changes fastest.
Arguments:
- states: float32 [12, 884736], P('band', 'dom'), may hold values from -6 to 6
- previous: float32 [12, 884736], P('band', 'dom'), may hold values from -6 to 6
- potential: float32 [884736], P('dom'), may hold values from -1 to 1
- screening: float32 [884736], P('dom'), may hold values from 0.25 to 1
- occupation: float32 [12], P('band'), may hold values from 0.1 to 2
- cell_scale: float32 [4096], P('dom'), may hold values from 0.5 to 2
- cell_matrix: float32 [343, 343], replicated, as said below
- connectivity: int32 [343, 4096], P(None, 'dom'), may hold values from 0 to 16806, as said below
Outputs:
- filtered: float32 [12, 884736], P('band', 'dom')
- potential_field: float32 [884736], P('dom')
The draws below stay inside these ranges and needn't reach their ends.
Inputs may be any that keep to these rules, and one draw needn't show every extreme that they name: `connectivity`: each column lists the 343 nodes of one cell as ids into its partition's extended box, in the order (k, j, i) with i fastest, each of k, j, i running over 0 to 6; the cell spans nodes 6 cz to 6 cz + 6 along z and likewise along y and x. The columns of one partition are its 64 cells in some order. `cell_matrix`: symmetric positive definite.
All inputs are finite; a program needn't handle non-finite values.
Results may differ from the reference program's by a relative error of at most 0.0001.
Values sent between devices are 32-bit elements; how exact they have to be, the bound alone decides.
A program may use at most 32 MiB of HBM per device.

```python
import math
import jax
import jax.numpy as jnp
from jax import lax

DEG = 6
NPC = 343
CPX = 8
CPY = 8
ITERS = 3
OX = 48
OY = 48
OZ = 6
NEXT = 16807
CELL_DEV = 64
PGY = 4
PGZ = 4
PGX = 4
NODES = 884736
CELLS = 4096
STATES = 12
N_DOM = 64


def draw_cell_matrix(key, part):
    base = jax.random.normal(key, (NPC, NPC), jnp.float32)
    product = jnp.dot(base, base.T, precision=lax.Precision.HIGHEST) / NPC
    return 0.5 * (product + product.T) + 0.5 * jnp.eye(NPC, dtype=jnp.float32)


def draw_connectivity(key, part):
    partitions = CELLS // CELL_DEV
    edge = DEG + 1
    row_x = OX + 1
    row_y = OY + 1
    cells = jnp.arange(CELL_DEV, dtype=jnp.int32)
    cell_x = cells % CPX
    cell_y = cells // CPX % CPY
    cell_z = cells // (CPX * CPY)
    nodes = jnp.arange(NPC, dtype=jnp.int32)
    node_x = nodes % edge
    node_y = nodes // edge % edge
    node_z = nodes // (edge * edge)
    grid_z = DEG * cell_z[None, :] + node_z[:, None]
    grid_y = DEG * cell_y[None, :] + node_y[:, None]
    grid_x = DEG * cell_x[None, :] + node_x[:, None]
    node_ids = (grid_z * row_y + grid_y) * row_x + grid_x
    orders = jax.vmap(lambda subkey: jax.random.permutation(subkey, CELL_DEV))(jax.random.split(key, partitions))
    table = node_ids[:, orders]
    return table.reshape(NPC, CELLS).astype(jnp.int32)


def block_scale(stream_key, shape, cuts, low, high):
    factor_of, own = 1.0, jax.random.fold_in(stream_key, 6)
    for axis_at, parts in cuts:
        steps = jnp.exp(jax.random.uniform(jax.random.fold_in(own, axis_at), (parts,), jnp.float32, low / len(cuts), high / len(cuts)))
        factor_of = factor_of * jnp.repeat(steps, shape[axis_at] // parts).reshape([-1 if axis == axis_at else 1 for axis in range(len(shape))])
    return factor_of


def centred(own_key, shape, scale, reach, cuts=(), held_as=jnp.bfloat16):
    array = scale * jax.random.normal(own_key, shape, jnp.float32)
    if cuts:
        array = array * block_scale(own_key, shape, cuts, -0.22, 0.18)
    return jnp.clip(array, -reach, reach).astype(held_as)


def setup_inputs(seed: int = 0) -> dict:
    key_list = jax.random.split(jax.random.key(seed), 9)
    return {
        "states": centred(key_list[0], (STATES, NODES), 1.0, 6.0, ((0, 12), (1, 64)), jnp.float32),
        "previous": centred(key_list[1], (STATES, NODES), 1.0, 6.0, ((0, 12), (1, 64)), jnp.float32),
        "potential": jnp.clip(jax.random.uniform(key_list[2], (NODES,), jnp.float32, -1.0, 1.0) * block_scale(key_list[2], (NODES,), ((0, 64),), -0.4, 0.0), -1.0, 1.0),
        "screening": jnp.clip(0.25 + 0.75 * jax.random.uniform(key_list[3], (NODES,), jnp.float32) ** block_scale(key_list[3], (NODES,), ((0, 64),), -0.2, 0.2), 0.25, 1.0),
        "occupation": jnp.clip(0.1 + 1.9 * jax.random.uniform(key_list[4], (STATES,), jnp.float32) ** block_scale(key_list[4], (STATES,), ((0, 12),), -0.2, 0.2), 0.1, 2.0),
        "cell_scale": jnp.clip(jnp.exp(math.log(2.0) - 1.3862944 * jax.random.uniform(key_list[5], (CELLS,), jnp.float32) ** block_scale(key_list[5], (CELLS,), ((0, 64),), -0.2, 0.2)), 0.5, 2.0),
        "cell_matrix": draw_cell_matrix(jax.random.fold_in(key_list[8], 71), 0),
        "connectivity": draw_connectivity(jax.random.fold_in(key_list[8], 71), 0),
    }


filter_center = 2.0
filter_halfwidth = 2.0


def to_grid(values):
    rows_count = values.shape[0]
    blocks = values.reshape(rows_count, PGZ, PGY, PGX, OZ, OY, OX)
    return jnp.transpose(blocks, (0, 1, 4, 2, 5, 3, 6)).reshape(rows_count, PGZ * OZ, PGY * OY, PGX * OX)


def from_grid(grid_values):
    rows_count = grid_values.shape[0]
    blocks = grid_values.reshape(rows_count, PGZ, OZ, PGY, OY, PGX, OX)
    return jnp.transpose(blocks, (0, 1, 3, 5, 2, 4, 6)).reshape(rows_count, -1)


def assemble(values, connectivity, cell_scale, cell_matrix):
    rows_count = values.shape[0]
    padded = jnp.pad(to_grid(values), ((0, 0), (0, 1), (0, 1), (0, 1)))

    def add_partition(position, accumulated):
        partition = jnp.asarray(position).astype(jnp.int32)
        part_x = partition % PGX
        part_y = (partition // PGX) % PGY
        part_z = partition // (PGX * PGY)
        zero_start = partition * 0
        corner = (zero_start, part_z * OZ, part_y * OY, part_x * OX)
        extent = (rows_count, OZ + 1, OY + 1, OX + 1)
        extended_box = lax.dynamic_slice(padded, corner, extent).reshape(rows_count, NEXT)
        first_cell = partition * CELL_DEV
        cell_nodes = lax.dynamic_slice_in_dim(connectivity, first_cell, CELL_DEV, 1)
        scales = lax.dynamic_slice_in_dim(cell_scale, first_cell, CELL_DEV, 0)
        gathered = jnp.take(extended_box, cell_nodes, axis=1)
        cell_terms = jnp.einsum("ij,kjc->kic", cell_matrix, gathered, precision=lax.Precision.HIGHEST) * scales
        local_terms = jnp.zeros((rows_count, NEXT), jnp.float32).at[:, cell_nodes].add(cell_terms)
        current = lax.dynamic_slice(accumulated, corner, extent)
        return lax.dynamic_update_slice(accumulated, current + local_terms.reshape(extent), corner)

    accumulated = lax.fori_loop(0, N_DOM, add_partition, jnp.zeros_like(padded))
    return from_grid(accumulated[:, :-1, :-1, :-1])


def reference(states, previous, potential, screening, occupation, cell_scale, cell_matrix, connectivity):
    applied = assemble(states, connectivity, cell_scale, cell_matrix)
    hamiltonian = 0.5 * applied + potential[None, :] * states
    filtered = (2.0 / filter_halfwidth) * (hamiltonian - filter_center * states) - previous
    density = jnp.sum(occupation[:, None] * filtered * filtered, axis=0)
    source = density / STATES

    def operator(values):
        return assemble(values[None, :], connectivity, cell_scale, cell_matrix)[0] + screening * values

    solution = jnp.zeros_like(source)
    residual = source
    direction = source
    norm_now = jnp.sum(residual * residual)
    for iteration in range(ITERS):
        image = operator(direction)
        step_size = norm_now / jnp.sum(direction * image)
        solution = solution + step_size * direction
        residual = residual - step_size * image
        norm_next = jnp.sum(residual * residual)
        direction = residual + (norm_next / norm_now) * direction
        norm_now = norm_next
    return filtered, solution
```

```python
import jax
import jax.numpy as jnp
from jax import lax
from jax.experimental import pallas as pl
from jax.experimental.pallas import tpu as pltpu
from jax.sharding import PartitionSpec as P

MESH = pl.DeviceIdType.MESH
F32 = jnp.float32
BF16 = jnp.bfloat16
STATES = 12
ZLO = 6
FILTER_CENTER = 2.0
FILTER_SCALE = 2.0 / 2.0


HALO = (
    ("x", (1, 0, 0)),
    ("x", (1, 0, 1)),
    ("x", (1, 1, 0)),
    ("x", (1, 1, 1)),
    ("y", (0, 1, 0)),
    ("y", (0, 1, 1)),
    ("z", (0, 0, 1)),
)


def roll(x, by, axis=1):
    by = by % x.shape[axis]
    return x if by == 0 else pltpu.roll(x, by, axis)


def iotas(rows=8, lanes=128):
    row = lax.broadcasted_iota(jnp.int32, (rows, lanes), 0)
    lane = lax.broadcasted_iota(jnp.int32, (rows, lanes), 1)
    return row, lane


def split(x):
    high = x.astype(BF16)
    return high, (x - high.astype(F32)).astype(BF16)


def column_table():
    row, lane = iotas(384, 384)
    g, cx = lane >> 3, lane & 7
    j = (g * 43) >> 8
    wanted = j * 48 + cx * 6 + (g - 6 * j)
    return jnp.where((row == wanted) & (lane < 288), 1.0, 0.0).astype(BF16)


def node_rows(rows):
    row, lane = iotas(rows, 384)
    k, v = row & 7, row >> 3
    return jnp.where((lane == 49 * k + v) & (k < 7) & (v < 49), 1.0, 0.0).astype(BF16)


def to_cells(tiles, table):
    n = tiles[0].shape[0]
    row, lane = iotas(n)
    group = lane >> 3
    chunks = []
    for cy in range(8):
        first, off = 288 * cy // 128, 288 * cy % 128
        parts = []
        for m in range(3):
            one = tiles[(first + m) % 18]
            if off:
                two = tiles[(first + m + 1) % 18]
                one = jnp.where(lane < 128 - off, roll(one, -off), roll(two, -off))
            parts.append(one)
        chunks.append(jnp.concatenate(parts, axis=1))
    stacked = jnp.concatenate(chunks, axis=0)
    high, low = split(stacked)
    both = jnp.dot(jnp.concatenate([high, low], axis=0), table, preferred_element_type=F32)
    moved = both[: 8 * n] + both[8 * n :]
    skewed = [
        [roll(moved[n * cy : n * cy + n, 128 * a : 128 * a + 128], 8 * cy) for a in range(3)]
        for cy in range(8)
    ]
    out = []
    for g in range(36):
        a, b = g // 16, g % 16
        got = jnp.where(group == b, skewed[0][a], 0.0)
        for cy in range(1, 8):
            got = jnp.where(group == (b + cy) % 16, skewed[cy][a], got)
        out.append(roll(got, -8 * b))
    return out


def from_cells(tiles, table):
    row, lane = iotas(8)
    group = lane >> 3
    placed = [roll(tiles[g], 8 * (g % 16)) for g in range(36)]
    rows = []
    for cy in range(8):
        parts = []
        for a in range(3):
            count = 16 if a < 2 else 4
            got = jnp.zeros((8, 128), F32)
            for b in range(count):
                got = jnp.where(group == (b + cy) % 16, placed[16 * a + b], got)
            parts.append(roll(got, -8 * cy))
        rows.append(jnp.concatenate(parts, axis=1))
    stacked = jnp.concatenate(rows, axis=0)
    high, low = split(stacked)
    both = lax.dot_general(
        jnp.concatenate([high, low], axis=0), table, (((1,), (1,)), ((), ())), preferred_element_type=F32
    )
    moved = both[:64] + both[64:]
    out = []
    for c in range(18):
        got = jnp.zeros((8, 128), F32)
        for cy in range(8):
            start = 288 * cy - 128 * c
            lo, hi = max(start, 0), min(start + 288, 128)
            if lo >= hi:
                continue
            off = start % 128
            for m in range(3):
                begin = start + 128 * m
                one_lo, one_hi = max(begin, lo), min(begin + 128, hi)
                if one_lo >= one_hi:
                    continue
                piece = roll(moved[8 * cy : 8 * cy + 8, 128 * m : 128 * m + 128], off)
                got = jnp.where((lane >= one_lo) & (lane < one_hi), piece, got)
        out.append(got)
    return out


def pack_ghosts(field):
    row, lane = iotas()
    cx, cy = lane & 7, lane >> 3
    x_tile = jnp.zeros((8, 128), F32)
    y_tile = jnp.zeros((8, 128), F32)
    for j in range(6):
        x_tile = jnp.where((cx == j) & (cy < 8), roll(field(6 * j), j), x_tile)
    for i in range(6):
        y_tile = jnp.where(cy == i, roll(field(i), 8 * i), y_tile)
    return x_tile, y_tile


def extended(field, xs, ys, z_row, high):
    row, lane = iotas()
    cx, cy = lane & 7, lane >> 3
    hx, hy, hz = high
    x_all = jnp.where(row == 6, roll(xs[1] * (hx * hz), 6, 0), xs[0] * hx)
    xy_all = jnp.where(row == 6, roll(xs[3] * (hx * hy * hz), 6, 0), xs[2] * (hx * hy))
    y_all = jnp.where(row == 6, roll(ys[1] * (hy * hz), 6, 0), ys[0] * hy)
    out = [None] * 49
    for g in range(36):
        above = jnp.broadcast_to(z_row(g) * hz, (8, 128))
        out[7 * (g // 6) + g % 6] = jnp.where(row == 6, above, field(g))
    for j in range(6):
        out[7 * j + 6] = jnp.where(cx == 7, roll(x_all, 7 - j), roll(out[7 * j], -1))
    for i in range(6):
        out[42 + i] = jnp.where(cy == 7, roll(y_all, 56 - 8 * i), roll(out[i], -8))
    corner = jnp.where(cx == 7, roll(x_all, -1), roll(out[0], -9))
    corner = jnp.where(cy == 7, roll(y_all, 55), corner)
    out[48] = jnp.where((cx == 7) & (cy == 7), roll(xy_all, 63), corner)
    return out


def cell_terms(tiles, matrix_high, matrix_low, scale_row):
    high = tiles.astype(BF16).astype(F32)
    low = tiles - high
    _, lane = iotas(512)
    both = jnp.where(lane < 64, high, roll(low, 64)).astype(BF16)
    got = jnp.dot(matrix_high, both, preferred_element_type=F32)
    got = got + jnp.dot(matrix_low, both, preferred_element_type=F32)
    got = got + roll(got, 64)
    return got * scale_row


def local_fold(term):
    row, lane = iotas()
    cx, cy = lane & 7, lane >> 3
    upper_x = []
    for j in range(6):
        got = term(7 * j + 6)
        if j == 0:
            got = got + jnp.where(cy >= 1, roll(term(48), 8), 0.0)
        upper_x.append(got)
    x_tile = jnp.where(lane == 62, roll(term(48), -1), 0.0)
    for j in range(6):
        x_tile = jnp.where((cx == j) & (cy < 8), roll(upper_x[j], j - 7), x_tile)
    y_tile = jnp.zeros((8, 128), F32)
    for i in range(6):
        got = term(42 + i)
        if i == 0:
            got = got + jnp.where(cx >= 1, roll(term(48), 1), 0.0)
        y_tile = jnp.where(cy == i, roll(got, 8 * i - 56), y_tile)
    out = []
    for g in range(36):
        j, i = g // 6, g % 6
        got = term(7 * j + i)
        if j == 0:
            got = got + jnp.where(cy >= 1, roll(term(42 + i), 8), 0.0)
        if i == 0:
            got = got + jnp.where(cx >= 1, roll(upper_x[j], 1), 0.0)
        out.append(got)
    return out, x_tile, y_tile


def finish_fold(partial, xs, ys, z_row, low):
    row, lane = iotas()
    cx, cy = lane & 7, lane >> 3
    lx, ly, lz = low
    kept = row < 6

    def both(tile, tile_z, mask):
        return jnp.where(kept, tile * mask, 0.0) + jnp.where(row == 0, roll(tile_z * (mask * lz), 2, 0), 0.0)

    x_all = both(xs[0], xs[1], lx)
    xy_all = both(xs[2], xs[3], lx * ly)
    y_all = both(ys[0], ys[1], ly)
    out = []
    for g in range(36):
        j, i = g // 6, g % 6
        below = jnp.broadcast_to(z_row(g) * lz, (8, 128))
        got = partial(g) + jnp.where(row == 0, below, 0.0)
        if i == 0:
            got = got + jnp.where(cx == 0, roll(x_all, -j), 0.0)
        if j == 0:
            got = got + jnp.where(cy == 0, roll(y_all, -8 * i), 0.0)
        if g == 0:
            got = got + jnp.where(lane == 0, roll(xy_all, -62), 0.0)
        out.append(jnp.where(kept & (lane < 64), got, 0.0))
    return out


def kernel(
    states_ref, previous_ref, potential_ref, screening_ref, occupation_ref, scale_ref, matrix_ref, ids_ref,
    filtered_ref, field_ref,
    pad, stage, table, padded_matrix, cell_matrix, scales,
    s_f, pps_f, grid_ext, terms, part,
    sent_x, sent_y, sent_z, got_x, got_y, got_z, z_both,
    dens, dens_in, half, half_in, full_in, vec, red_out, red_in, nat, nat_in,
    halo_send, halo_recv, band_send, band_recv, red_send, red_recv,
):
    dom, band = lax.axis_index("dom"), lax.axis_index("band")
    px, py, pz = lax.rem(dom, 4), lax.rem(lax.div(dom, 4), 4), lax.div(dom, 16)
    z_lo, core = lax.div(band, 2), lax.rem(band, 2)
    z_hi = lax.rem(py, 2)

    def place(x, y, z):
        return x + 4 * y + 16 * z

    def near(step, sign, mirrored):
        x = lax.rem(px + (sign * step[0] + 4), 4)
        y = lax.rem(py + (sign * step[1] + 4), 4)
        z = lax.rem(pz + (sign * step[2] + 4), 4)
        flipped = mirrored and step[1] % 2 == 1
        return (place(x, y, z), 2 * (ZLO - 1 - z_lo) + core if flipped else band)

    partner = (dom, 2 * z_lo + (1 - core))

    def chip(z):
        return (dom, 2 * z + core)

    group_one, group_two = [], []
    for e in range(1, 8):
        x = lax.rem(px + e % 4, 4)
        y = lax.rem(py + 2 * (e // 4), 4)
        group_one.append((place(x, y, pz), band))
    for e in range(1, 8):
        z = lax.rem(pz + e % 4, 4)
        if e // 4:
            y = py + 1 - 2 * z_hi
            group_two.append((place(px, y, z), 2 * (ZLO - 1 - z_lo) + core))
        else:
            group_two.append((place(px, py, z), band))

    greeted = []
    for _, step in HALO:
        for sign in (1, -1):
            greeted.append(near(step, sign, False))
            if step[1]:
                greeted.append(near(step, sign, True))
    greeted.append(partner)
    for e in range(1, ZLO):
        greeted.append(chip(lax.rem(z_lo + e, ZLO)))
    greeted += group_one + group_two
    barrier = pltpu.get_barrier_semaphore()
    for device in greeted:
        pl.semaphore_signal(barrier, inc=1, device_id=device, device_id_type=MESH)

    def flag(test):
        return jnp.where(test, 1.0, 0.0).astype(F32)

    high = (flag(px < 3), flag(py < 3), flag(pz < 3))
    low = (flag(px > 0), flag(py > 0), flag(pz > 0))
    row, lane = iotas()

    table[...] = column_table()
    pad[...] = jnp.zeros_like(pad)
    sent_z[...] = jnp.zeros_like(sent_z)
    pad[0, 0:108, :] = states_ref[...]
    first = to_cells([pad[0, pl.ds(c, 8, stride=18), :] for c in range(18)], table[...])
    for g in range(36):
        s_f[8 * g : 8 * g + 8, :] = first[g]
    grid_ext[...] = jnp.zeros_like(grid_ext)

    def copies(at, mirrored, sign):
        made = []
        counts = {"x": 0, "y": 0, "z": 0}
        for e, (kind, step) in enumerate(HALO):
            c = counts[kind]
            counts[kind] += 1
            src = {"x": sent_x, "y": sent_y, "z": sent_z}[kind].at[at]
            dst = {"x": got_x.at[at, c], "y": got_y.at[at, c], "z": got_z.at[at]}[kind]
            made.append(
                pltpu.make_async_remote_copy(
                    src_ref=src,
                    dst_ref=dst,
                    send_sem=halo_send.at[at, e],
                    recv_sem=halo_recv.at[at, e],
                    device_id=near(step, sign, mirrored),
                    device_id_type=MESH,
                )
            )
        return made

    def put_z(at, source, sublane):
        lower = source[pl.ds(sublane, 18, stride=8), :]
        upper = source[pl.ds(144 + sublane, 18, stride=8), :]
        _, wide = iotas(18)
        sent_z[at, 0:18, :] = jnp.where(wide < 64, lower, roll(upper, 64))

    def take_z(at):
        rows = got_z[at]
        z_both[0] = rows
        z_both[1] = roll(rows, 64)

    def z_row(g):
        return z_both[g // 18, g % 18 : g % 18 + 1, :]

    def start_extend(n, source, mirrored):
        at = 2 * n
        x_tile, y_tile = pack_ghosts(lambda g: source[8 * g : 8 * g + 8, :])
        sent_x[at] = x_tile
        sent_y[at] = y_tile
        put_z(at, source, 0)
        made = copies(at, mirrored, -1)
        for copy in made:
            copy.start()
        return made

    def middle(n, source, made, mirrored):
        at = 2 * n
        for copy in made:
            copy.wait_recv()
        take_z(at)
        tiles = extended(
            lambda g: source[8 * g : 8 * g + 8, :],
            [got_x[at, c] for c in range(4)],
            [got_y[at, c] for c in range(2)],
            z_row,
            high,
        )
        for v in range(49):
            grid_ext[8 * v : 8 * v + 8, :] = tiles[v]
        terms[...] = cell_terms(grid_ext[...], cell_matrix[0], cell_matrix[1], scales[0:1, :])
        folded, x_tile, y_tile = local_fold(lambda v: terms[8 * v : 8 * v + 8, :])
        sent_x[at + 1] = x_tile
        sent_y[at + 1] = y_tile
        for g in range(36):
            part[8 * g : 8 * g + 8, :] = folded[g]
        put_z(at + 1, part, 6)
        out = copies(at + 1, mirrored, 1)
        for copy in out:
            copy.start()
        return out

    def finish(n, made):
        at = 2 * n + 1
        for copy in made:
            copy.wait_recv()
        take_z(at)
        return finish_fold(
            lambda g: part[8 * g : 8 * g + 8, :],
            [got_x[at, c] for c in range(4)],
            [got_y[at, c] for c in range(2)],
            z_row,
            low,
        )

    pl.semaphore_wait(barrier, len(greeted))
    extend_0 = start_extend(0, s_f, False)

    pad[1, 0:108, :] = previous_ref[...]
    pad[2, 0:108, :] = potential_ref[...]
    pad[3, 0:108, :] = screening_ref[...]
    three = to_cells(
        [
            jnp.concatenate([pad[m, pl.ds(c, 8, stride=18), :] for m in (1, 2, 3)], axis=0)
            for c in range(18)
        ],
        table[...],
    )
    for g in range(36):
        for m in range(3):
            pps_f[m, 8 * g : 8 * g + 8, :] = three[g][8 * m : 8 * m + 8]
    padded_matrix[...] = jnp.zeros_like(padded_matrix)
    padded_matrix[0:343, 0:343] = matrix_ref[...]
    by_row, by_column = node_rows(400), node_rows(512)
    for h, piece in enumerate(split(padded_matrix[...])):
        rows_moved = jnp.dot(by_row, piece, preferred_element_type=F32).astype(BF16)
        cell_matrix[h] = lax.dot_general(
            rows_moved, by_column, (((1,), (1,)), ((), ())), preferred_element_type=F32
        ).astype(BF16)
    own_row, _ = iotas(128, 64)
    first_id = 6 * 49 * ((own_row & 63) >> 3) + 6 * (own_row & 7)
    matches = jnp.where(first_id == ids_ref[0:1, :], 1.0, 0.0).astype(F32)
    given = jnp.broadcast_to(scale_ref[...], (8, 64))
    scales[...] = lax.dot_general(
        given, matches, (((1,), (1,)), ((), ())), precision=lax.Precision.HIGHEST, preferred_element_type=F32
    )

    fold_0 = middle(0, s_f, extend_0, False)
    summed = finish(0, fold_0)
    weight = occupation_ref[...]
    kept = []
    squares = []
    for g in range(36):
        rows = slice(8 * g, 8 * g + 8)
        here = s_f[rows, :]
        hamiltonian = 0.5 * summed[g] + pps_f[1, rows, :] * here
        value = FILTER_SCALE * (hamiltonian - FILTER_CENTER * here) - pps_f[0, rows, :]
        stage[rows, :] = value
        squares.append(weight * value * value)
    for m in range(18):
        dens[8 * m : 8 * m + 8, :] = squares[m] + roll(squares[m + 18], 64)

    mine = pl.multiple_of(72 * core, 8)
    other = pl.multiple_of(72 * (1 - core), 8)

    def band_copy(src, dst, at_send, at_recv, device):
        return pltpu.make_async_remote_copy(
            src_ref=src,
            dst_ref=dst,
            send_sem=band_send.at[at_send],
            recv_sem=band_recv.at[at_recv],
            device_id=device,
            device_id_type=MESH,
        )

    swap = band_copy(dens.at[pl.ds(other, 72), :], dens_in, 0, 0, partner)
    swap.start()
    swap.wait_recv()
    half[...] = dens[pl.ds(mine, 72), :] + dens_in[...]

    not_first, not_last = z_lo > 0, z_lo < ZLO - 1
    slot_first = jnp.maximum(z_lo - 1, 0)
    slot_last = jnp.minimum(z_lo, ZLO - 2)

    to_first = band_copy(half, half_in.at[slot_first], 1, 1 + slot_first, chip(0))
    to_last = band_copy(half, half_in.at[slot_last], 2, 1 + slot_last, chip(ZLO - 1))

    @pl.when(not_first)
    def _():
        to_first.start()

    @pl.when(not_last)
    def _():
        to_last.start()

    natural = from_cells([stage[8 * g : 8 * g + 8, :] for g in range(36)], table[...])
    for c in range(18):
        nat[0, pl.ds(c, 8, stride=18), :] = natural[c]
    filtered_ref[...] = nat[0, 0:108, :]

    is_end = (z_lo == 0) | (z_lo == ZLO - 1)

    @pl.when(is_end)
    def _():
        arrived = [band_copy(half, half_in.at[s], 1, 1 + s, partner) for s in range(ZLO - 1)]
        for copy in arrived:
            copy.wait_recv()
        total = half[...]
        for s in range(ZLO - 1):
            total = total + half_in[s]
        dens_own = total * (1.0 / STATES)
        full_in[0] = dens_own
        again = band_copy(full_in.at[0], full_in.at[1], 3, 6, partner)
        again.start()
        again.wait_recv()
        first_half = jnp.where(core == 0, full_in[0], full_in[1])
        second_half = jnp.where(core == 0, full_in[1], full_in[0])
        both = (first_half, second_half)
        R, W, Q, SS, PP = 0, 1, 2, 3, 4
        for m in range(18):
            tile = both[m // 9][8 * (m % 9) : 8 * (m % 9) + 8]
            vec[R, 8 * m : 8 * m + 8, :] = jnp.where(lane < 64, tile, 0.0)
            vec[R, 8 * (m + 18) : 8 * (m + 18) + 8, :] = jnp.where(lane < 64, roll(tile, 64), 0.0)

        def with_screening(got, v):
            return [
                got[g] + pps_f[2, 8 * g : 8 * g + 8, :] * vec[v, 8 * g : 8 * g + 8, :] for g in range(36)
            ]

        def put(v, tiles):
            for g in range(36):
                vec[v, 8 * g : 8 * g + 8, :] = tiles[g]

        def dot_row(a, b):
            got = vec[a] * vec[b]
            return jnp.sum(got, axis=0, keepdims=True)

        def start_reduce(n, pairs):
            tile = jnp.zeros((8, 128), F32)
            for m, (a, b) in enumerate(pairs):
                tile = jnp.where(row == m, jnp.broadcast_to(dot_row(a, b), (8, 128)), tile)
            red_out[n, 0] = tile
            return send_reduce(n, 0, group_one)

        def send_reduce(n, level, devices):
            made = []
            for e, device in enumerate(devices):
                made.append(
                    pltpu.make_async_remote_copy(
                        src_ref=red_out.at[n, level],
                        dst_ref=red_in.at[n, level, e],
                        send_sem=red_send.at[n, level, e],
                        recv_sem=red_recv.at[n, level, e],
                        device_id=device,
                        device_id_type=MESH,
                    )
                )
            for copy in made:
                copy.start()
            return made

        def take(n, level, made):
            for copy in made:
                copy.wait_recv()
            got = red_out[n, level]
            for e in range(7):
                got = got + red_in[n, level, e]
            return got

        def second_level(n, made):
            red_out[n, 1] = take(n, 0, made)
            return send_reduce(n, 1, group_two)

        def scalars(n, made):
            got = jnp.sum(take(n, 1, made), axis=1, keepdims=True)
            return got[0:1], got[1:2], got[2:3]

        everything = []

        made = start_extend(1, vec.at[R], True)
        out = middle(1, vec.at[R], made, True)
        put(W, with_screening(finish(1, out), R))
        everything += made + out

        red_a = start_reduce(0, ((R, R), (R, W)))
        made = start_extend(2, vec.at[W], True)
        red_b = second_level(0, red_a)
        out = middle(2, vec.at[W], made, True)
        put(Q, with_screening(finish(2, out), W))
        norm_0, image_0, _ = scalars(0, red_b)
        everything += made + out + red_a + red_b

        alpha_0 = norm_0 / image_0
        vec[PP] = vec[R]
        vec[SS] = vec[W]
        vec[5] = alpha_0 * vec[R]
        vec[6] = vec[Q]
        vec[R] = vec[R] - alpha_0 * vec[SS]
        vec[W] = vec[W] - alpha_0 * vec[Q]

        red_a = start_reduce(1, ((R, R), (R, W), (R, SS)))
        made = start_extend(3, vec.at[W], True)
        red_b = second_level(1, red_a)
        out = middle(3, vec.at[W], made, True)
        put(Q, with_screening(finish(3, out), W))
        norm_1, rw_1, rs_1 = scalars(1, red_b)
        everything += made + out + red_a + red_b

        beta_1 = norm_1 / norm_0
        image_1 = rw_1 + 2.0 * beta_1 * rs_1 + beta_1 * beta_1 * image_0
        alpha_1 = norm_1 / image_1
        vec[PP] = vec[R] + beta_1 * vec[PP]
        vec[SS] = vec[W] + beta_1 * vec[SS]
        vec[6] = vec[Q] + beta_1 * vec[6]
        vec[5] = vec[5] + alpha_1 * vec[PP]
        vec[R] = vec[R] - alpha_1 * vec[SS]
        vec[W] = vec[W] - alpha_1 * vec[6]

        red_a = start_reduce(2, ((R, R), (R, W), (R, SS)))
        red_b = second_level(2, red_a)
        norm_2, rw_2, rs_2 = scalars(2, red_b)
        everything += red_a + red_b
        beta_2 = norm_2 / norm_1
        image_2 = rw_2 + 2.0 * beta_2 * rs_2 + beta_2 * beta_2 * image_1
        alpha_2 = norm_2 / image_2
        vec[5] = vec[5] + alpha_2 * (vec[R] + beta_2 * vec[PP])

        natural = from_cells([vec[5, 8 * g : 8 * g + 8, :] for g in range(36)], table[...])
        for c in range(18):
            nat[1, pl.ds(c, 8, stride=18), :] = natural[c]
        onward = [
            band_copy(nat.at[1, 0:112], nat_in, 4 + s, 7, chip(jnp.where(z_lo == 0, 1 + s, ZLO - 2 - s)))
            for s in range(2)
        ]
        for copy in onward:
            copy.start()
        field_ref[...] = nat[1, 0:108, :]
        again.wait_send()
        for copy in everything + onward:
            copy.wait_send()

    @pl.when(jnp.logical_not(is_end))
    def _():
        band_copy(nat.at[1, 0:112], nat_in, 4, 7, partner).wait_recv()
        field_ref[...] = nat_in[0:108, :]

    swap.wait_send()

    @pl.when(not_first)
    def _():
        to_first.wait_send()

    @pl.when(not_last)
    def _():
        to_last.wait_send()

    for copy in extend_0 + fold_0:
        copy.wait_send()


def per_device(states, previous, potential, screening, occupation, cell_scale, cell_matrix, connectivity):
    vmem = pl.BlockSpec(memory_space=pltpu.VMEM)
    filtered, field = pl.pallas_call(
        kernel,
        out_shape=(jax.ShapeDtypeStruct((108, 128), F32), jax.ShapeDtypeStruct((108, 128), F32)),
        in_specs=[vmem] * 8,
        out_specs=(vmem, vmem),
        scratch_shapes=[
            pltpu.VMEM((4, 144, 128), F32),
            pltpu.VMEM((288, 128), F32),
            pltpu.VMEM((384, 384), BF16),
            pltpu.VMEM((384, 384), F32),
            pltpu.VMEM((2, 400, 512), BF16),
            pltpu.VMEM((8, 128), F32),
            pltpu.VMEM((288, 128), F32),
            pltpu.VMEM((3, 288, 128), F32),
            pltpu.VMEM((512, 128), F32),
            pltpu.VMEM((400, 128), F32),
            pltpu.VMEM((288, 128), F32),
            pltpu.VMEM((8, 8, 128), F32),
            pltpu.VMEM((8, 8, 128), F32),
            pltpu.VMEM((8, 24, 128), F32),
            pltpu.VMEM((8, 4, 8, 128), F32),
            pltpu.VMEM((8, 2, 8, 128), F32),
            pltpu.VMEM((8, 24, 128), F32),
            pltpu.VMEM((2, 24, 128), F32),
            pltpu.VMEM((144, 128), F32),
            pltpu.VMEM((72, 128), F32),
            pltpu.VMEM((72, 128), F32),
            pltpu.VMEM((5, 72, 128), F32),
            pltpu.VMEM((2, 72, 128), F32),
            pltpu.VMEM((7, 288, 128), F32),
            pltpu.VMEM((3, 2, 8, 128), F32),
            pltpu.VMEM((3, 2, 7, 8, 128), F32),
            pltpu.VMEM((2, 144, 128), F32),
            pltpu.VMEM((112, 128), F32),
            pltpu.SemaphoreType.DMA((8, 7)),
            pltpu.SemaphoreType.DMA((8, 7)),
            pltpu.SemaphoreType.DMA((6,)),
            pltpu.SemaphoreType.DMA((8,)),
            pltpu.SemaphoreType.DMA((3, 2, 7)),
            pltpu.SemaphoreType.DMA((3, 2, 7)),
        ],
        compiler_params=pltpu.CompilerParams(collective_id=0, has_side_effects=True),
        name="step",
    )(
        states.reshape(108, 128),
        previous.reshape(108, 128),
        potential.reshape(108, 128),
        screening.reshape(108, 128),
        occupation.reshape(1, 1),
        cell_scale.reshape(1, 64),
        cell_matrix,
        connectivity[0:1, :],
    )
    return filtered.reshape(1, 13824), field.reshape(13824)


def solution(mesh):
    in_specs = (
        P("band", "dom"),
        P("band", "dom"),
        P("dom"),
        P("dom"),
        P("band"),
        P("dom"),
        P(),
        P(None, "dom"),
    )
    out_specs = (P("band", "dom"), P("dom"))
    return jax.shard_map(per_device, mesh=mesh, in_specs=in_specs, out_specs=out_specs, check_vma=False)
```

```python
import jax
import jax.numpy as jnp
from jax import lax
from jax.experimental import pallas as pl
from jax.experimental.pallas import tpu as pltpu
from jax.sharding import PartitionSpec as P

MESH = pl.DeviceIdType.MESH
F32 = jnp.float32
BF16 = jnp.bfloat16
STATES = 12
ZLO = 6
FILTER_CENTER = 2.0
FILTER_SCALE = 2.0 / 2.0


AROUND = [(x, y, z) for y in (1, -1, 0) for x in (1, -1, 0) for z in (1, -1, 0) if (x, y, z) != (0, 0, 0)]
BELOW = [d for d in AROUND if max(d) <= 0]
TILES = 38
CORE_ROWS = 288
ROWS = 8 * TILES


def side(step):
    return 0 if step > 0 else 1

def roll(x, by, axis=1):
    by = by % x.shape[axis]
    return x if by == 0 else pltpu.roll(x, by, axis)


def iotas(rows=8, lanes=128):
    row = lax.broadcasted_iota(jnp.int32, (rows, lanes), 0)
    lane = lax.broadcasted_iota(jnp.int32, (rows, lanes), 1)
    return row, lane


def split(x):
    high = x.astype(BF16)
    return high, (x - high.astype(F32)).astype(BF16)


def column_table():
    row, lane = iotas(384, 384)
    g, cx = lane >> 3, lane & 7
    j = (g * 43) >> 8
    wanted = j * 48 + cx * 6 + (g - 6 * j)
    return jnp.where((row == wanted) & (lane < 288), 1.0, 0.0).astype(BF16)


def node_rows(rows):
    row, lane = iotas(rows, 384)
    k, v = row & 7, row >> 3
    return jnp.where((lane == 49 * k + v) & (k < 7) & (v < 49), 1.0, 0.0).astype(BF16)


def to_cells(tiles, table):
    n = tiles[0].shape[0]
    row, lane = iotas(n)
    group = lane >> 3
    chunks = []
    for cy in range(8):
        first, off = 288 * cy // 128, 288 * cy % 128
        parts = []
        for m in range(3):
            one = tiles[(first + m) % 18]
            if off:
                two = tiles[(first + m + 1) % 18]
                one = jnp.where(lane < 128 - off, roll(one, -off), roll(two, -off))
            parts.append(one)
        chunks.append(jnp.concatenate(parts, axis=1))
    stacked = jnp.concatenate(chunks, axis=0)
    high, low = split(stacked)
    both = jnp.dot(jnp.concatenate([high, low], axis=0), table, preferred_element_type=F32)
    moved = both[: 8 * n] + both[8 * n :]
    skewed = [
        [roll(moved[n * cy : n * cy + n, 128 * a : 128 * a + 128], 8 * cy) for a in range(3)]
        for cy in range(8)
    ]
    out = []
    for g in range(36):
        a, b = g // 16, g % 16
        got = jnp.where(group == b, skewed[0][a], 0.0)
        for cy in range(1, 8):
            got = jnp.where(group == (b + cy) % 16, skewed[cy][a], got)
        out.append(roll(got, -8 * b))
    return out


def split_exact(x):
    high, low = split(x)
    return high, low, (x - high.astype(F32) - low.astype(F32)).astype(BF16)


def from_cells(tiles, table):
    row, lane = iotas(8)
    group = lane >> 3
    placed = [roll(tiles[g], 8 * (g % 16)) for g in range(36)]
    rows = []
    for cy in range(8):
        parts = []
        for a in range(3):
            count = 16 if a < 2 else 4
            got = jnp.zeros((8, 128), F32)
            for b in range(count):
                got = jnp.where(group == (b + cy) % 16, placed[16 * a + b], got)
            parts.append(roll(got, -8 * cy))
        rows.append(jnp.concatenate(parts, axis=1))
    stacked = jnp.concatenate(rows, axis=0)
    both = lax.dot_general(
        jnp.concatenate(split_exact(stacked), axis=0), table, (((1,), (1,)), ((), ())), preferred_element_type=F32
    )
    moved = both[:64] + both[64:128] + both[128:]
    out = []
    for c in range(18):
        got = jnp.zeros((8, 128), F32)
        for cy in range(8):
            start = 288 * cy - 128 * c
            lo, hi = max(start, 0), min(start + 288, 128)
            if lo >= hi:
                continue
            off = start % 128
            for m in range(3):
                begin = start + 128 * m
                one_lo, one_hi = max(begin, lo), min(begin + 128, hi)
                if one_lo >= one_hi:
                    continue
                piece = roll(moved[8 * cy : 8 * cy + 8, 128 * m : 128 * m + 128], off)
                got = jnp.where((lane >= one_lo) & (lane < one_hi), piece, got)
        out.append(got)
    return out


def cell_terms(tiles, matrix_high, matrix_low, scale_row):
    high = tiles.astype(BF16).astype(F32)
    low = tiles - high
    _, lane = iotas(512)
    both = jnp.where(lane < 64, high, roll(low, 64)).astype(BF16)
    got = jnp.dot(matrix_high, both, preferred_element_type=F32)
    got = got + jnp.dot(matrix_low, both, preferred_element_type=F32)
    got = got + roll(got, 64)
    return got * scale_row


def local_fold(term):
    row, lane = iotas()
    cx, cy = lane & 7, lane >> 3
    upper_x = []
    for j in range(6):
        got = term(7 * j + 6)
        if j == 0:
            got = got + jnp.where(cy >= 1, roll(term(48), 8), 0.0)
        upper_x.append(got)
    x_tile = jnp.where(lane == 62, roll(term(48), -1), 0.0)
    for j in range(6):
        x_tile = jnp.where((cx == j) & (cy < 8), roll(upper_x[j], j - 7), x_tile)
    y_tile = jnp.zeros((8, 128), F32)
    for i in range(6):
        got = term(42 + i)
        if i == 0:
            got = got + jnp.where(cx >= 1, roll(term(48), 1), 0.0)
        y_tile = jnp.where(cy == i, roll(got, 8 * i - 56), y_tile)
    out = []
    for g in range(36):
        j, i = g // 6, g % 6
        got = term(7 * j + i)
        if j == 0:
            got = got + jnp.where(cy >= 1, roll(term(42 + i), 8), 0.0)
        if i == 0:
            got = got + jnp.where(cx >= 1, roll(upper_x[j], 1), 0.0)
        out.append(got)
    return out, x_tile, y_tile


def column_to_row(tile, at):
    row, lane = iotas()
    return jnp.sum(jnp.where(row == lane, jnp.broadcast_to(tile[:, at : at + 1], (8, 128)), 0.0), axis=0, keepdims=True)


def row_to_column(values):
    row, lane = iotas()
    return jnp.sum(jnp.where(row == lane, jnp.broadcast_to(values, (8, 128)), 0.0), axis=1, keepdims=True)


def wide(values):
    return jnp.broadcast_to(values, (8, 128))


def low_faces(field):
    row, lane = iotas()
    cx, cy = lane & 7, lane >> 3
    x_tile = jnp.zeros((8, 128), F32)
    y_tile = jnp.zeros((8, 128), F32)
    for j in range(6):
        x_tile = jnp.where((cx == j) & (cy < 8), roll(field(6 * j), j), x_tile)
    for i in range(6):
        y_tile = jnp.where(cy == i, roll(field(i), 8 * i), y_tile)
    return x_tile, y_tile


def from_above(field, x_tile, x_row, y_tile, y_row, edge, corner, z_row, high):
    row, lane = iotas()
    hx, hy, hz = high
    line = jnp.where(lane[0:1] == 6, roll(corner * hz, 6), edge)
    x_all = jnp.where(row == 6, wide(x_row * hz), x_tile)
    x_all = hx * jnp.where(lane == 62, wide(row_to_column(line) * hy), x_all)
    y_all = hy * jnp.where(row == 6, wide(y_row * hz), y_tile)
    core = [jnp.where(row == 6, wide(z_row(g) * hz), field(g)) for g in range(36)]
    return core + [x_all, y_all]


def extended(field):
    row, lane = iotas()
    cx, cy = lane & 7, lane >> 3
    x_all, y_all = field(36), field(37)
    out = [None] * 49
    for g in range(36):
        out[7 * (g // 6) + g % 6] = field(g)
    for j in range(6):
        out[7 * j + 6] = jnp.where(cx == 7, roll(x_all, 7 - j), roll(field(6 * j), -1))
    for i in range(6):
        out[42 + i] = jnp.where(cy == 7, roll(y_all, 56 - 8 * i), roll(field(i), -8))
    corner = jnp.where(cx == 7, roll(x_all, -1), roll(field(0), -9))
    corner = jnp.where(cy == 7, roll(y_all, 55), corner)
    out[48] = jnp.where(lane == 63, roll(x_all, 1), corner)
    return out


def shared(part, x_high, y_high):
    row, lane = iotas()
    x_low, y_low = low_faces(part)
    x_low = jnp.where(lane == 62, roll(y_high, 62), x_low)
    y_out = jnp.where(lane == 55, roll(x_high, -7), y_high)
    y_low = jnp.where(lane == 55, roll(x_high, 55), y_low)
    edges = [column_to_row(t, at) for t in (x_high, x_low) for at in (62, 0)]
    return (x_high, x_low), (y_out, y_low), edges


def absorb(part, x_high, y_high, xs, x_rows, ys, y_rows, edges, z_row, low, high):
    row, lane = iotas()
    cx, cy = lane & 7, lane >> 3
    hx, hy, hz = high
    lx, ly, lz = low

    def with_rows(tile, rows):
        return tile + jnp.where(row == 6, wide(rows[0]), jnp.where(row == 0, wide(rows[1] * lz), 0.0))

    x_up, x_down = with_rows(xs[0], x_rows[0]), with_rows(xs[1], x_rows[1]) * lx
    y_up, y_down = with_rows(ys[0], y_rows[0]), with_rows(ys[1], y_rows[1]) * ly
    lines = edges[0] + jnp.where(lane == 6, roll(edges[1], 6), jnp.where(lane == 0, roll(edges[2] * lz, -6), 0.0))
    columns = [wide(row_to_column(lines[c : c + 1])) for c in range(4)]
    up_row, down_row = row == 6, row == 0

    def vertical(up, down):
        return jnp.where(up_row, wide(up), jnp.where(down_row, wide(down * lz), 0.0))

    x_all = x_high + x_up + vertical(z_row(0, 36), z_row(1, 36))
    x_all = x_all + jnp.where(lane == 62, roll(y_up, 7) + columns[0], 0.0)
    x_all = x_all + jnp.where(lane == 0, roll(y_down, -55) + columns[1] * ly, 0.0)
    y_all = y_high + jnp.where(cy < 6, y_up, 0.0) + vertical(z_row(0, 37), z_row(1, 37))
    y_all = y_all + jnp.where(lane == 0, roll(x_down, -62) + columns[2] * lx, 0.0)
    top = jnp.where(up_row, hz, 1.0)
    x_all = x_all * (top * hx) * jnp.where(lane == 62, hy, 1.0)
    y_all = y_all * (top * hy)
    inside = jnp.where(lane < 64, top, 0.0)
    out = []
    for g in range(36):
        j, i = g // 6, g % 6
        got = part(g) + vertical(z_row(0, g), z_row(1, g))
        if i == 0:
            got = got + jnp.where((cx == 0) & (cy < 8), roll(x_down, -j), 0.0)
        if j == 0:
            got = got + jnp.where(cy == 0, roll(y_down, -8 * i), 0.0)
        if g == 0:
            got = got + jnp.where(lane == 0, columns[3] * (lx * ly), 0.0)
        out.append(jnp.where(lane < 64, got * inside, 0.0))
    return out + [x_all, y_all]


def kernel(
    states_ref, previous_ref, potential_ref, screening_ref, occupation_ref, scale_ref, matrix_ref, ids_ref,
    filtered_ref, field_ref,
    pad, raw_matrix, ids, table, padded_matrix, cell_matrix, scales,
    own, screen, vec, grid_ext, terms, part, faces,
    sent_x, sent_y, sent_z, sent_e, got_x, got_y, got_z, got_xr, got_yr, got_e, z_both,
    dens, dens_in, half, half_in, full_in, red_out, red_in, nat, nat_f, factors,
    in_sem, out_sem, halo_send, halo_recv, band_send, band_recv, red_send, red_recv,
):
    dom, band = lax.axis_index("dom"), lax.axis_index("band")
    px, py, pz = lax.rem(dom, 4), lax.rem(lax.div(dom, 4), 4), lax.div(dom, 16)
    z_lo, core = lax.div(band, 2), lax.rem(band, 2)
    z_hi = lax.rem(py, 2)
    across = 2 * (ZLO - 1 - z_lo) + core

    def place(x, y, z):
        return x + 4 * y + 16 * z

    def near(step, mirrored):
        x = lax.rem(px + (step[0] + 4), 4)
        y = lax.rem(py + (step[1] + 4), 4)
        z = lax.rem(pz + (step[2] + 4), 4)
        return (place(x, y, z), across if mirrored and step[1] else band)

    partner = (dom, 2 * z_lo + (1 - core))

    def chip(z):
        return (dom, 2 * z + core)

    group_one = [(place(lax.rem(px + e % 4, 4), lax.rem(py + 2 * (e // 4), 4), pz), band) for e in range(1, 8)]
    group_two = []
    for e in range(1, 8):
        z = lax.rem(pz + e % 4, 4)
        if e // 4:
            group_two.append((place(px, py + 1 - 2 * z_hi, z), across))
        else:
            group_two.append((place(px, py, z), band))

    greeted = [near(step, False) for step in AROUND]
    greeted += [near(step, True) for step in AROUND if step[1]]
    greeted.append(partner)
    greeted += [chip(lax.rem(z_lo + e, ZLO)) for e in range(1, ZLO)]
    greeted += group_one + group_two
    barrier = pltpu.get_barrier_semaphore()
    for device in greeted:
        pl.semaphore_signal(barrier, inc=1, device_id=device, device_id_type=MESH)

    loads = [
        pltpu.make_async_copy(states_ref.at[:, 0, :], pad.at[0, pl.ds(0, 108), :], in_sem.at[0]),
        pltpu.make_async_copy(previous_ref.at[:, 0, :], pad.at[1, pl.ds(0, 108), :], in_sem.at[1]),
        pltpu.make_async_copy(potential_ref, pad.at[2, pl.ds(0, 108), :], in_sem.at[2]),
        pltpu.make_async_copy(screening_ref, pad.at[3, pl.ds(0, 108), :], in_sem.at[3]),
        pltpu.make_async_copy(matrix_ref, raw_matrix, in_sem.at[4]),
        pltpu.make_async_copy(ids_ref.at[:, pl.ds(0, 128)], ids, in_sem.at[5]),
    ]
    for load in loads:
        load.start()

    def flag(test):
        return jnp.where(test, 1.0, 0.0).astype(F32)

    high = (flag(px < 3), flag(py < 3), flag(pz < 3))
    low = (flag(px > 0), flag(py > 0), flag(pz > 0))
    row, lane = iotas()

    table[...] = column_table()
    for m in range(4):
        pad[m, 108:144, :] = jnp.zeros((36, 128), F32)
    grid_ext[...] = jnp.zeros_like(grid_ext)
    sent_z[...] = jnp.zeros_like(sent_z)
    loads[0].wait()
    first = to_cells([pad[0, pl.ds(c, 8, stride=18), :] for c in range(18)], table[...])
    for g in range(36):
        own[8 * g : 8 * g + 8, :] = first[g]

    def tile_of(source):
        return lambda g: source[8 * g : 8 * g + 8, :]

    def copy_to(at, step, mirrored):
        x, y, z = step
        s, t = side(-x), side(-y)
        if x and y:
            src = sent_e.at[at, pl.ds(2 * side(x) + side(y), 1)]
            dst = got_e.at[at, 0 if z == 0 else 1 + side(-z), pl.ds(2 * s + t, 1)]
        elif x:
            src, dst = sent_x.at[at, side(x)], got_x.at[at, s]
            if z:
                src = src.at[pl.ds(6 if z > 0 else 0, 1)]
                dst = got_xr.at[at, pl.ds(2 * s + side(-z), 1)]
        elif y:
            src, dst = sent_y.at[at, side(y)], got_y.at[at, t]
            if z:
                src = src.at[pl.ds(6 if z > 0 else 0, 1)]
                dst = got_yr.at[at, pl.ds(2 * t + side(-z), 1)]
        else:
            src, dst = sent_z.at[at, side(z)], got_z.at[at, side(-z)]
        e = AROUND.index(step)
        return pltpu.make_async_remote_copy(
            src_ref=src,
            dst_ref=dst,
            send_sem=halo_send.at[at, e],
            recv_sem=halo_recv.at[at, e],
            device_id=near(step, mirrored),
            device_id_type=MESH,
        )

    def start_copies(at, steps, mirrored):
        made = [copy_to(at, step, mirrored) for step in steps]
        for copy in made:
            copy.start()
        return made

    _, lane_18 = iotas(18)

    def put_z(at, s, source, sublane):
        lower = source[pl.ds(sublane, 18, stride=8), :]
        upper = source[pl.ds(144 + sublane, 18, stride=8), :]
        sent_z[at, s, 0:18, :] = jnp.where(lane_18 < 64, lower, roll(upper, 64))

    def take_z(at, s):
        rows = got_z[at, s]
        z_both[s, 0] = rows
        z_both[s, 1] = roll(rows, 64)

    def z_row(s, m):
        if m >= 36:
            return z_both[s, 0, m - 18 : m - 17, :]
        return z_both[s, m // 18, m % 18 : m % 18 + 1, :]

    def products(source):
        tiles = extended(tile_of(source))
        for v in range(49):
            grid_ext[8 * v : 8 * v + 8, :] = tiles[v]
        terms[...] = cell_terms(grid_ext[...], cell_matrix[0], cell_matrix[1], scales[0:1, :])

    def start_sums(at, source, factor, extra, mirrored):
        products(source)
        folded, x_high, y_high = local_fold(lambda v: terms[8 * v : 8 * v + 8, :])
        for g in range(36):
            part[8 * g : 8 * g + 8, :] = factor * folded[g] + extra(g)
        x_high, y_high = factor * x_high, factor * y_high
        faces[0], faces[1] = x_high, y_high
        xs, ys, edges = shared(tile_of(part), x_high, y_high)
        for s in range(2):
            sent_x[at, s] = xs[s]
            sent_y[at, s] = ys[s]
            put_z(at, s, part, 6 if s == 0 else 0)
            k = 6 if s == 0 else 0
            sent_z[at, s, 18:19, :] = x_high[k : k + 1]
            sent_z[at, s, 19:20, :] = y_high[k : k + 1]
        for c in range(4):
            sent_e[at, c : c + 1, :] = edges[c]
        return start_copies(at, AROUND, mirrored)

    def finish_sums(at, made):
        for copy in made:
            copy.wait_recv()
        take_z(at, 0)
        take_z(at, 1)
        return absorb(
            tile_of(part),
            faces[0],
            faces[1],
            [got_x[at, s] for s in range(2)],
            [[got_xr[at, 2 * s + t : 2 * s + t + 1, :] for t in range(2)] for s in range(2)],
            [got_y[at, s] for s in range(2)],
            [[got_yr[at, 2 * s + t : 2 * s + t + 1, :] for t in range(2)] for s in range(2)],
            [got_e[at, t] for t in range(3)],
            z_row,
            low,
            high,
        )

    x_tile, y_tile = low_faces(tile_of(own))
    sent_x[0, 1] = x_tile
    sent_y[0, 1] = y_tile
    sent_e[0, 3:4, :] = column_to_row(own[0:8, :], 0)
    put_z(0, 1, own, 0)
    pl.semaphore_wait(barrier, len(greeted))
    ghosts = start_copies(0, BELOW, False)

    for load in loads[1:]:
        load.wait()
    three = to_cells(
        [
            jnp.concatenate([pad[m, pl.ds(c, 8, stride=18), :] for m in (1, 2, 3)], axis=0)
            for c in range(18)
        ],
        table[...],
    )
    for g in range(36):
        rows = slice(8 * g, 8 * g + 8)
        screen[rows, :] = three[g][16:24]
        vec[0, rows, :] = FILTER_SCALE * ((three[g][8:16] - FILTER_CENTER) * own[rows, :]) - three[g][0:8]
    padded_matrix[...] = jnp.zeros_like(padded_matrix)
    padded_matrix[0:343, 0:343] = raw_matrix[...]
    by_row, by_column = node_rows(400), node_rows(512)
    for h, piece in enumerate(split(padded_matrix[...])):
        rows_moved = jnp.dot(by_row, piece, preferred_element_type=F32).astype(BF16)
        cell_matrix[h] = lax.dot_general(
            rows_moved, by_column, (((1,), (1,)), ((), ())), preferred_element_type=F32
        ).astype(BF16)
    _, lane_64 = iotas(64)
    first_id = 6 * 49 * ((lane_64 & 63) >> 3) + 6 * (lane_64 & 7)
    matches = jnp.where(first_id == jnp.broadcast_to(ids[:, 0:1], (64, 128)), 1.0, 0.0).astype(F32)
    given = jnp.broadcast_to(scale_ref[...], (8, 64))
    scales[...] = jnp.dot(given, matches, precision=lax.Precision.HIGHEST, preferred_element_type=F32)

    for copy in ghosts:
        copy.wait_recv()
    take_z(0, 0)
    compact = from_above(
        tile_of(own),
        got_x[0, 0],
        got_xr[0, 0:1, :],
        got_y[0, 0],
        got_yr[0, 0:1, :],
        got_e[0, 0, 0:1, :],
        got_e[0, 1, 0:1, :],
        lambda g: z_row(0, g),
        high,
    )
    for m in range(TILES):
        vec[1, 8 * m : 8 * m + 8, :] = compact[m]
    summing = start_sums(1, vec.at[1], 0.5 * FILTER_SCALE, tile_of(vec.at[0]), False)
    values = finish_sums(1, summing)
    weight = occupation_ref[0]
    squares = [weight * value * value for value in values]
    for m in range(20):
        tile = squares[m]
        if m + 20 < TILES:
            tile = tile + roll(squares[m + 20], 64)
        dens[8 * m : 8 * m + 8, :] = tile

    mine = pl.multiple_of(80 * core, 8)
    other = pl.multiple_of(80 * (1 - core), 8)

    def band_copy(src, dst, at_send, at_recv, device):
        return pltpu.make_async_remote_copy(
            src_ref=src,
            dst_ref=dst,
            send_sem=band_send.at[at_send],
            recv_sem=band_recv.at[at_recv],
            device_id=device,
            device_id_type=MESH,
        )

    swap = band_copy(dens.at[pl.ds(other, 80), :], dens_in, 0, 0, partner)
    swap.start()
    for m in range(36):
        vec[0, 8 * m : 8 * m + 8, :] = values[m]
    swap.wait_recv()
    half[...] = dens[pl.ds(mine, 80), :] + dens_in[...]

    not_first, not_last = z_lo > 0, z_lo < ZLO - 1
    slot_first = jnp.maximum(z_lo - 1, 0)
    slot_last = jnp.minimum(z_lo, ZLO - 2)
    to_first = band_copy(half, half_in.at[slot_first], 1, 1 + slot_first, chip(0))
    to_last = band_copy(half, half_in.at[slot_last], 2, 1 + slot_last, chip(ZLO - 1))

    @pl.when(not_first)
    def _():
        to_first.start()

    @pl.when(not_last)
    def _():
        to_last.start()

    natural = from_cells([jnp.where(row < 6, vec[0, 8 * g : 8 * g + 8, :], 0.0) for g in range(36)], table[...])
    for c in range(18):
        nat_f[pl.ds(c, 8, stride=18), :] = natural[c]
    store = pltpu.make_async_copy(nat_f.at[pl.ds(0, 108), :], filtered_ref.at[:, 0, :], out_sem)
    store.start()

    is_end = (z_lo == 0) | (z_lo == ZLO - 1)
    B, W, Q, R1, W1 = 0, 1, 2, 3, 4

    @pl.when(is_end)
    def _():
        arrived = [band_copy(half, half_in.at[s], 1, 1 + s, partner) for s in range(ZLO - 1)]
        for copy in arrived:
            copy.wait_recv()
        total = half[...]
        for s in range(ZLO - 1):
            total = total + half_in[s]
        full_in[0] = total * (1.0 / STATES)
        again = band_copy(full_in.at[0], full_in.at[1], 3, 6, partner)
        again.start()
        again.wait_recv()
        both = (
            jnp.where(core == 0, full_in[0], full_in[1]),
            jnp.where(core == 0, full_in[1], full_in[0]),
        )
        for m in range(20):
            tile = both[m // 10][8 * (m % 10) : 8 * (m % 10) + 8]
            vec[B, 8 * m : 8 * m + 8, :] = jnp.where(lane < 64, tile, 0.0)
            if m + 20 < TILES:
                vec[B, 8 * (m + 20) : 8 * (m + 20) + 8, :] = jnp.where(lane < 64, roll(tile, 64), 0.0)

        def put(v, tiles):
            for m in range(TILES):
                vec[v, 8 * m : 8 * m + 8, :] = tiles[m]

        def screened(v):
            return lambda g: screen[8 * g : 8 * g + 8, :] * vec[v, 8 * g : 8 * g + 8, :]

        def onto_row(got):
            got = jnp.sum(got.reshape(36, 8, 128), axis=0)
            return jnp.sum(jnp.where(row < 6, got, 0.0), axis=0, keepdims=True)

        def dot_row(a, b):
            return onto_row(vec[a, 0:CORE_ROWS, :] * vec[b, 0:CORE_ROWS, :])

        def send_reduce(n, level, devices):
            made = [
                pltpu.make_async_remote_copy(
                    src_ref=red_out.at[n, level],
                    dst_ref=red_in.at[n, level, e],
                    send_sem=red_send.at[n, level, e],
                    recv_sem=red_recv.at[n, level, e],
                    device_id=device,
                    device_id_type=MESH,
                )
                for e, device in enumerate(devices)
            ]
            for copy in made:
                copy.start()
            return made

        def start_reduce(n, rows):
            tile = jnp.zeros((8, 128), F32)
            for m, values in enumerate(rows):
                tile = jnp.where(row == m, wide(values), tile)
            red_out[n, 0] = tile
            return send_reduce(n, 0, group_one)

        def take(n, level, made):
            for copy in made:
                copy.wait_recv()
            got = red_out[n, level]
            for e in range(7):
                got = got + red_in[n, level, e]
            return got

        def second_level(n, made):
            red_out[n, 1] = take(n, 0, made)
            return send_reduce(n, 1, group_two)

        def scalars(n, made, count):
            got = jnp.sum(take(n, 1, made), axis=1, keepdims=True)
            return [got[m : m + 1] for m in range(count)]

        def hand_on(n, v):
            natural = from_cells(
                [jnp.where(row < 6, vec[v, 8 * g : 8 * g + 8, :], 0.0) for g in range(36)], table[...]
            )
            for c in range(18):
                nat[n, pl.ds(c, 8, stride=18), :] = natural[c]
            return onward(nat.at[n, 0:112], nat.at[n, 0:112], n)

        def onward(src, dst, n):
            made = [
                band_copy(src, dst, 4 + 2 * n + s, 7 + n, chip(jnp.where(z_lo == 0, 1 + s, ZLO - 2 - s)))
                for s in range(2)
            ]
            for copy in made:
                copy.start()
            return made

        sent = [again]
        made = start_sums(2, vec.at[B], 1.0, screened(B), True)
        sent += made + hand_on(0, B)
        put(W, finish_sums(2, made))

        red_a = start_reduce(0, [dot_row(B, B), dot_row(B, W)])
        made = start_sums(3, vec.at[W], 1.0, screened(W), True)
        red_b = second_level(0, red_a)
        sent += made + red_a + red_b + hand_on(1, W)
        put(Q, finish_sums(3, made))
        norm_0, image_0 = scalars(0, red_b, 2)
        alpha_0 = norm_0 / image_0

        vec[R1] = vec[B] - alpha_0 * vec[W]
        vec[W1] = vec[W] - alpha_0 * vec[Q]
        products(vec.at[W1])
        energy = jnp.sum((grid_ext[0:392, :] * terms[0:392, :]).reshape(49, 8, 128), axis=0)
        energy = jnp.sum(jnp.where(lane < 64, energy, 0.0), axis=0, keepdims=True)
        owned = vec[W1, 0:CORE_ROWS, :]
        energy = energy + onto_row(screen[...] * owned * owned)
        red_a = start_reduce(
            1,
            [
                dot_row(R1, R1),
                dot_row(R1, W1),
                dot_row(R1, W),
                dot_row(W1, W1),
                dot_row(W1, W),
                energy,
                dot_row(W1, Q),
                dot_row(W, Q),
            ],
        )
        sent += hand_on(2, Q)
        red_b = second_level(1, red_a)
        norm_1, rw, rv, ww, wv, waw, wav, vav = scalars(1, red_b, 8)
        c_b, c_w, c_q = combine(alpha_0, norm_0, image_0, norm_1, rw, rv, ww, wv, waw, wav, vav)
        tile = jnp.where(row == 0, wide(c_b), jnp.where(row == 1, wide(c_w), wide(c_q)))
        factors[0] = tile
        sent += red_a + red_b + onward(factors.at[0], factors.at[1], 3)
        field_ref[...] = c_b * nat[0, 0:108, :] + c_w * nat[1, 0:108, :] + c_q * nat[2, 0:108, :]
        for copy in sent:
            copy.wait_send()

    @pl.when(jnp.logical_not(is_end))
    def _():
        for n in range(3):
            band_copy(nat.at[n, 0:112], nat.at[n, 0:112], 4, 7 + n, partner).wait_recv()
        band_copy(factors.at[0], factors.at[1], 4, 10, partner).wait_recv()
        field_ref[...] = (
            factors[1, 0:1, :] * nat[0, 0:108, :]
            + factors[1, 1:2, :] * nat[1, 0:108, :]
            + factors[1, 2:3, :] * nat[2, 0:108, :]
        )

    swap.wait_send()

    @pl.when(not_first)
    def _():
        to_first.wait_send()

    @pl.when(not_last)
    def _():
        to_last.wait_send()

    for copy in ghosts + summing:
        copy.wait_send()
    store.wait()


def combine(alpha_0, norm_0, image_0, norm_1, rw, rv, ww, wv, waw, wav, vav):
    beta_1 = norm_1 / norm_0
    image_1 = rw + 2.0 * beta_1 * rv + beta_1 * beta_1 * image_0
    alpha_1 = norm_1 / image_1
    r_s = rw + beta_1 * rv
    s_s = ww + 2.0 * beta_1 * wv + beta_1 * beta_1 * (wv_self(alpha_0, wv, vav))
    r_as = ww + beta_1 * wv
    s_as = waw + 2.0 * beta_1 * wav + beta_1 * beta_1 * vav
    norm_2 = jnp.maximum(norm_1 - 2.0 * alpha_1 * r_s + alpha_1 * alpha_1 * s_s, 0.0)
    r2_ar2 = rw - 2.0 * alpha_1 * r_as + alpha_1 * alpha_1 * s_as
    r2_s = r_s - alpha_1 * s_s
    beta_2 = norm_2 / norm_1
    image_2 = r2_ar2 + 2.0 * beta_2 * r2_s + beta_2 * beta_2 * image_1
    alpha_2 = jnp.where(image_2 > 0.0, norm_2 / image_2, 0.0)
    grown = alpha_0 + alpha_1 * (1.0 + beta_1)
    c_b = grown + alpha_2 * (1.0 + beta_2 * (1.0 + beta_1))
    c_w = -alpha_1 * alpha_0 - alpha_2 * (grown + beta_2 * alpha_0)
    c_q = alpha_2 * alpha_1 * alpha_0
    return c_b, c_w, c_q


def wv_self(alpha_0, wv, vav):
    return wv + alpha_0 * vav


def per_device(states, previous, potential, screening, occupation, cell_scale, cell_matrix, connectivity):
    vmem = pl.BlockSpec(memory_space=pltpu.VMEM)
    anywhere = pl.BlockSpec(memory_space=pl.ANY)
    scalar = pl.BlockSpec(memory_space=pltpu.SMEM)
    filtered, field = pl.pallas_call(
        kernel,
        out_shape=(jax.ShapeDtypeStruct((108, 1, 128), F32), jax.ShapeDtypeStruct((108, 128), F32)),
        in_specs=[anywhere] * 4 + [scalar, vmem, anywhere, anywhere],
        out_specs=(anywhere, vmem),
        scratch_shapes=[
            pltpu.VMEM((4, 144, 128), F32),
            pltpu.VMEM((343, 343), F32),
            pltpu.VMEM((64, 128), jnp.int32),
            pltpu.VMEM((384, 384), BF16),
            pltpu.VMEM((384, 384), F32),
            pltpu.VMEM((2, 400, 512), BF16),
            pltpu.VMEM((8, 128), F32),
            pltpu.VMEM((288, 128), F32),
            pltpu.VMEM((288, 128), F32),
            pltpu.VMEM((5, ROWS, 128), F32),
            pltpu.VMEM((512, 128), F32),
            pltpu.VMEM((400, 128), F32),
            pltpu.VMEM((288, 128), F32),
            pltpu.VMEM((2, 8, 128), F32),
            pltpu.VMEM((4, 2, 8, 128), F32),
            pltpu.VMEM((4, 2, 8, 128), F32),
            pltpu.VMEM((4, 2, 24, 128), F32),
            pltpu.VMEM((4, 8, 128), F32),
            pltpu.VMEM((4, 2, 8, 128), F32),
            pltpu.VMEM((4, 2, 8, 128), F32),
            pltpu.VMEM((4, 2, 24, 128), F32),
            pltpu.VMEM((4, 8, 128), F32),
            pltpu.VMEM((4, 8, 128), F32),
            pltpu.VMEM((4, 3, 8, 128), F32),
            pltpu.VMEM((2, 2, 24, 128), F32),
            pltpu.VMEM((160, 128), F32),
            pltpu.VMEM((80, 128), F32),
            pltpu.VMEM((80, 128), F32),
            pltpu.VMEM((5, 80, 128), F32),
            pltpu.VMEM((2, 80, 128), F32),
            pltpu.VMEM((2, 2, 8, 128), F32),
            pltpu.VMEM((2, 2, 7, 8, 128), F32),
            pltpu.VMEM((3, 144, 128), F32),
            pltpu.VMEM((144, 128), F32),
            pltpu.VMEM((2, 8, 128), F32),
            pltpu.SemaphoreType.DMA((6,)),
            pltpu.SemaphoreType.DMA,
            pltpu.SemaphoreType.DMA((4, 26)),
            pltpu.SemaphoreType.DMA((4, 26)),
            pltpu.SemaphoreType.DMA((12,)),
            pltpu.SemaphoreType.DMA((11,)),
            pltpu.SemaphoreType.DMA((2, 2, 7)),
            pltpu.SemaphoreType.DMA((2, 2, 7)),
        ],
        compiler_params=pltpu.CompilerParams(collective_id=0, has_side_effects=True),
        name="step",
    )(
        states.reshape(108, 1, 128),
        previous.reshape(108, 1, 128),
        potential.reshape(108, 128),
        screening.reshape(108, 128),
        occupation,
        cell_scale.reshape(1, 64),
        cell_matrix,
        connectivity.T,
    )
    return filtered.reshape(1, 13824), field.reshape(13824)


def solution(mesh):
    in_specs = (
        P("band", "dom"),
        P("band", "dom"),
        P("dom"),
        P("dom"),
        P("band"),
        P("dom"),
        P(),
        P(None, "dom"),
    )
    out_specs = (P("band", "dom"), P("dom"))
    return jax.shard_map(per_device, mesh=mesh, in_specs=in_specs, out_specs=out_specs, check_vma=False)
```

```python
import jax
import jax.numpy as jnp
from jax import lax
from jax.experimental import pallas as pl
from jax.experimental.pallas import tpu as pltpu
from jax.sharding import PartitionSpec as P

MESH = pl.DeviceIdType.MESH
F32 = jnp.float32
BF16 = jnp.bfloat16
STATES = 12
ZLO = 6
FILTER_CENTER = 2.0
FILTER_SCALE = 2.0 / 2.0


AROUND = [(x, y, z) for y in (1, -1, 0) for x in (1, -1, 0) for z in (1, -1, 0) if (x, y, z) != (0, 0, 0)]
LEVEL = [d for d in AROUND if d[1] == 0]
BELOW = [d for d in LEVEL if max(d) <= 0]
TILES = 38
CORE_ROWS = 288
ROWS = 8 * TILES


def side(step):
    return 0 if step > 0 else 1

def roll(x, by, axis=1):
    by = by % x.shape[axis]
    return x if by == 0 else pltpu.roll(x, by, axis)


def iotas(rows=8, lanes=128):
    row = lax.broadcasted_iota(jnp.int32, (rows, lanes), 0)
    lane = lax.broadcasted_iota(jnp.int32, (rows, lanes), 1)
    return row, lane


def split(x):
    high = x.astype(BF16)
    return high, (x - high.astype(F32)).astype(BF16)


def column_table():
    row, lane = iotas(384, 384)
    g, cx = lane >> 3, lane & 7
    j = (g * 43) >> 8
    wanted = j * 48 + cx * 6 + (g - 6 * j)
    return jnp.where((row == wanted) & (lane < 288), 1.0, 0.0).astype(BF16)


def node_rows(rows):
    row, lane = iotas(rows, 384)
    k, v = row & 7, row >> 3
    return jnp.where((lane == 49 * k + v) & (k < 7) & (v < 49), 1.0, 0.0).astype(BF16)


def to_cells(tiles, table):
    n = tiles[0].shape[0]
    row, lane = iotas(n)
    group = lane >> 3
    chunks = []
    for cy in range(8):
        first, off = 288 * cy // 128, 288 * cy % 128
        parts = []
        for m in range(3):
            one = tiles[(first + m) % 18]
            if off:
                two = tiles[(first + m + 1) % 18]
                one = jnp.where(lane < 128 - off, roll(one, -off), roll(two, -off))
            parts.append(one)
        chunks.append(jnp.concatenate(parts, axis=1))
    stacked = jnp.concatenate(chunks, axis=0)
    high, low = split(stacked)
    both = jnp.dot(jnp.concatenate([high, low], axis=0), table, preferred_element_type=F32)
    moved = both[: 8 * n] + both[8 * n :]
    skewed = [
        [roll(moved[n * cy : n * cy + n, 128 * a : 128 * a + 128], 8 * cy) for a in range(3)]
        for cy in range(8)
    ]
    out = []
    for g in range(36):
        a, b = g // 16, g % 16
        got = jnp.where(group == b, skewed[0][a], 0.0)
        for cy in range(1, 8):
            got = jnp.where(group == (b + cy) % 16, skewed[cy][a], got)
        out.append(roll(got, -8 * b))
    return out


def split_exact(x):
    high, low = split(x)
    return high, low, (x - high.astype(F32) - low.astype(F32)).astype(BF16)


def from_cells(tiles, table):
    row, lane = iotas(8)
    group = lane >> 3
    placed = [roll(tiles[g], 8 * (g % 16)) for g in range(36)]
    rows = []
    for cy in range(8):
        parts = []
        for a in range(3):
            count = 16 if a < 2 else 4
            got = jnp.zeros((8, 128), F32)
            for b in range(count):
                got = jnp.where(group == (b + cy) % 16, placed[16 * a + b], got)
            parts.append(roll(got, -8 * cy))
        rows.append(jnp.concatenate(parts, axis=1))
    stacked = jnp.concatenate(rows, axis=0)
    both = lax.dot_general(
        jnp.concatenate(split_exact(stacked), axis=0), table, (((1,), (1,)), ((), ())), preferred_element_type=F32
    )
    moved = both[:64] + both[64:128] + both[128:]
    out = []
    for c in range(18):
        got = jnp.zeros((8, 128), F32)
        for cy in range(8):
            start = 288 * cy - 128 * c
            lo, hi = max(start, 0), min(start + 288, 128)
            if lo >= hi:
                continue
            off = start % 128
            for m in range(3):
                begin = start + 128 * m
                one_lo, one_hi = max(begin, lo), min(begin + 128, hi)
                if one_lo >= one_hi:
                    continue
                piece = roll(moved[8 * cy : 8 * cy + 8, 128 * m : 128 * m + 128], off)
                got = jnp.where((lane >= one_lo) & (lane < one_hi), piece, got)
        out.append(got)
    return out


def cell_terms(tiles, matrix_high, matrix_low, scale_row):
    high = tiles.astype(BF16).astype(F32)
    low = tiles - high
    _, lane = iotas(512)
    both = jnp.where(lane < 64, high, roll(low, 64)).astype(BF16)
    got = jnp.dot(matrix_high, both, preferred_element_type=F32)
    got = got + jnp.dot(matrix_low, both, preferred_element_type=F32)
    got = got + roll(got, 64)
    return got * scale_row


def local_fold(term):
    row, lane = iotas()
    cx, cy = lane & 7, lane >> 3
    upper_x = []
    for j in range(6):
        got = term(7 * j + 6)
        if j == 0:
            got = got + jnp.where(cy >= 1, roll(term(48), 8), 0.0)
        upper_x.append(got)
    x_tile = jnp.where(lane == 62, roll(term(48), -1), 0.0)
    for j in range(6):
        x_tile = jnp.where((cx == j) & (cy < 8), roll(upper_x[j], j - 7), x_tile)
    y_tile = jnp.zeros((8, 128), F32)
    for i in range(6):
        got = term(42 + i)
        if i == 0:
            got = got + jnp.where(cx >= 1, roll(term(48), 1), 0.0)
        y_tile = jnp.where(cy == i, roll(got, 8 * i - 56), y_tile)
    out = []
    for g in range(36):
        j, i = g // 6, g % 6
        got = term(7 * j + i)
        if j == 0:
            got = got + jnp.where(cy >= 1, roll(term(42 + i), 8), 0.0)
        if i == 0:
            got = got + jnp.where(cx >= 1, roll(upper_x[j], 1), 0.0)
        out.append(got)
    return out, x_tile, y_tile


def column_to_row(tile, at):
    row, lane = iotas()
    return jnp.sum(jnp.where(row == lane, jnp.broadcast_to(tile[:, at : at + 1], (8, 128)), 0.0), axis=0, keepdims=True)


def row_to_column(values):
    row, lane = iotas()
    return jnp.sum(jnp.where(row == lane, jnp.broadcast_to(values, (8, 128)), 0.0), axis=1, keepdims=True)


def wide(values):
    return jnp.broadcast_to(values, (8, 128))


def low_faces(field):
    row, lane = iotas()
    cx, cy = lane & 7, lane >> 3
    x_tile = jnp.zeros((8, 128), F32)
    y_tile = jnp.zeros((8, 128), F32)
    for j in range(6):
        x_tile = jnp.where((cx == j) & (cy < 8), roll(field(6 * j), j), x_tile)
    for i in range(6):
        y_tile = jnp.where(cy == i, roll(field(i), 8 * i), y_tile)
    return x_tile, y_tile


def from_above(field, x_tile, x_row, y_all, y_row, z_row, high):
    row, _ = iotas()
    hx, _, hz = high
    x_all = hx * jnp.where(row == 6, wide(x_row * hz), x_tile)
    y_all = jnp.where(row == 6, wide(y_row * hz), y_all)
    core = [jnp.where(row == 6, wide(z_row(g) * hz), field(g)) for g in range(36)]
    return core + [x_all, y_all]


def extended(field):
    row, lane = iotas()
    cx, cy = lane & 7, lane >> 3
    x_all, y_all = field(36), field(37)
    out = [None] * 49
    for g in range(36):
        out[7 * (g // 6) + g % 6] = field(g)
    for j in range(6):
        out[7 * j + 6] = jnp.where(cx == 7, roll(x_all, 7 - j), roll(field(6 * j), -1))
    for i in range(6):
        out[42 + i] = jnp.where(cy == 7, roll(y_all, 56 - 8 * i), roll(field(i), -8))
    corner = jnp.where(cx == 7, roll(x_all, -1), roll(field(0), -9))
    corner = jnp.where(cy == 7, roll(y_all, 55), corner)
    out[48] = jnp.where(lane == 63, roll(x_all, 1), corner)
    return out


def shared(part, x_high, y_high):
    row, lane = iotas()
    x_low, y_low = low_faces(part)
    x_low = jnp.where(lane == 62, roll(y_high, 62), x_low)
    y_out = jnp.where(lane == 55, roll(x_high, -7), y_high)
    y_low = jnp.where(lane == 55, roll(x_high, 55), y_low)
    edges = [column_to_row(t, at) for t in (x_high, x_low) for at in (62, 0)]
    return (x_high, x_low), (y_out, y_low), edges


def with_y(part, x_high, y_high, y_up, y_down):
    row, lane = iotas()
    cy = lane >> 3
    first = [part(i) + jnp.where(cy == 0, roll(y_down, -8 * i), 0.0) for i in range(6)]
    x_high = x_high + jnp.where(lane == 62, roll(y_up, 7), jnp.where(lane == 0, roll(y_down, -55), 0.0))
    return first, x_high, y_high + jnp.where(cy < 6, y_up, 0.0)


def absorb_level(part, x_high, y_high, xs, x_rows, z_row, low, high):
    row, lane = iotas()
    cx, cy = lane & 7, lane >> 3
    hx, hy, hz = high
    lx, _, lz = low
    up_row, down_row = row == 6, row == 0

    def vertical(up, down):
        return jnp.where(up_row, wide(up), jnp.where(down_row, wide(down * lz), 0.0))

    x_up = xs[0] + vertical(x_rows[0][0], x_rows[0][1])
    x_down = (xs[1] + vertical(x_rows[1][0], x_rows[1][1])) * lx
    x_all = x_high + x_up + vertical(z_row(0, 36), z_row(1, 36))
    y_all = y_high + vertical(z_row(0, 37), z_row(1, 37))
    y_all = y_all + jnp.where(lane == 0, roll(x_down, -62), 0.0)
    top = jnp.where(up_row, hz, 1.0)
    x_all = x_all * (top * hx) * jnp.where(lane == 62, hy, 1.0)
    y_all = y_all * (top * hy)
    out = []
    for g in range(36):
        got = part(g) + vertical(z_row(0, g), z_row(1, g))
        if g % 6 == 0:
            got = got + jnp.where((cx == 0) & (cy < 8), roll(x_down, -(g // 6)), 0.0)
        out.append(jnp.where(lane < 64, got * top, 0.0))
    return out + [x_all, y_all]


def absorb(part, x_high, y_high, xs, x_rows, ys, y_rows, edges, z_row, low, high):
    row, lane = iotas()
    cx, cy = lane & 7, lane >> 3
    hx, hy, hz = high
    lx, ly, lz = low

    def with_rows(tile, rows):
        return tile + jnp.where(row == 6, wide(rows[0]), jnp.where(row == 0, wide(rows[1] * lz), 0.0))

    x_up, x_down = with_rows(xs[0], x_rows[0]), with_rows(xs[1], x_rows[1]) * lx
    y_up, y_down = with_rows(ys[0], y_rows[0]), with_rows(ys[1], y_rows[1]) * ly
    lines = edges[0] + jnp.where(lane == 6, roll(edges[1], 6), jnp.where(lane == 0, roll(edges[2] * lz, -6), 0.0))
    columns = [wide(row_to_column(lines[c : c + 1])) for c in range(4)]
    up_row, down_row = row == 6, row == 0

    def vertical(up, down):
        return jnp.where(up_row, wide(up), jnp.where(down_row, wide(down * lz), 0.0))

    x_all = x_high + x_up + vertical(z_row(0, 36), z_row(1, 36))
    x_all = x_all + jnp.where(lane == 62, roll(y_up, 7) + columns[0], 0.0)
    x_all = x_all + jnp.where(lane == 0, roll(y_down, -55) + columns[1] * ly, 0.0)
    y_all = y_high + jnp.where(cy < 6, y_up, 0.0) + vertical(z_row(0, 37), z_row(1, 37))
    y_all = y_all + jnp.where(lane == 0, roll(x_down, -62) + columns[2] * lx, 0.0)
    top = jnp.where(up_row, hz, 1.0)
    x_all = x_all * (top * hx) * jnp.where(lane == 62, hy, 1.0)
    y_all = y_all * (top * hy)
    inside = jnp.where(lane < 64, top, 0.0)
    out = []
    for g in range(36):
        j, i = g // 6, g % 6
        got = part(g) + vertical(z_row(0, g), z_row(1, g))
        if i == 0:
            got = got + jnp.where((cx == 0) & (cy < 8), roll(x_down, -j), 0.0)
        if j == 0:
            got = got + jnp.where(cy == 0, roll(y_down, -8 * i), 0.0)
        if g == 0:
            got = got + jnp.where(lane == 0, columns[3] * (lx * ly), 0.0)
        out.append(jnp.where(lane < 64, got * inside, 0.0))
    return out + [x_all, y_all]


def kernel(
    states_ref, previous_ref, potential_ref, screening_ref, occupation_ref, scale_ref, matrix_ref, ids_ref,
    filtered_ref, field_ref,
    pad, raw_matrix, ids, table, padded_matrix, cell_matrix, scales,
    own, screen, vec, grid_ext, terms, part, faces,
    sent_x, sent_y, sent_z, sent_e, got_x, got_y, got_z, got_xr, got_yr, got_e, z_both,
    dens, dens_in, half, half_in, full_in, red_out, red_in, nat, nat_f, factors,
    in_sem, out_sem, halo_send, halo_recv, band_send, band_recv, red_send, red_recv,
):
    dom, band = lax.axis_index("dom"), lax.axis_index("band")
    px, py, pz = lax.rem(dom, 4), lax.rem(lax.div(dom, 4), 4), lax.div(dom, 16)
    z_lo, core = lax.div(band, 2), lax.rem(band, 2)
    z_hi = lax.rem(py, 2)
    across = 2 * (ZLO - 1 - z_lo) + core

    def place(x, y, z):
        return x + 4 * y + 16 * z

    def near(step, mirrored):
        x = lax.rem(px + (step[0] + 4), 4)
        y = lax.rem(py + (step[1] + 4), 4)
        z = lax.rem(pz + (step[2] + 4), 4)
        return (place(x, y, z), across if mirrored and step[1] else band)

    partner = (dom, 2 * z_lo + (1 - core))

    def chip(z):
        return (dom, 2 * z + core)

    y_at = lax.div(dom, 8)
    group_one, group_two = [], []
    for e in range(1, 8):
        x = lax.rem(px + e % 4, 4)
        y = py + 1 - 2 * z_hi if e // 4 else py
        group_one.append((place(x, y, pz), across if e // 4 else band))
    for e in range(1, 8):
        group_two.append((lax.rem(dom, 8) + 8 * lax.rem(y_at + e, 8), band))

    is_end = (z_lo == 0) | (z_lo == ZLO - 1)
    greeted = [near((0, 1, 0), False), near((0, -1, 0), False)] + [near(step, False) for step in LEVEL]
    greeted.append(partner)
    greeted += [chip(lax.rem(z_lo + e, ZLO)) for e in range(1, ZLO)]
    ends_greeted = [near(step, True) for step in AROUND if step[1]] + group_one + group_two
    barrier = pltpu.get_barrier_semaphore()

    def greet(devices):
        for device in devices:
            pl.semaphore_signal(barrier, inc=1, device_id=device, device_id_type=MESH)

    greet(greeted)

    @pl.when(is_end)
    def _():
        greet(ends_greeted)

    loads = [
        pltpu.make_async_copy(states_ref.at[:, 0, :], pad.at[0, pl.ds(0, 108), :], in_sem.at[0]),
        pltpu.make_async_copy(previous_ref.at[:, 0, :], pad.at[1, pl.ds(0, 108), :], in_sem.at[1]),
        pltpu.make_async_copy(potential_ref, pad.at[2, pl.ds(0, 108), :], in_sem.at[2]),
        pltpu.make_async_copy(screening_ref, pad.at[3, pl.ds(0, 108), :], in_sem.at[3]),
        pltpu.make_async_copy(matrix_ref, raw_matrix, in_sem.at[4]),
        pltpu.make_async_copy(ids_ref.at[:, pl.ds(0, 128)], ids, in_sem.at[5]),
    ]
    for load in loads:
        load.start()

    def flag(test):
        return jnp.where(test, 1.0, 0.0).astype(F32)

    high = (flag(px < 3), flag(py < 3), flag(pz < 3))
    low = (flag(px > 0), flag(py > 0), flag(pz > 0))
    row, lane = iotas()

    table[...] = column_table()
    for m in range(4):
        pad[m, 108:144, :] = jnp.zeros((36, 128), F32)
    grid_ext[...] = jnp.zeros_like(grid_ext)
    sent_z[...] = jnp.zeros_like(sent_z)
    loads[0].wait()
    first = to_cells([pad[0, pl.ds(c, 8, stride=18), :] for c in range(18)], table[...])
    for g in range(36):
        own[8 * g : 8 * g + 8, :] = first[g]

    def tile_of(source):
        return lambda g: source[8 * g : 8 * g + 8, :]

    def copy_to(at, step, mirrored):
        x, y, z = step
        s, t = side(-x), side(-y)
        if x and y:
            src = sent_e.at[at, pl.ds(2 * side(x) + side(y), 1)]
            dst = got_e.at[at, 0 if z == 0 else 1 + side(-z), pl.ds(2 * s + t, 1)]
        elif x:
            src, dst = sent_x.at[at, side(x)], got_x.at[at, s]
            if z:
                src = src.at[pl.ds(6 if z > 0 else 0, 1)]
                dst = got_xr.at[at, pl.ds(2 * s + side(-z), 1)]
        elif y:
            src, dst = sent_y.at[at, side(y)], got_y.at[at, t]
            if z:
                src = src.at[pl.ds(6 if z > 0 else 0, 1)]
                dst = got_yr.at[at, pl.ds(2 * t + side(-z), 1)]
        else:
            src, dst = sent_z.at[at, side(z)], got_z.at[at, side(-z)]
        e = AROUND.index(step)
        return pltpu.make_async_remote_copy(
            src_ref=src,
            dst_ref=dst,
            send_sem=halo_send.at[at, e],
            recv_sem=halo_recv.at[at, e],
            device_id=near(step, mirrored),
            device_id_type=MESH,
        )

    def start_copies(at, steps, mirrored):
        made = [copy_to(at, step, mirrored) for step in steps]
        for copy in made:
            copy.start()
        return made

    _, lane_18 = iotas(18)

    def put_z(at, s, source, sublane):
        lower = source[pl.ds(sublane, 18, stride=8), :]
        upper = source[pl.ds(144 + sublane, 18, stride=8), :]
        sent_z[at, s, 0:18, :] = jnp.where(lane_18 < 64, lower, roll(upper, 64))

    def take_z(at, s):
        rows = got_z[at, s]
        z_both[s, 0] = rows
        z_both[s, 1] = roll(rows, 64)

    def z_row(s, m):
        if m >= 36:
            return z_both[s, 0, m - 18 : m - 17, :]
        return z_both[s, m // 18, m % 18 : m % 18 + 1, :]

    def products(source):
        tiles = extended(tile_of(source))
        for v in range(49):
            grid_ext[8 * v : 8 * v + 8, :] = tiles[v]
        terms[...] = cell_terms(grid_ext[...], cell_matrix[0], cell_matrix[1], scales[0:1, :])

    def cell_sums(source, factor, extra):
        products(source)
        folded, x_high, y_high = local_fold(lambda v: terms[8 * v : 8 * v + 8, :])
        for g in range(36):
            part[8 * g : 8 * g + 8, :] = factor * folded[g] + extra(g)
        faces[0], faces[1] = factor * x_high, factor * y_high

    def put_level(at, xs, x_high, y_high):
        for s in range(2):
            k = 6 if s == 0 else 0
            sent_x[at, s] = xs[s]
            put_z(at, s, part, k)
            sent_z[at, s, 18:19, :] = x_high[k : k + 1]
            sent_z[at, s, 19:20, :] = y_high[k : k + 1]

    def start_sums(at, source, factor, extra, mirrored):
        cell_sums(source, factor, extra)
        x_high, y_high = faces[0], faces[1]
        xs, ys, edges = shared(tile_of(part), x_high, y_high)
        put_level(at, xs, x_high, y_high)
        for s in range(2):
            sent_y[at, s] = ys[s]
        for c in range(4):
            sent_e[at, c : c + 1, :] = edges[c]
        return start_copies(at, AROUND, mirrored)

    def finish_sums(at, made):
        for copy in made:
            copy.wait_recv()
        take_z(at, 0)
        take_z(at, 1)
        return absorb(
            tile_of(part),
            faces[0],
            faces[1],
            [got_x[at, s] for s in range(2)],
            [[got_xr[at, 2 * s + t : 2 * s + t + 1, :] for t in range(2)] for s in range(2)],
            [got_y[at, s] for s in range(2)],
            [[got_yr[at, 2 * s + t : 2 * s + t + 1, :] for t in range(2)] for s in range(2)],
            [got_e[at, t] for t in range(3)],
            z_row,
            low,
            high,
        )

    x_tile, y_tile = low_faces(tile_of(own))
    sent_y[0, 1] = y_tile
    put_z(0, 1, own, 0)

    @pl.when(is_end)
    def _():
        pl.semaphore_wait(barrier, len(greeted) + len(ends_greeted))

    @pl.when(jnp.logical_not(is_end))
    def _():
        pl.semaphore_wait(barrier, len(greeted))

    ghosts = start_copies(0, [(0, -1, 0)], False)

    for load in loads[1:]:
        load.wait()
    three = to_cells(
        [
            jnp.concatenate([pad[m, pl.ds(c, 8, stride=18), :] for m in (1, 2, 3)], axis=0)
            for c in range(18)
        ],
        table[...],
    )
    for g in range(36):
        rows = slice(8 * g, 8 * g + 8)
        screen[rows, :] = three[g][16:24]
        vec[0, rows, :] = FILTER_SCALE * ((three[g][8:16] - FILTER_CENTER) * own[rows, :]) - three[g][0:8]
    padded_matrix[...] = jnp.zeros_like(padded_matrix)
    padded_matrix[0:343, 0:343] = raw_matrix[...]
    by_row, by_column = node_rows(400), node_rows(512)
    for h, piece in enumerate(split(padded_matrix[...])):
        rows_moved = jnp.dot(by_row, piece, preferred_element_type=F32).astype(BF16)
        cell_matrix[h] = lax.dot_general(
            rows_moved, by_column, (((1,), (1,)), ((), ())), preferred_element_type=F32
        ).astype(BF16)
    _, lane_64 = iotas(64)
    first_id = 6 * 49 * ((lane_64 & 63) >> 3) + 6 * (lane_64 & 7)
    matches = jnp.where(first_id == jnp.broadcast_to(ids[:, 0:1], (64, 128)), 1.0, 0.0).astype(F32)
    given = jnp.broadcast_to(scale_ref[...], (8, 64))
    scales[...] = jnp.dot(given, matches, precision=lax.Precision.HIGHEST, preferred_element_type=F32)

    ghosts[0].wait_recv()
    y_all = got_y[0, 0] * high[1]
    sent_x[0, 1] = jnp.where(lane == 62, roll(y_all, 62), x_tile)
    sent_z[0, 1, 19:20, :] = y_all[0:1]
    ghosts_level = start_copies(0, BELOW, False)
    for copy in ghosts_level:
        copy.wait_recv()
    take_z(0, 0)
    compact = from_above(
        tile_of(own), got_x[0, 0], got_xr[0, 0:1, :], y_all, z_row(0, 37), lambda g: z_row(0, g), high
    )
    for m in range(TILES):
        vec[1, 8 * m : 8 * m + 8, :] = compact[m]

    cell_sums(vec.at[1], 0.5 * FILTER_SCALE, tile_of(vec.at[0]))
    x_high, y_high = faces[0], faces[1]
    _, ys, _ = shared(tile_of(part), x_high, y_high)
    for s in range(2):
        sent_y[1, s] = ys[s]
    summing = start_copies(1, [(0, 1, 0), (0, -1, 0)], False)
    for copy in summing:
        copy.wait_recv()
    along, x_high, y_high = with_y(tile_of(part), x_high, y_high, got_y[1, 0], got_y[1, 1] * low[1])
    for i in range(6):
        part[8 * i : 8 * i + 8, :] = along[i]
    xs, _, _ = shared(tile_of(part), x_high, y_high)
    put_level(1, xs, x_high, y_high)
    summing_level = start_copies(1, LEVEL, False)
    for copy in summing_level:
        copy.wait_recv()
    take_z(1, 0)
    take_z(1, 1)
    values = absorb_level(
        tile_of(part),
        x_high,
        y_high,
        [got_x[1, s] for s in range(2)],
        [[got_xr[1, 2 * s + t : 2 * s + t + 1, :] for t in range(2)] for s in range(2)],
        z_row,
        low,
        high,
    )
    weight = occupation_ref[0]
    squares = [weight * value * value for value in values]
    for m in range(20):
        tile = squares[m]
        if m + 20 < TILES:
            tile = tile + roll(squares[m + 20], 64)
        dens[8 * m : 8 * m + 8, :] = tile

    mine = pl.multiple_of(80 * core, 8)
    other = pl.multiple_of(80 * (1 - core), 8)

    def band_copy(src, dst, at_send, at_recv, device):
        return pltpu.make_async_remote_copy(
            src_ref=src,
            dst_ref=dst,
            send_sem=band_send.at[at_send],
            recv_sem=band_recv.at[at_recv],
            device_id=device,
            device_id_type=MESH,
        )

    swap = band_copy(dens.at[pl.ds(other, 80), :], dens_in, 0, 0, partner)
    swap.start()
    for m in range(36):
        vec[0, 8 * m : 8 * m + 8, :] = values[m]
    swap.wait_recv()
    half[...] = dens[pl.ds(mine, 80), :] + dens_in[...]

    not_first, not_last = z_lo > 0, z_lo < ZLO - 1
    slot_first = jnp.maximum(z_lo - 1, 0)
    slot_last = jnp.minimum(z_lo, ZLO - 2)
    to_first = band_copy(half, half_in.at[slot_first], 1, 1 + slot_first, chip(0))
    to_last = band_copy(half, half_in.at[slot_last], 2, 1 + slot_last, chip(ZLO - 1))

    @pl.when(not_first)
    def _():
        to_first.start()

    @pl.when(not_last)
    def _():
        to_last.start()

    natural = from_cells([jnp.where(row < 6, vec[0, 8 * g : 8 * g + 8, :], 0.0) for g in range(36)], table[...])
    for c in range(18):
        nat_f[pl.ds(c, 8, stride=18), :] = natural[c]
    store = pltpu.make_async_copy(nat_f.at[pl.ds(0, 108), :], filtered_ref.at[:, 0, :], out_sem)
    store.start()

    B, W, Q, R1, W1 = 0, 1, 2, 3, 4

    @pl.when(is_end)
    def _():
        arrived = [band_copy(half, half_in.at[s], 1, 1 + s, partner) for s in range(ZLO - 1)]
        for copy in arrived:
            copy.wait_recv()
        total = half[...]
        for s in range(ZLO - 1):
            total = total + half_in[s]
        full_in[0] = total * (1.0 / STATES)
        again = band_copy(full_in.at[0], full_in.at[1], 3, 6, partner)
        again.start()
        again.wait_recv()
        both = (
            jnp.where(core == 0, full_in[0], full_in[1]),
            jnp.where(core == 0, full_in[1], full_in[0]),
        )
        for m in range(20):
            tile = both[m // 10][8 * (m % 10) : 8 * (m % 10) + 8]
            vec[B, 8 * m : 8 * m + 8, :] = jnp.where(lane < 64, tile, 0.0)
            if m + 20 < TILES:
                vec[B, 8 * (m + 20) : 8 * (m + 20) + 8, :] = jnp.where(lane < 64, roll(tile, 64), 0.0)

        def put(v, tiles):
            for m in range(TILES):
                vec[v, 8 * m : 8 * m + 8, :] = tiles[m]

        def screened(v):
            return lambda g: screen[8 * g : 8 * g + 8, :] * vec[v, 8 * g : 8 * g + 8, :]

        def onto_row(got):
            got = jnp.sum(got.reshape(36, 8, 128), axis=0)
            return jnp.sum(jnp.where(row < 6, got, 0.0), axis=0, keepdims=True)

        def dot_row(a, b):
            return onto_row(vec[a, 0:CORE_ROWS, :] * vec[b, 0:CORE_ROWS, :])

        def send_reduce(n, level, devices):
            made = [
                pltpu.make_async_remote_copy(
                    src_ref=red_out.at[n, level],
                    dst_ref=red_in.at[n, level, e],
                    send_sem=red_send.at[n, level, e],
                    recv_sem=red_recv.at[n, level, e],
                    device_id=device,
                    device_id_type=MESH,
                )
                for e, device in enumerate(devices)
            ]
            for copy in made:
                copy.start()
            return made

        def start_reduce(n, rows):
            tile = jnp.zeros((8, 128), F32)
            for m, values in enumerate(rows):
                tile = jnp.where(row == m, wide(values), tile)
            red_out[n, 0] = tile
            return send_reduce(n, 0, group_one)

        def take(n, level, made):
            for copy in made:
                copy.wait_recv()
            got = red_out[n, level]
            for e in range(7):
                got = got + red_in[n, level, e]
            return got

        def second_level(n, made):
            red_out[n, 1] = take(n, 0, made)
            return send_reduce(n, 1, group_two)

        def scalars(n, made, count):
            got = jnp.sum(take(n, 1, made), axis=1, keepdims=True)
            return [got[m : m + 1] for m in range(count)]

        def hand_on(n, v):
            natural = from_cells(
                [jnp.where(row < 6, vec[v, 8 * g : 8 * g + 8, :], 0.0) for g in range(36)], table[...]
            )
            for c in range(18):
                nat[n, pl.ds(c, 8, stride=18), :] = natural[c]
            return onward(nat.at[n, 0:112], nat.at[n, 0:112], n)

        def onward(src, dst, n):
            made = [
                band_copy(src, dst, 4 + 2 * n + s, 7 + n, chip(jnp.where(z_lo == 0, 1 + s, ZLO - 2 - s)))
                for s in range(2)
            ]
            for copy in made:
                copy.start()
            return made

        def energy_row(v):
            cells = jnp.sum((grid_ext[0:392, :] * terms[0:392, :]).reshape(49, 8, 128), axis=0)
            cells = jnp.sum(jnp.where(lane < 64, cells, 0.0), axis=0, keepdims=True)
            owned = vec[v, 0:CORE_ROWS, :]
            return cells + onto_row(screen[...] * owned * owned)

        sent = [again]
        made = start_sums(2, vec.at[B], 1.0, screened(B), True)
        red_a = start_reduce(0, [dot_row(B, B), energy_row(B)])
        sent += made + red_a + hand_on(0, B)
        put(W, finish_sums(2, made))
        red_b = second_level(0, red_a)
        made = start_sums(3, vec.at[W], 1.0, screened(W), True)
        sent += made + red_b + hand_on(1, W)
        put(Q, finish_sums(3, made))
        norm_0, image_0 = scalars(0, red_b, 2)
        alpha_0 = norm_0 / image_0

        vec[R1] = vec[B] - alpha_0 * vec[W]
        vec[W1] = vec[W] - alpha_0 * vec[Q]
        products(vec.at[W1])
        red_a = start_reduce(
            1,
            [
                dot_row(R1, R1),
                dot_row(R1, W1),
                dot_row(R1, W),
                dot_row(W1, W1),
                dot_row(W1, W),
                energy_row(W1),
                dot_row(W1, Q),
                dot_row(W, Q),
            ],
        )
        sent += hand_on(2, Q)
        red_b = second_level(1, red_a)
        norm_1, rw, rv, ww, wv, waw, wav, vav = scalars(1, red_b, 8)
        c_b, c_w, c_q = combine(alpha_0, norm_0, image_0, norm_1, rw, rv, ww, wv, waw, wav, vav)
        tile = jnp.where(row == 0, wide(c_b), jnp.where(row == 1, wide(c_w), wide(c_q)))
        factors[0] = tile
        sent += red_a + red_b + onward(factors.at[0], factors.at[1], 3)
        field_ref[...] = c_b * nat[0, 0:108, :] + c_w * nat[1, 0:108, :] + c_q * nat[2, 0:108, :]
        for copy in sent:
            copy.wait_send()

    @pl.when(jnp.logical_not(is_end))
    def _():
        for n in range(3):
            band_copy(nat.at[n, 0:112], nat.at[n, 0:112], 4, 7 + n, partner).wait_recv()
        band_copy(factors.at[0], factors.at[1], 4, 10, partner).wait_recv()
        field_ref[...] = (
            factors[1, 0:1, :] * nat[0, 0:108, :]
            + factors[1, 1:2, :] * nat[1, 0:108, :]
            + factors[1, 2:3, :] * nat[2, 0:108, :]
        )

    swap.wait_send()

    @pl.when(not_first)
    def _():
        to_first.wait_send()

    @pl.when(not_last)
    def _():
        to_last.wait_send()

    for copy in ghosts + ghosts_level + summing + summing_level:
        copy.wait_send()
    store.wait()


def combine(alpha_0, norm_0, image_0, norm_1, rw, rv, ww, wv, waw, wav, vav):
    beta_1 = norm_1 / norm_0
    image_1 = rw + 2.0 * beta_1 * rv + beta_1 * beta_1 * image_0
    alpha_1 = norm_1 / image_1
    r_s = rw + beta_1 * rv
    s_s = ww + 2.0 * beta_1 * wv + beta_1 * beta_1 * (wv_self(alpha_0, wv, vav))
    r_as = ww + beta_1 * wv
    s_as = waw + 2.0 * beta_1 * wav + beta_1 * beta_1 * vav
    norm_2 = jnp.maximum(norm_1 - 2.0 * alpha_1 * r_s + alpha_1 * alpha_1 * s_s, 0.0)
    r2_ar2 = rw - 2.0 * alpha_1 * r_as + alpha_1 * alpha_1 * s_as
    r2_s = r_s - alpha_1 * s_s
    beta_2 = norm_2 / norm_1
    image_2 = r2_ar2 + 2.0 * beta_2 * r2_s + beta_2 * beta_2 * image_1
    alpha_2 = jnp.where(image_2 > 0.0, norm_2 / image_2, 0.0)
    grown = alpha_0 + alpha_1 * (1.0 + beta_1)
    c_b = grown + alpha_2 * (1.0 + beta_2 * (1.0 + beta_1))
    c_w = -alpha_1 * alpha_0 - alpha_2 * (grown + beta_2 * alpha_0)
    c_q = alpha_2 * alpha_1 * alpha_0
    return c_b, c_w, c_q


def wv_self(alpha_0, wv, vav):
    return wv + alpha_0 * vav


def per_device(states, previous, potential, screening, occupation, cell_scale, cell_matrix, connectivity):
    vmem = pl.BlockSpec(memory_space=pltpu.VMEM)
    anywhere = pl.BlockSpec(memory_space=pl.ANY)
    scalar = pl.BlockSpec(memory_space=pltpu.SMEM)
    filtered, field = pl.pallas_call(
        kernel,
        out_shape=(jax.ShapeDtypeStruct((108, 1, 128), F32), jax.ShapeDtypeStruct((108, 128), F32)),
        in_specs=[anywhere] * 4 + [scalar, vmem, anywhere, anywhere],
        out_specs=(anywhere, vmem),
        scratch_shapes=[
            pltpu.VMEM((4, 144, 128), F32),
            pltpu.VMEM((343, 343), F32),
            pltpu.VMEM((64, 128), jnp.int32),
            pltpu.VMEM((384, 384), BF16),
            pltpu.VMEM((384, 384), F32),
            pltpu.VMEM((2, 400, 512), BF16),
            pltpu.VMEM((8, 128), F32),
            pltpu.VMEM((288, 128), F32),
            pltpu.VMEM((288, 128), F32),
            pltpu.VMEM((5, ROWS, 128), F32),
            pltpu.VMEM((512, 128), F32),
            pltpu.VMEM((400, 128), F32),
            pltpu.VMEM((288, 128), F32),
            pltpu.VMEM((2, 8, 128), F32),
            pltpu.VMEM((4, 2, 8, 128), F32),
            pltpu.VMEM((4, 2, 8, 128), F32),
            pltpu.VMEM((4, 2, 24, 128), F32),
            pltpu.VMEM((4, 8, 128), F32),
            pltpu.VMEM((4, 2, 8, 128), F32),
            pltpu.VMEM((4, 2, 8, 128), F32),
            pltpu.VMEM((4, 2, 24, 128), F32),
            pltpu.VMEM((4, 8, 128), F32),
            pltpu.VMEM((4, 8, 128), F32),
            pltpu.VMEM((4, 3, 8, 128), F32),
            pltpu.VMEM((2, 2, 24, 128), F32),
            pltpu.VMEM((160, 128), F32),
            pltpu.VMEM((80, 128), F32),
            pltpu.VMEM((80, 128), F32),
            pltpu.VMEM((5, 80, 128), F32),
            pltpu.VMEM((2, 80, 128), F32),
            pltpu.VMEM((2, 2, 8, 128), F32),
            pltpu.VMEM((2, 2, 7, 8, 128), F32),
            pltpu.VMEM((3, 144, 128), F32),
            pltpu.VMEM((144, 128), F32),
            pltpu.VMEM((2, 8, 128), F32),
            pltpu.SemaphoreType.DMA((6,)),
            pltpu.SemaphoreType.DMA,
            pltpu.SemaphoreType.DMA((4, 26)),
            pltpu.SemaphoreType.DMA((4, 26)),
            pltpu.SemaphoreType.DMA((12,)),
            pltpu.SemaphoreType.DMA((11,)),
            pltpu.SemaphoreType.DMA((2, 2, 7)),
            pltpu.SemaphoreType.DMA((2, 2, 7)),
        ],
        compiler_params=pltpu.CompilerParams(collective_id=0, has_side_effects=True),
        name="step",
    )(
        states.reshape(108, 1, 128),
        previous.reshape(108, 1, 128),
        potential.reshape(108, 128),
        screening.reshape(108, 128),
        occupation,
        cell_scale.reshape(1, 64),
        cell_matrix,
        connectivity.T,
    )
    return filtered.reshape(1, 13824), field.reshape(13824)


def solution(mesh):
    in_specs = (
        P("band", "dom"),
        P("band", "dom"),
        P("dom"),
        P("dom"),
        P("band"),
        P("dom"),
        P(),
        P(None, "dom"),
    )
    out_specs = (P("band", "dom"), P("dom"))
    return jax.shard_map(per_device, mesh=mesh, in_specs=in_specs, out_specs=out_specs, check_vma=False)
```

```python
import jax
import jax.numpy as jnp
from jax import lax
from jax.experimental import pallas as pl
from jax.experimental.pallas import tpu as pltpu
from jax.sharding import PartitionSpec as P

MESH = pl.DeviceIdType.MESH
F32 = jnp.float32
BF16 = jnp.bfloat16
STATES = 12
ZLO = 6
FILTER_CENTER = 2.0
FILTER_SCALE = 2.0 / 2.0


AROUND = [(x, y, z) for y in (1, -1, 0) for x in (1, -1, 0) for z in (1, -1, 0) if (x, y, z) != (0, 0, 0)]
BELOW = [d for d in AROUND if max(d) <= 0]
TILES = 38
CORE_ROWS = 288
ROWS = 8 * TILES


class Guarded:
    def __init__(self, copy, goes, comes):
        self.copy, self.goes, self.comes = copy, goes, comes

    def start(self):
        pl.when(self.goes)(self.copy.start)

    def wait_send(self):
        pl.when(self.goes)(self.copy.wait_send)

    def wait_recv(self):
        pl.when(self.comes)(self.copy.wait_recv)


def back(step):
    return tuple(-d for d in step)


def side(step):
    return 0 if step > 0 else 1

def roll(x, by, axis=1):
    by = by % x.shape[axis]
    return x if by == 0 else pltpu.roll(x, by, axis)


def iotas(rows=8, lanes=128):
    row = lax.broadcasted_iota(jnp.int32, (rows, lanes), 0)
    lane = lax.broadcasted_iota(jnp.int32, (rows, lanes), 1)
    return row, lane


def split(x):
    high = x.astype(BF16)
    return high, (x - high.astype(F32)).astype(BF16)


def column_table():
    row, lane = iotas(384, 384)
    g, cx = lane >> 3, lane & 7
    j = (g * 43) >> 8
    wanted = j * 48 + cx * 6 + (g - 6 * j)
    return jnp.where((row == wanted) & (lane < 288), 1.0, 0.0).astype(BF16)


def node_rows(rows):
    row, lane = iotas(rows, 384)
    k, v = row & 7, row >> 3
    return jnp.where((lane == 49 * k + v) & (k < 7) & (v < 49), 1.0, 0.0).astype(BF16)


def to_cells(tiles, table):
    n = tiles[0].shape[0]
    row, lane = iotas(n)
    group = lane >> 3
    chunks = []
    for cy in range(8):
        first, off = 288 * cy // 128, 288 * cy % 128
        parts = []
        for m in range(3):
            one = tiles[(first + m) % 18]
            if off:
                two = tiles[(first + m + 1) % 18]
                one = jnp.where(lane < 128 - off, roll(one, -off), roll(two, -off))
            parts.append(one)
        chunks.append(jnp.concatenate(parts, axis=1))
    stacked = jnp.concatenate(chunks, axis=0)
    high, low = split(stacked)
    both = jnp.dot(jnp.concatenate([high, low], axis=0), table, preferred_element_type=F32)
    moved = both[: 8 * n] + both[8 * n :]
    skewed = [
        [roll(moved[n * cy : n * cy + n, 128 * a : 128 * a + 128], 8 * cy) for a in range(3)]
        for cy in range(8)
    ]
    out = []
    for g in range(36):
        a, b = g // 16, g % 16
        got = jnp.where(group == b, skewed[0][a], 0.0)
        for cy in range(1, 8):
            got = jnp.where(group == (b + cy) % 16, skewed[cy][a], got)
        out.append(roll(got, -8 * b))
    return out


def split_exact(x):
    high, low = split(x)
    return high, low, (x - high.astype(F32) - low.astype(F32)).astype(BF16)


def from_cells(tiles, table):
    row, lane = iotas(8)
    group = lane >> 3
    placed = [roll(tiles[g], 8 * (g % 16)) for g in range(36)]
    rows = []
    for cy in range(8):
        parts = []
        for a in range(3):
            count = 16 if a < 2 else 4
            got = jnp.zeros((8, 128), F32)
            for b in range(count):
                got = jnp.where(group == (b + cy) % 16, placed[16 * a + b], got)
            parts.append(roll(got, -8 * cy))
        rows.append(jnp.concatenate(parts, axis=1))
    stacked = jnp.concatenate(rows, axis=0)
    both = lax.dot_general(
        jnp.concatenate(split_exact(stacked), axis=0), table, (((1,), (1,)), ((), ())), preferred_element_type=F32
    )
    moved = both[:64] + both[64:128] + both[128:]
    out = []
    for c in range(18):
        got = jnp.zeros((8, 128), F32)
        for cy in range(8):
            start = 288 * cy - 128 * c
            lo, hi = max(start, 0), min(start + 288, 128)
            if lo >= hi:
                continue
            off = start % 128
            for m in range(3):
                begin = start + 128 * m
                one_lo, one_hi = max(begin, lo), min(begin + 128, hi)
                if one_lo >= one_hi:
                    continue
                piece = roll(moved[8 * cy : 8 * cy + 8, 128 * m : 128 * m + 128], off)
                got = jnp.where((lane >= one_lo) & (lane < one_hi), piece, got)
        out.append(got)
    return out


def cell_terms(tiles, matrix_high, matrix_low, scale_row):
    high = tiles.astype(BF16).astype(F32)
    low = tiles - high
    _, lane = iotas(512)
    both = jnp.where(lane < 64, high, roll(low, 64)).astype(BF16)
    got = jnp.dot(matrix_high, both, preferred_element_type=F32)
    got = got + jnp.dot(matrix_low, both, preferred_element_type=F32)
    got = got + roll(got, 64)
    return got * scale_row


def local_fold(term):
    row, lane = iotas()
    cx, cy = lane & 7, lane >> 3
    upper_x = []
    for j in range(6):
        got = term(7 * j + 6)
        if j == 0:
            got = got + jnp.where(cy >= 1, roll(term(48), 8), 0.0)
        upper_x.append(got)
    x_tile = jnp.where(lane == 62, roll(term(48), -1), 0.0)
    for j in range(6):
        x_tile = jnp.where((cx == j) & (cy < 8), roll(upper_x[j], j - 7), x_tile)
    y_tile = jnp.zeros((8, 128), F32)
    for i in range(6):
        got = term(42 + i)
        if i == 0:
            got = got + jnp.where(cx >= 1, roll(term(48), 1), 0.0)
        y_tile = jnp.where(cy == i, roll(got, 8 * i - 56), y_tile)
    out = []
    for g in range(36):
        j, i = g // 6, g % 6
        got = term(7 * j + i)
        if j == 0:
            got = got + jnp.where(cy >= 1, roll(term(42 + i), 8), 0.0)
        if i == 0:
            got = got + jnp.where(cx >= 1, roll(upper_x[j], 1), 0.0)
        out.append(got)
    return out, x_tile, y_tile


def column_to_row(tile, at):
    row, lane = iotas()
    return jnp.sum(jnp.where(row == lane, jnp.broadcast_to(tile[:, at : at + 1], (8, 128)), 0.0), axis=0, keepdims=True)


def row_to_column(values):
    row, lane = iotas()
    return jnp.sum(jnp.where(row == lane, jnp.broadcast_to(values, (8, 128)), 0.0), axis=1, keepdims=True)


def wide(values):
    return jnp.broadcast_to(values, (8, 128))


def low_faces(field):
    row, lane = iotas()
    cx, cy = lane & 7, lane >> 3
    x_tile = jnp.zeros((8, 128), F32)
    y_tile = jnp.zeros((8, 128), F32)
    for j in range(6):
        x_tile = jnp.where((cx == j) & (cy < 8), roll(field(6 * j), j), x_tile)
    for i in range(6):
        y_tile = jnp.where(cy == i, roll(field(i), 8 * i), y_tile)
    return x_tile, y_tile


def from_above(field, x_tile, x_row, y_tile, y_row, edge, corner, z_row, high):
    row, lane = iotas()
    hx, hy, hz = high
    line = jnp.where(lane[0:1] == 6, roll(corner * hz, 6), edge)
    x_all = jnp.where(row == 6, wide(x_row * hz), x_tile)
    x_all = hx * jnp.where(lane == 62, wide(row_to_column(line) * hy), x_all)
    y_all = hy * jnp.where(row == 6, wide(y_row * hz), y_tile)
    core = [jnp.where(row == 6, wide(z_row(g) * hz), field(g)) for g in range(36)]
    return core + [x_all, y_all]


def extended(field):
    row, lane = iotas()
    cx, cy = lane & 7, lane >> 3
    x_all, y_all = field(36), field(37)
    out = [None] * 49
    for g in range(36):
        out[7 * (g // 6) + g % 6] = field(g)
    for j in range(6):
        out[7 * j + 6] = jnp.where(cx == 7, roll(x_all, 7 - j), roll(field(6 * j), -1))
    for i in range(6):
        out[42 + i] = jnp.where(cy == 7, roll(y_all, 56 - 8 * i), roll(field(i), -8))
    corner = jnp.where(cx == 7, roll(x_all, -1), roll(field(0), -9))
    corner = jnp.where(cy == 7, roll(y_all, 55), corner)
    out[48] = jnp.where(lane == 63, roll(x_all, 1), corner)
    return out


def shared(part, x_high, y_high):
    row, lane = iotas()
    x_low, y_low = low_faces(part)
    x_low = jnp.where(lane == 62, roll(y_high, 62), x_low)
    y_out = jnp.where(lane == 55, roll(x_high, -7), y_high)
    y_low = jnp.where(lane == 55, roll(x_high, 55), y_low)
    edges = [column_to_row(t, at) for t in (x_high, x_low) for at in (62, 0)]
    return (x_high, x_low), (y_out, y_low), edges


def absorb(part, x_high, y_high, xs, x_rows, ys, y_rows, edges, z_row, low, high):
    row, lane = iotas()
    cx, cy = lane & 7, lane >> 3
    hx, hy, hz = high
    lx, ly, lz = low

    def with_rows(tile, rows):
        return tile + jnp.where(row == 6, wide(rows[0]), jnp.where(row == 0, wide(rows[1] * lz), 0.0))

    x_up, x_down = with_rows(xs[0], x_rows[0]), with_rows(xs[1], x_rows[1]) * lx
    y_up, y_down = with_rows(ys[0], y_rows[0]), with_rows(ys[1], y_rows[1]) * ly
    lines = edges[0] + jnp.where(lane == 6, roll(edges[1], 6), jnp.where(lane == 0, roll(edges[2] * lz, -6), 0.0))
    columns = [wide(row_to_column(lines[c : c + 1])) for c in range(4)]
    up_row, down_row = row == 6, row == 0

    def vertical(up, down):
        return jnp.where(up_row, wide(up), jnp.where(down_row, wide(down * lz), 0.0))

    x_all = x_high + x_up + vertical(z_row(0, 36), z_row(1, 36))
    x_all = x_all + jnp.where(lane == 62, roll(y_up, 7) + columns[0], 0.0)
    x_all = x_all + jnp.where(lane == 0, roll(y_down, -55) + columns[1] * ly, 0.0)
    y_all = y_high + jnp.where(cy < 6, y_up, 0.0) + vertical(z_row(0, 37), z_row(1, 37))
    y_all = y_all + jnp.where(lane == 0, roll(x_down, -62) + columns[2] * lx, 0.0)
    top = jnp.where(up_row, hz, 1.0)
    x_all = x_all * (top * hx) * jnp.where(lane == 62, hy, 1.0)
    y_all = y_all * (top * hy)
    inside = jnp.where(lane < 64, top, 0.0)
    out = []
    for g in range(36):
        j, i = g // 6, g % 6
        got = part(g) + vertical(z_row(0, g), z_row(1, g))
        if i == 0:
            got = got + jnp.where((cx == 0) & (cy < 8), roll(x_down, -j), 0.0)
        if j == 0:
            got = got + jnp.where(cy == 0, roll(y_down, -8 * i), 0.0)
        if g == 0:
            got = got + jnp.where(lane == 0, columns[3] * (lx * ly), 0.0)
        out.append(jnp.where(lane < 64, got * inside, 0.0))
    return out + [x_all, y_all]


def kernel(
    states_ref, previous_ref, potential_ref, screening_ref, occupation_ref, scale_ref, matrix_ref, ids_ref,
    filtered_ref, field_ref,
    pad, raw_matrix, ids, given_scale, occupied, table, padded_matrix, cell_matrix, scales,
    own, screen, vec, grid_ext, terms, part, faces,
    sent_x, sent_y, sent_z, sent_e, got_x, got_y, got_z, got_xr, got_yr, got_e, z_both,
    dens, dens_in, half, half_in, full_in, red_out, red_in, nat, nat_f, factors,
    in_sem, out_sem, halo_send, halo_recv, band_send, band_recv, red_send, red_recv,
):
    dom, band = lax.axis_index("dom"), lax.axis_index("band")
    px, py, pz = lax.rem(dom, 4), lax.rem(lax.div(dom, 4), 4), lax.div(dom, 16)
    z_lo, core = lax.div(band, 2), lax.rem(band, 2)
    z_hi = lax.rem(py, 2)
    across = 2 * (ZLO - 1 - z_lo) + core

    def place(x, y, z):
        return x + 4 * y + 16 * z

    def near(step, mirrored):
        x = lax.rem(px + (step[0] + 4), 4)
        y = lax.rem(py + (step[1] + 4), 4)
        z = lax.rem(pz + (step[2] + 4), 4)
        return (place(x, y, z), across if mirrored and step[1] else band)

    partner = (dom, 2 * z_lo + (1 - core))

    def chip(z):
        return (dom, 2 * z + core)

    y_at = lax.div(dom, 8)
    group_one, group_two = [], []
    for e in range(1, 8):
        x = lax.rem(px + e % 4, 4)
        y = py + 1 - 2 * z_hi if e // 4 else py
        group_one.append((place(x, y, pz), across if e // 4 else band))
    for e in range(1, 8):
        group_two.append((lax.rem(dom, 8) + 8 * lax.rem(y_at + e, 8), band))

    is_end = (z_lo == 0) | (z_lo == ZLO - 1)
    def inside(step):
        tests = []
        for at, d in zip((px, py, pz), step):
            if d:
                tests.append(at < 3 if d > 0 else at > 0)
        found = tests[0]
        for test in tests[1:]:
            found = found & test
        return found

    for got in (got_x, got_y, got_z, got_xr, got_yr, got_e):
        got[...] = jnp.zeros_like(got)
    barrier = pltpu.get_barrier_semaphore()

    def greet(device):
        pl.semaphore_signal(barrier, inc=1, device_id=device, device_id_type=MESH)

    for step in AROUND:
        pl.when(inside(step))(lambda step=step: greet(near(step, False)))
    others = [partner] + [chip(lax.rem(z_lo + e, ZLO)) for e in range(1, ZLO)]
    for device in others:
        greet(device)

    @pl.when(is_end)
    def _():
        for step in AROUND:
            if step[1]:
                pl.when(inside(step))(lambda step=step: greet(near(step, True)))
        for device in group_one + group_two:
            greet(device)

    def along(at):
        return 1 + lax.div(at + 3, 4) + lax.div(6 - at, 4)

    level = along(px) * along(pz)
    at_end = lax.div(z_lo, ZLO - 1) + lax.div(ZLO - 1 - z_lo, ZLO - 1)
    n_greeted = level * along(py) - 1 + len(others) + at_end * (level * (along(py) - 1) + len(group_one) + len(group_two))

    loads = [
        pltpu.make_async_copy(states_ref.at[:, 0, :], pad.at[0, pl.ds(0, 108), :], in_sem.at[0]),
        pltpu.make_async_copy(previous_ref.at[:, 0, :], pad.at[1, pl.ds(0, 108), :], in_sem.at[1]),
        pltpu.make_async_copy(potential_ref, pad.at[2, pl.ds(0, 108), :], in_sem.at[2]),
        pltpu.make_async_copy(screening_ref, pad.at[3, pl.ds(0, 108), :], in_sem.at[3]),
        pltpu.make_async_copy(matrix_ref, raw_matrix, in_sem.at[4]),
        pltpu.make_async_copy(ids_ref.at[:, pl.ds(0, 128)], ids, in_sem.at[5]),
        pltpu.make_async_copy(scale_ref, given_scale, in_sem.at[6]),
        pltpu.make_async_copy(occupation_ref, occupied, in_sem.at[7]),
    ]
    for load in loads:
        load.start()

    def flag(test):
        return jnp.where(test, 1.0, 0.0).astype(F32)

    high = (flag(px < 3), flag(py < 3), flag(pz < 3))
    low = (flag(px > 0), flag(py > 0), flag(pz > 0))
    row, lane = iotas()

    table[...] = column_table()
    for m in range(4):
        pad[m, 108:144, :] = jnp.zeros((36, 128), F32)
    grid_ext[...] = jnp.zeros_like(grid_ext)
    sent_z[...] = jnp.zeros_like(sent_z)
    loads[0].wait()
    first = to_cells([pad[0, pl.ds(c, 8, stride=18), :] for c in range(18)], table[...])
    for g in range(36):
        own[8 * g : 8 * g + 8, :] = first[g]

    def tile_of(source):
        return lambda g: source[8 * g : 8 * g + 8, :]

    def copy_to(at, step, mirrored):
        x, y, z = step
        s, t = side(-x), side(-y)
        if x and y:
            src = sent_e.at[at, pl.ds(2 * side(x) + side(y), 1)]
            dst = got_e.at[at, 0 if z == 0 else 1 + side(-z), pl.ds(2 * s + t, 1)]
        elif x:
            src, dst = sent_x.at[at, side(x)], got_x.at[at, s]
            if z:
                src = src.at[pl.ds(6 if z > 0 else 0, 1)]
                dst = got_xr.at[at, pl.ds(2 * s + side(-z), 1)]
        elif y:
            src, dst = sent_y.at[at, side(y)], got_y.at[at, t]
            if z:
                src = src.at[pl.ds(6 if z > 0 else 0, 1)]
                dst = got_yr.at[at, pl.ds(2 * t + side(-z), 1)]
        else:
            src, dst = sent_z.at[at, side(z)], got_z.at[at, side(-z)]
        e = AROUND.index(step)
        return pltpu.make_async_remote_copy(
            src_ref=src,
            dst_ref=dst,
            send_sem=halo_send.at[at, e],
            recv_sem=halo_recv.at[at, e],
            device_id=near(step, mirrored),
            device_id_type=MESH,
        )

    def start_copies(at, steps, mirrored):
        made = [Guarded(copy_to(at, step, mirrored), inside(step), inside(back(step))) for step in steps]
        for copy in made:
            copy.start()
        return made

    _, lane_18 = iotas(18)

    def put_z(at, s, source, sublane):
        lower = source[pl.ds(sublane, 18, stride=8), :]
        upper = source[pl.ds(144 + sublane, 18, stride=8), :]
        sent_z[at, s, 0:18, :] = jnp.where(lane_18 < 64, lower, roll(upper, 64))

    def take_z(at, s):
        rows = got_z[at, s]
        z_both[s, 0] = rows
        z_both[s, 1] = roll(rows, 64)

    def z_row(s, m):
        if m >= 36:
            return z_both[s, 0, m - 18 : m - 17, :]
        return z_both[s, m // 18, m % 18 : m % 18 + 1, :]

    def products(source):
        tiles = extended(tile_of(source))
        for v in range(49):
            grid_ext[8 * v : 8 * v + 8, :] = tiles[v]
        terms[...] = cell_terms(grid_ext[...], cell_matrix[0], cell_matrix[1], scales[0:1, :])

    def cell_sums(source, factor, extra):
        products(source)
        folded, x_high, y_high = local_fold(lambda v: terms[8 * v : 8 * v + 8, :])
        for g in range(36):
            part[8 * g : 8 * g + 8, :] = factor * folded[g] + extra(g)
        faces[0], faces[1] = factor * x_high, factor * y_high

    def put_level(at, xs, x_high, y_high):
        for s in range(2):
            k = 6 if s == 0 else 0
            sent_x[at, s] = xs[s]
            put_z(at, s, part, k)
            sent_z[at, s, 18:19, :] = x_high[k : k + 1]
            sent_z[at, s, 19:20, :] = y_high[k : k + 1]

    def start_sums(at, source, factor, extra, mirrored):
        cell_sums(source, factor, extra)
        x_high, y_high = faces[0], faces[1]
        xs, ys, edges = shared(tile_of(part), x_high, y_high)
        put_level(at, xs, x_high, y_high)
        for s in range(2):
            sent_y[at, s] = ys[s]
        for c in range(4):
            sent_e[at, c : c + 1, :] = edges[c]
        return start_copies(at, AROUND, mirrored)

    def finish_sums(at, made):
        for copy in made:
            copy.wait_recv()
        take_z(at, 0)
        take_z(at, 1)
        return absorb(
            tile_of(part),
            faces[0],
            faces[1],
            [got_x[at, s] for s in range(2)],
            [[got_xr[at, 2 * s + t : 2 * s + t + 1, :] for t in range(2)] for s in range(2)],
            [got_y[at, s] for s in range(2)],
            [[got_yr[at, 2 * s + t : 2 * s + t + 1, :] for t in range(2)] for s in range(2)],
            [got_e[at, t] for t in range(3)],
            z_row,
            low,
            high,
        )

    x_tile, y_tile = low_faces(tile_of(own))
    sent_x[0, 1] = x_tile
    sent_y[0, 1] = y_tile
    sent_e[0, 3:4, :] = column_to_row(own[0:8, :], 0)
    put_z(0, 1, own, 0)

    pl.semaphore_wait(barrier, n_greeted)
    ghosts = start_copies(0, BELOW, False)

    for load in loads[1:]:
        load.wait()
    three = to_cells(
        [
            jnp.concatenate([pad[m, pl.ds(c, 8, stride=18), :] for m in (1, 2, 3)], axis=0)
            for c in range(18)
        ],
        table[...],
    )
    for g in range(36):
        rows = slice(8 * g, 8 * g + 8)
        screen[rows, :] = three[g][16:24]
        vec[0, rows, :] = FILTER_SCALE * ((three[g][8:16] - FILTER_CENTER) * own[rows, :]) - three[g][0:8]
    padded_matrix[...] = jnp.zeros_like(padded_matrix)
    padded_matrix[0:343, 0:343] = raw_matrix[...]
    by_row, by_column = node_rows(400), node_rows(512)
    for h, piece in enumerate(split(padded_matrix[...])):
        rows_moved = jnp.dot(by_row, piece, preferred_element_type=F32).astype(BF16)
        cell_matrix[h] = lax.dot_general(
            rows_moved, by_column, (((1,), (1,)), ((), ())), preferred_element_type=F32
        ).astype(BF16)
    _, lane_64 = iotas(64)
    first_id = 6 * 49 * ((lane_64 & 63) >> 3) + 6 * (lane_64 & 7)
    matches = jnp.where(first_id == jnp.broadcast_to(ids[:, 0:1], (64, 128)), 1.0, 0.0).astype(F32)
    given = jnp.broadcast_to(given_scale[...], (8, 64))
    scales[...] = jnp.dot(given, matches, precision=lax.Precision.HIGHEST, preferred_element_type=F32)

    for copy in ghosts:
        copy.wait_recv()
    take_z(0, 0)
    compact = from_above(
        tile_of(own),
        got_x[0, 0],
        got_xr[0, 0:1, :],
        got_y[0, 0],
        got_yr[0, 0:1, :],
        got_e[0, 0, 0:1, :],
        got_e[0, 1, 0:1, :],
        lambda g: z_row(0, g),
        high,
    )
    for m in range(TILES):
        vec[1, 8 * m : 8 * m + 8, :] = compact[m]
    summing = start_sums(1, vec.at[1], 0.5 * FILTER_SCALE, tile_of(vec.at[0]), False)
    values = finish_sums(1, summing)
    weight = occupied[...]
    squares = [weight * value * value for value in values]
    for m in range(20):
        tile = squares[m]
        if m + 20 < TILES:
            tile = tile + roll(squares[m + 20], 64)
        dens[8 * m : 8 * m + 8, :] = tile

    mine = pl.multiple_of(80 * core, 8)
    other = pl.multiple_of(80 * (1 - core), 8)

    def band_copy(src, dst, at_send, at_recv, device):
        return pltpu.make_async_remote_copy(
            src_ref=src,
            dst_ref=dst,
            send_sem=band_send.at[at_send],
            recv_sem=band_recv.at[at_recv],
            device_id=device,
            device_id_type=MESH,
        )

    swap = band_copy(dens.at[pl.ds(other, 80), :], dens_in, 0, 0, partner)
    swap.start()
    for m in range(36):
        vec[0, 8 * m : 8 * m + 8, :] = values[m]
    swap.wait_recv()
    half[...] = dens[pl.ds(mine, 80), :] + dens_in[...]

    not_first, not_last = z_lo > 0, z_lo < ZLO - 1
    slot_first = jnp.maximum(z_lo - 1, 0)
    slot_last = jnp.minimum(z_lo, ZLO - 2)
    to_first = band_copy(half, half_in.at[slot_first], 1, 1 + slot_first, chip(0))
    to_last = band_copy(half, half_in.at[slot_last], 2, 1 + slot_last, chip(ZLO - 1))

    @pl.when(not_first)
    def _():
        to_first.start()

    @pl.when(not_last)
    def _():
        to_last.start()

    natural = from_cells([jnp.where(row < 6, vec[0, 8 * g : 8 * g + 8, :], 0.0) for g in range(36)], table[...])
    for c in range(18):
        nat_f[pl.ds(c, 8, stride=18), :] = natural[c]
    store = pltpu.make_async_copy(nat_f.at[pl.ds(0, 108), :], filtered_ref.at[:, 0, :], out_sem)
    store.start()

    B, W, Q, R1, W1 = 0, 1, 2, 3, 4

    @pl.when(is_end)
    def _():
        arrived = [band_copy(half, half_in.at[s], 1, 1 + s, partner) for s in range(ZLO - 1)]
        for copy in arrived:
            copy.wait_recv()
        total = half[...]
        for s in range(ZLO - 1):
            total = total + half_in[s]
        full_in[0] = total * (1.0 / STATES)
        again = band_copy(full_in.at[0], full_in.at[1], 3, 6, partner)
        again.start()
        again.wait_recv()
        both = (
            jnp.where(core == 0, full_in[0], full_in[1]),
            jnp.where(core == 0, full_in[1], full_in[0]),
        )
        for m in range(20):
            tile = both[m // 10][8 * (m % 10) : 8 * (m % 10) + 8]
            vec[B, 8 * m : 8 * m + 8, :] = jnp.where(lane < 64, tile, 0.0)
            if m + 20 < TILES:
                vec[B, 8 * (m + 20) : 8 * (m + 20) + 8, :] = jnp.where(lane < 64, roll(tile, 64), 0.0)

        def put(v, tiles):
            for m in range(TILES):
                vec[v, 8 * m : 8 * m + 8, :] = tiles[m]

        def screened(v):
            return lambda g: screen[8 * g : 8 * g + 8, :] * vec[v, 8 * g : 8 * g + 8, :]

        def onto_row(got):
            got = jnp.sum(got.reshape(36, 8, 128), axis=0)
            return jnp.sum(jnp.where(row < 6, got, 0.0), axis=0, keepdims=True)

        def dot_row(a, b):
            return onto_row(vec[a, 0:CORE_ROWS, :] * vec[b, 0:CORE_ROWS, :])

        def send_reduce(n, level, devices):
            made = [
                pltpu.make_async_remote_copy(
                    src_ref=red_out.at[n, level],
                    dst_ref=red_in.at[n, level, e],
                    send_sem=red_send.at[n, level, e],
                    recv_sem=red_recv.at[n, level, e],
                    device_id=device,
                    device_id_type=MESH,
                )
                for e, device in enumerate(devices)
            ]
            for copy in made:
                copy.start()
            return made

        def start_reduce(n, rows):
            tile = jnp.zeros((8, 128), F32)
            for m, values in enumerate(rows):
                tile = jnp.where(row == m, wide(values), tile)
            red_out[n, 0] = tile
            return send_reduce(n, 0, group_one)

        def take(n, level, made):
            for copy in made:
                copy.wait_recv()
            got = red_out[n, level]
            for e in range(7):
                got = got + red_in[n, level, e]
            return got

        def second_level(n, made):
            red_out[n, 1] = take(n, 0, made)
            return send_reduce(n, 1, group_two)

        def scalars(n, made, count):
            got = jnp.sum(take(n, 1, made), axis=1, keepdims=True)
            return [got[m : m + 1] for m in range(count)]

        def hand_on(n, v):
            natural = from_cells(
                [jnp.where(row < 6, vec[v, 8 * g : 8 * g + 8, :], 0.0) for g in range(36)], table[...]
            )
            for c in range(18):
                nat[n, pl.ds(c, 8, stride=18), :] = natural[c]
            return onward(nat.at[n, 0:112], nat.at[n, 0:112], n)

        def onward(src, dst, n):
            made = [
                band_copy(src, dst, 4 + 2 * n + s, 7 + n, chip(jnp.where(z_lo == 0, 1 + s, ZLO - 2 - s)))
                for s in range(2)
            ]
            for copy in made:
                copy.start()
            return made

        def energy_row(v):
            cells = jnp.sum((grid_ext[0:392, :] * terms[0:392, :]).reshape(49, 8, 128), axis=0)
            cells = jnp.sum(jnp.where(lane < 64, cells, 0.0), axis=0, keepdims=True)
            owned = vec[v, 0:CORE_ROWS, :]
            return cells + onto_row(screen[...] * owned * owned)

        sent = [again]
        made = start_sums(2, vec.at[B], 1.0, screened(B), True)
        red_a = start_reduce(0, [dot_row(B, B), energy_row(B)])
        sent += made + red_a + hand_on(0, B)
        put(W, finish_sums(2, made))
        red_b = second_level(0, red_a)
        made = start_sums(3, vec.at[W], 1.0, screened(W), True)
        sent += made + red_b + hand_on(1, W)
        put(Q, finish_sums(3, made))
        norm_0, image_0 = scalars(0, red_b, 2)
        alpha_0 = norm_0 / image_0

        vec[R1] = vec[B] - alpha_0 * vec[W]
        vec[W1] = vec[W] - alpha_0 * vec[Q]
        products(vec.at[W1])
        red_a = start_reduce(
            1,
            [
                dot_row(R1, R1),
                dot_row(R1, W1),
                dot_row(R1, W),
                dot_row(W1, W1),
                dot_row(W1, W),
                energy_row(W1),
                dot_row(W1, Q),
                dot_row(W, Q),
            ],
        )
        sent += hand_on(2, Q)
        red_b = second_level(1, red_a)
        norm_1, rw, rv, ww, wv, waw, wav, vav = scalars(1, red_b, 8)
        c_b, c_w, c_q = combine(alpha_0, norm_0, image_0, norm_1, rw, rv, ww, wv, waw, wav, vav)
        tile = jnp.where(row == 0, wide(c_b), jnp.where(row == 1, wide(c_w), wide(c_q)))
        factors[0] = tile
        sent += red_a + red_b + onward(factors.at[0], factors.at[1], 3)
        field_ref[...] = c_b * nat[0, 0:108, :] + c_w * nat[1, 0:108, :] + c_q * nat[2, 0:108, :]
        for copy in sent:
            copy.wait_send()

    @pl.when(jnp.logical_not(is_end))
    def _():
        for n in range(3):
            band_copy(nat.at[n, 0:112], nat.at[n, 0:112], 4, 7 + n, partner).wait_recv()
        band_copy(factors.at[0], factors.at[1], 4, 10, partner).wait_recv()
        field_ref[...] = (
            factors[1, 0:1, :] * nat[0, 0:108, :]
            + factors[1, 1:2, :] * nat[1, 0:108, :]
            + factors[1, 2:3, :] * nat[2, 0:108, :]
        )

    swap.wait_send()

    @pl.when(not_first)
    def _():
        to_first.wait_send()

    @pl.when(not_last)
    def _():
        to_last.wait_send()

    for copy in ghosts + summing:
        copy.wait_send()
    store.wait()


def combine(alpha_0, norm_0, image_0, norm_1, rw, rv, ww, wv, waw, wav, vav):
    beta_1 = norm_1 / norm_0
    image_1 = rw + 2.0 * beta_1 * rv + beta_1 * beta_1 * image_0
    alpha_1 = norm_1 / image_1
    r_s = rw + beta_1 * rv
    s_s = ww + 2.0 * beta_1 * wv + beta_1 * beta_1 * (wv_self(alpha_0, wv, vav))
    r_as = ww + beta_1 * wv
    s_as = waw + 2.0 * beta_1 * wav + beta_1 * beta_1 * vav
    norm_2 = jnp.maximum(norm_1 - 2.0 * alpha_1 * r_s + alpha_1 * alpha_1 * s_s, 0.0)
    r2_ar2 = rw - 2.0 * alpha_1 * r_as + alpha_1 * alpha_1 * s_as
    r2_s = r_s - alpha_1 * s_s
    beta_2 = norm_2 / norm_1
    image_2 = r2_ar2 + 2.0 * beta_2 * r2_s + beta_2 * beta_2 * image_1
    alpha_2 = jnp.where(image_2 > 0.0, norm_2 / image_2, 0.0)
    grown = alpha_0 + alpha_1 * (1.0 + beta_1)
    c_b = grown + alpha_2 * (1.0 + beta_2 * (1.0 + beta_1))
    c_w = -alpha_1 * alpha_0 - alpha_2 * (grown + beta_2 * alpha_0)
    c_q = alpha_2 * alpha_1 * alpha_0
    return c_b, c_w, c_q


def wv_self(alpha_0, wv, vav):
    return wv + alpha_0 * vav


def per_device(states, previous, potential, screening, occupation, cell_scale, cell_matrix, connectivity):
    vmem = pl.BlockSpec(memory_space=pltpu.VMEM)
    anywhere = pl.BlockSpec(memory_space=pl.ANY)
    filtered, field = pl.pallas_call(
        kernel,
        out_shape=(jax.ShapeDtypeStruct((108, 1, 128), F32), jax.ShapeDtypeStruct((108, 128), F32)),
        in_specs=[anywhere] * 8,
        out_specs=(anywhere, vmem),
        scratch_shapes=[
            pltpu.VMEM((4, 144, 128), F32),
            pltpu.VMEM((343, 343), F32),
            pltpu.VMEM((64, 128), jnp.int32),
            pltpu.VMEM((1, 64), F32),
            pltpu.VMEM((1, 1), F32),
            pltpu.VMEM((384, 384), BF16),
            pltpu.VMEM((384, 384), F32),
            pltpu.VMEM((2, 400, 512), BF16),
            pltpu.VMEM((8, 128), F32),
            pltpu.VMEM((288, 128), F32),
            pltpu.VMEM((288, 128), F32),
            pltpu.VMEM((5, ROWS, 128), F32),
            pltpu.VMEM((512, 128), F32),
            pltpu.VMEM((400, 128), F32),
            pltpu.VMEM((288, 128), F32),
            pltpu.VMEM((2, 8, 128), F32),
            pltpu.VMEM((4, 2, 8, 128), F32),
            pltpu.VMEM((4, 2, 8, 128), F32),
            pltpu.VMEM((4, 2, 24, 128), F32),
            pltpu.VMEM((4, 8, 128), F32),
            pltpu.VMEM((4, 2, 8, 128), F32),
            pltpu.VMEM((4, 2, 8, 128), F32),
            pltpu.VMEM((4, 2, 24, 128), F32),
            pltpu.VMEM((4, 8, 128), F32),
            pltpu.VMEM((4, 8, 128), F32),
            pltpu.VMEM((4, 3, 8, 128), F32),
            pltpu.VMEM((2, 2, 24, 128), F32),
            pltpu.VMEM((160, 128), F32),
            pltpu.VMEM((80, 128), F32),
            pltpu.VMEM((80, 128), F32),
            pltpu.VMEM((5, 80, 128), F32),
            pltpu.VMEM((2, 80, 128), F32),
            pltpu.VMEM((2, 2, 8, 128), F32),
            pltpu.VMEM((2, 2, 7, 8, 128), F32),
            pltpu.VMEM((3, 144, 128), F32),
            pltpu.VMEM((144, 128), F32),
            pltpu.VMEM((2, 8, 128), F32),
            pltpu.SemaphoreType.DMA((8,)),
            pltpu.SemaphoreType.DMA,
            pltpu.SemaphoreType.DMA((4, 26)),
            pltpu.SemaphoreType.DMA((4, 26)),
            pltpu.SemaphoreType.DMA((12,)),
            pltpu.SemaphoreType.DMA((11,)),
            pltpu.SemaphoreType.DMA((2, 2, 7)),
            pltpu.SemaphoreType.DMA((2, 2, 7)),
        ],
        compiler_params=pltpu.CompilerParams(collective_id=0, has_side_effects=True),
        name="step",
    )(
        states.reshape(108, 1, 128),
        previous.reshape(108, 1, 128),
        potential.reshape(108, 128),
        screening.reshape(108, 128),
        occupation.reshape(1, 1),
        cell_scale.reshape(1, 64),
        cell_matrix,
        connectivity.T,
    )
    return filtered.reshape(1, 13824), field.reshape(13824)


def solution(mesh):
    in_specs = (
        P("band", "dom"),
        P("band", "dom"),
        P("dom"),
        P("dom"),
        P("band"),
        P("dom"),
        P(),
        P(None, "dom"),
    )
    out_specs = (P("band", "dom"), P("dom"))
    return jax.shard_map(per_device, mesh=mesh, in_specs=in_specs, out_specs=out_specs, check_vma=False)
```

```python
import jax
import jax.numpy as jnp
from jax import lax
from jax.experimental import pallas as pl
from jax.experimental.pallas import tpu as pltpu
from jax.sharding import PartitionSpec as P

MESH = pl.DeviceIdType.MESH
F32 = jnp.float32
BF16 = jnp.bfloat16
STATES = 12
ZLO = 6
FILTER_CENTER = 2.0
FILTER_SCALE = 2.0 / 2.0


AROUND = [(x, y, z) for y in (1, -1, 0) for x in (1, -1, 0) for z in (1, -1, 0) if (x, y, z) != (0, 0, 0)]
BELOW = [d for d in AROUND if max(d) <= 0]
TILES = 38
CORE_ROWS = 288
ROWS = 8 * TILES


class Guarded:
    def __init__(self, copy, goes, comes):
        self.copy, self.goes, self.comes = copy, goes, comes

    def start(self):
        pl.when(self.goes)(self.copy.start)

    def wait_send(self):
        pl.when(self.goes)(self.copy.wait_send)

    def wait_recv(self):
        pl.when(self.comes)(self.copy.wait_recv)


def back(step):
    return tuple(-d for d in step)


def side(step):
    return 0 if step > 0 else 1

def roll(x, by, axis=1):
    by = by % x.shape[axis]
    return x if by == 0 else pltpu.roll(x, by, axis)


def iotas(rows=8, lanes=128):
    row = lax.broadcasted_iota(jnp.int32, (rows, lanes), 0)
    lane = lax.broadcasted_iota(jnp.int32, (rows, lanes), 1)
    return row, lane


def split(x):
    high = x.astype(BF16)
    return high, (x - high.astype(F32)).astype(BF16)


def column_table():
    row, lane = iotas(384, 384)
    g, cx = lane >> 3, lane & 7
    j = (g * 43) >> 8
    wanted = j * 48 + cx * 6 + (g - 6 * j)
    return jnp.where((row == wanted) & (lane < 288), 1.0, 0.0).astype(BF16)


def node_rows(rows):
    row, lane = iotas(rows, 384)
    k, v = row & 7, row >> 3
    return jnp.where((lane == 49 * k + v) & (k < 7) & (v < 49), 1.0, 0.0).astype(BF16)


def to_cells(tiles, table):
    n = tiles[0].shape[0]
    row, lane = iotas(n)
    group = lane >> 3
    chunks = []
    for cy in range(8):
        first, off = 288 * cy // 128, 288 * cy % 128
        parts = []
        for m in range(3):
            one = tiles[(first + m) % 18]
            if off:
                two = tiles[(first + m + 1) % 18]
                one = jnp.where(lane < 128 - off, roll(one, -off), roll(two, -off))
            parts.append(one)
        chunks.append(jnp.concatenate(parts, axis=1))
    stacked = jnp.concatenate(chunks, axis=0)
    high, low = split(stacked)
    both = jnp.dot(jnp.concatenate([high, low], axis=0), table, preferred_element_type=F32)
    moved = both[: 8 * n] + both[8 * n :]
    skewed = [
        [roll(moved[n * cy : n * cy + n, 128 * a : 128 * a + 128], 8 * cy) for a in range(3)]
        for cy in range(8)
    ]
    out = []
    for g in range(36):
        a, b = g // 16, g % 16
        got = jnp.where(group == b, skewed[0][a], 0.0)
        for cy in range(1, 8):
            got = jnp.where(group == (b + cy) % 16, skewed[cy][a], got)
        out.append(roll(got, -8 * b))
    return out


def split_exact(x):
    high, low = split(x)
    return high, low, (x - high.astype(F32) - low.astype(F32)).astype(BF16)


def from_cells(tiles, table):
    row, lane = iotas(8)
    group = lane >> 3
    placed = [roll(tiles[g], 8 * (g % 16)) for g in range(36)]
    rows = []
    for cy in range(8):
        parts = []
        for a in range(3):
            count = 16 if a < 2 else 4
            got = jnp.zeros((8, 128), F32)
            for b in range(count):
                got = jnp.where(group == (b + cy) % 16, placed[16 * a + b], got)
            parts.append(roll(got, -8 * cy))
        rows.append(jnp.concatenate(parts, axis=1))
    stacked = jnp.concatenate(rows, axis=0)
    both = lax.dot_general(
        jnp.concatenate(split_exact(stacked), axis=0), table, (((1,), (1,)), ((), ())), preferred_element_type=F32
    )
    moved = both[:64] + both[64:128] + both[128:]
    out = []
    for c in range(18):
        got = jnp.zeros((8, 128), F32)
        for cy in range(8):
            start = 288 * cy - 128 * c
            lo, hi = max(start, 0), min(start + 288, 128)
            if lo >= hi:
                continue
            off = start % 128
            for m in range(3):
                begin = start + 128 * m
                one_lo, one_hi = max(begin, lo), min(begin + 128, hi)
                if one_lo >= one_hi:
                    continue
                piece = roll(moved[8 * cy : 8 * cy + 8, 128 * m : 128 * m + 128], off)
                got = jnp.where((lane >= one_lo) & (lane < one_hi), piece, got)
        out.append(got)
    return out


def cell_terms(tiles, matrix_high, matrix_low, scale_row):
    high = tiles.astype(BF16).astype(F32)
    low = tiles - high
    _, lane = iotas(512)
    both = jnp.where(lane < 64, high, roll(low, 64)).astype(BF16)
    got = jnp.dot(matrix_high, both, preferred_element_type=F32)
    got = got + jnp.dot(matrix_low, both, preferred_element_type=F32)
    got = got + roll(got, 64)
    return got * scale_row


def local_fold(term):
    row, lane = iotas()
    cx, cy = lane & 7, lane >> 3
    upper_x = []
    for j in range(6):
        got = term(7 * j + 6)
        if j == 0:
            got = got + jnp.where(cy >= 1, roll(term(48), 8), 0.0)
        upper_x.append(got)
    x_tile = jnp.where(lane == 62, roll(term(48), -1), 0.0)
    for j in range(6):
        x_tile = jnp.where((cx == j) & (cy < 8), roll(upper_x[j], j - 7), x_tile)
    y_tile = jnp.zeros((8, 128), F32)
    for i in range(6):
        got = term(42 + i)
        if i == 0:
            got = got + jnp.where(cx >= 1, roll(term(48), 1), 0.0)
        y_tile = jnp.where(cy == i, roll(got, 8 * i - 56), y_tile)
    out = []
    for g in range(36):
        j, i = g // 6, g % 6
        got = term(7 * j + i)
        if j == 0:
            got = got + jnp.where(cy >= 1, roll(term(42 + i), 8), 0.0)
        if i == 0:
            got = got + jnp.where(cx >= 1, roll(upper_x[j], 1), 0.0)
        out.append(got)
    return out, x_tile, y_tile


def column_to_row(tile, at):
    row, lane = iotas()
    return jnp.sum(jnp.where(row == lane, jnp.broadcast_to(tile[:, at : at + 1], (8, 128)), 0.0), axis=0, keepdims=True)


def row_to_column(values):
    row, lane = iotas()
    return jnp.sum(jnp.where(row == lane, jnp.broadcast_to(values, (8, 128)), 0.0), axis=1, keepdims=True)


def wide(values):
    return jnp.broadcast_to(values, (8, 128))


def low_faces(field):
    row, lane = iotas()
    cx, cy = lane & 7, lane >> 3
    x_tile = jnp.zeros((8, 128), F32)
    y_tile = jnp.zeros((8, 128), F32)
    for j in range(6):
        x_tile = jnp.where((cx == j) & (cy < 8), roll(field(6 * j), j), x_tile)
    for i in range(6):
        y_tile = jnp.where(cy == i, roll(field(i), 8 * i), y_tile)
    return x_tile, y_tile


def from_above(field, x_tile, x_row, y_tile, y_row, edge, corner, z_row, high):
    row, lane = iotas()
    hx, hy, hz = high
    line = jnp.where(lane[0:1] == 6, roll(corner * hz, 6), edge)
    x_all = jnp.where(row == 6, wide(x_row * hz), x_tile)
    x_all = hx * jnp.where(lane == 62, wide(row_to_column(line) * hy), x_all)
    y_all = hy * jnp.where(row == 6, wide(y_row * hz), y_tile)
    core = [jnp.where(row == 6, wide(z_row(g) * hz), field(g)) for g in range(36)]
    return core + [x_all, y_all]


def extended(field):
    row, lane = iotas()
    cx, cy = lane & 7, lane >> 3
    x_all, y_all = field(36), field(37)
    out = [None] * 49
    for g in range(36):
        out[7 * (g // 6) + g % 6] = field(g)
    for j in range(6):
        out[7 * j + 6] = jnp.where(cx == 7, roll(x_all, 7 - j), roll(field(6 * j), -1))
    for i in range(6):
        out[42 + i] = jnp.where(cy == 7, roll(y_all, 56 - 8 * i), roll(field(i), -8))
    corner = jnp.where(cx == 7, roll(x_all, -1), roll(field(0), -9))
    corner = jnp.where(cy == 7, roll(y_all, 55), corner)
    out[48] = jnp.where(lane == 63, roll(x_all, 1), corner)
    return out


def shared(part, x_high, y_high):
    row, lane = iotas()
    x_low, y_low = low_faces(part)
    x_low = jnp.where(lane == 62, roll(y_high, 62), x_low)
    y_out = jnp.where(lane == 55, roll(x_high, -7), y_high)
    y_low = jnp.where(lane == 55, roll(x_high, 55), y_low)
    edges = [column_to_row(t, at) for t in (x_high, x_low) for at in (62, 0)]
    return (x_high, x_low), (y_out, y_low), edges


def absorb(part, x_high, y_high, xs, x_rows, ys, y_rows, edges, z_row, low, high):
    row, lane = iotas()
    cx, cy = lane & 7, lane >> 3
    hx, hy, hz = high
    lx, ly, lz = low

    def with_rows(tile, rows):
        return tile + jnp.where(row == 6, wide(rows[0]), jnp.where(row == 0, wide(rows[1] * lz), 0.0))

    x_up, x_down = with_rows(xs[0], x_rows[0]), with_rows(xs[1], x_rows[1]) * lx
    y_up, y_down = with_rows(ys[0], y_rows[0]), with_rows(ys[1], y_rows[1]) * ly
    lines = edges[0] + jnp.where(lane == 6, roll(edges[1], 6), jnp.where(lane == 0, roll(edges[2] * lz, -6), 0.0))
    columns = [wide(row_to_column(lines[c : c + 1])) for c in range(4)]
    up_row, down_row = row == 6, row == 0

    def vertical(up, down):
        return jnp.where(up_row, wide(up), jnp.where(down_row, wide(down * lz), 0.0))

    x_all = x_high + x_up + vertical(z_row(0, 36), z_row(1, 36))
    x_all = x_all + jnp.where(lane == 62, roll(y_up, 7) + columns[0], 0.0)
    x_all = x_all + jnp.where(lane == 0, roll(y_down, -55) + columns[1] * ly, 0.0)
    y_all = y_high + jnp.where(cy < 6, y_up, 0.0) + vertical(z_row(0, 37), z_row(1, 37))
    y_all = y_all + jnp.where(lane == 0, roll(x_down, -62) + columns[2] * lx, 0.0)
    top = jnp.where(up_row, hz, 1.0)
    x_all = x_all * (top * hx) * jnp.where(lane == 62, hy, 1.0)
    y_all = y_all * (top * hy)
    inside = jnp.where(lane < 64, top, 0.0)
    out = []
    for g in range(36):
        j, i = g // 6, g % 6
        got = part(g) + vertical(z_row(0, g), z_row(1, g))
        if i == 0:
            got = got + jnp.where((cx == 0) & (cy < 8), roll(x_down, -j), 0.0)
        if j == 0:
            got = got + jnp.where(cy == 0, roll(y_down, -8 * i), 0.0)
        if g == 0:
            got = got + jnp.where(lane == 0, columns[3] * (lx * ly), 0.0)
        out.append(jnp.where(lane < 64, got * inside, 0.0))
    return out + [x_all, y_all]


def kernel(
    states_ref, previous_ref, potential_ref, screening_ref, occupation_ref, scale_ref, matrix_ref, ids_ref,
    filtered_ref, field_ref,
    pad, raw_matrix, ids, given_scale, occupied, table, padded_matrix, cell_matrix, scales,
    own, screen, vec, grid_ext, terms, part, faces,
    sent_x, sent_y, sent_z, sent_e, got_x, got_y, got_z, got_xr, got_yr, got_e, z_both,
    dens, dens_in, half, half_in, full_in, red_out, red_in, last_out, last_in, nat, nat_f, factors,
    in_sem, out_sem, halo_send, halo_recv, band_send, band_recv, red_send, red_recv, last_send, last_recv,
):
    dom, band = lax.axis_index("dom"), lax.axis_index("band")
    px, py, pz = lax.rem(dom, 4), lax.rem(lax.div(dom, 4), 4), lax.div(dom, 16)
    z_lo, core = lax.div(band, 2), lax.rem(band, 2)
    z_hi = lax.rem(py, 2)
    across = 2 * (ZLO - 1 - z_lo) + core

    def place(x, y, z):
        return x + 4 * y + 16 * z

    def near(step, mirrored):
        x = lax.rem(px + (step[0] + 4), 4)
        y = lax.rem(py + (step[1] + 4), 4)
        z = lax.rem(pz + (step[2] + 4), 4)
        return (place(x, y, z), across if mirrored and step[1] else band)

    partner = (dom, 2 * z_lo + (1 - core))

    def chip(z):
        return (dom, 2 * z + core)

    y_at = lax.div(dom, 8)
    group_one, group_two = [], []
    for e in range(1, 8):
        x = lax.rem(px + e % 4, 4)
        y = py + 1 - 2 * z_hi if e // 4 else py
        group_one.append((place(x, y, pz), across if e // 4 else band))
    for e in range(1, 8):
        group_two.append((lax.rem(dom, 8) + 8 * lax.rem(y_at + e, 8), band))

    served = [
        [(device, 2 * jnp.where(z_lo == 0, 1 + s, ZLO - 2 - s) + core) for device in [dom] + [d for d, _ in group_two]]
        for s in range(2)
    ]
    serving = 2 * jnp.where(z_lo < ZLO // 2, 0, ZLO - 1) + core

    is_end = (z_lo == 0) | (z_lo == ZLO - 1)
    def inside(step):
        tests = []
        for at, d in zip((px, py, pz), step):
            if d:
                tests.append(at < 3 if d > 0 else at > 0)
        found = tests[0]
        for test in tests[1:]:
            found = found & test
        return found

    for got in (got_x, got_y, got_z, got_xr, got_yr, got_e):
        got[...] = jnp.zeros_like(got)
    barrier = pltpu.get_barrier_semaphore()

    def greet(device):
        pl.semaphore_signal(barrier, inc=1, device_id=device, device_id_type=MESH)

    for step in AROUND:
        pl.when(inside(step))(lambda step=step: greet(near(step, False)))
    others = [partner] + [chip(lax.rem(z_lo + e, ZLO)) for e in range(1, ZLO)]
    for device in others:
        greet(device)

    @pl.when(is_end)
    def _():
        for step in AROUND:
            if step[1]:
                pl.when(inside(step))(lambda step=step: greet(near(step, True)))
        for device in group_one + group_two + served[0][1:] + served[1][1:]:
            greet(device)

    @pl.when(jnp.logical_not(is_end))
    def _():
        for device, _ in group_two:
            greet((device, serving))

    def along(at):
        return 1 + lax.div(at + 3, 4) + lax.div(6 - at, 4)

    level = along(px) * along(pz)
    at_end = lax.div(z_lo, ZLO - 1) + lax.div(ZLO - 1 - z_lo, ZLO - 1)
    n_greeted = level * along(py) - 1 + len(others) + len(group_two)
    n_greeted = n_greeted + at_end * (level * (along(py) - 1) + len(group_one) + 2 * len(group_two))

    loads = [
        pltpu.make_async_copy(states_ref.at[:, 0, :], pad.at[0, pl.ds(0, 108), :], in_sem.at[0]),
        pltpu.make_async_copy(previous_ref.at[:, 0, :], pad.at[1, pl.ds(0, 108), :], in_sem.at[1]),
        pltpu.make_async_copy(potential_ref, pad.at[2, pl.ds(0, 108), :], in_sem.at[2]),
        pltpu.make_async_copy(screening_ref, pad.at[3, pl.ds(0, 108), :], in_sem.at[3]),
        pltpu.make_async_copy(matrix_ref, raw_matrix, in_sem.at[4]),
        pltpu.make_async_copy(ids_ref.at[:, pl.ds(0, 128)], ids, in_sem.at[5]),
        pltpu.make_async_copy(scale_ref, given_scale, in_sem.at[6]),
        pltpu.make_async_copy(occupation_ref, occupied, in_sem.at[7]),
    ]
    for load in loads:
        load.start()

    def flag(test):
        return jnp.where(test, 1.0, 0.0).astype(F32)

    high = (flag(px < 3), flag(py < 3), flag(pz < 3))
    low = (flag(px > 0), flag(py > 0), flag(pz > 0))
    row, lane = iotas()

    table[...] = column_table()
    for m in range(4):
        pad[m, 108:144, :] = jnp.zeros((36, 128), F32)
    grid_ext[...] = jnp.zeros_like(grid_ext)
    sent_z[...] = jnp.zeros_like(sent_z)
    loads[0].wait()
    first = to_cells([pad[0, pl.ds(c, 8, stride=18), :] for c in range(18)], table[...])
    for g in range(36):
        own[8 * g : 8 * g + 8, :] = first[g]

    def tile_of(source):
        return lambda g: source[8 * g : 8 * g + 8, :]

    def copy_to(at, step, mirrored):
        x, y, z = step
        s, t = side(-x), side(-y)
        if x and y:
            src = sent_e.at[at, pl.ds(2 * side(x) + side(y), 1)]
            dst = got_e.at[at, 0 if z == 0 else 1 + side(-z), pl.ds(2 * s + t, 1)]
        elif x:
            src, dst = sent_x.at[at, side(x)], got_x.at[at, s]
            if z:
                src = src.at[pl.ds(6 if z > 0 else 0, 1)]
                dst = got_xr.at[at, pl.ds(2 * s + side(-z), 1)]
        elif y:
            src, dst = sent_y.at[at, side(y)], got_y.at[at, t]
            if z:
                src = src.at[pl.ds(6 if z > 0 else 0, 1)]
                dst = got_yr.at[at, pl.ds(2 * t + side(-z), 1)]
        else:
            src, dst = sent_z.at[at, side(z)], got_z.at[at, side(-z)]
        e = AROUND.index(step)
        return pltpu.make_async_remote_copy(
            src_ref=src,
            dst_ref=dst,
            send_sem=halo_send.at[at, e],
            recv_sem=halo_recv.at[at, e],
            device_id=near(step, mirrored),
            device_id_type=MESH,
        )

    def start_copies(at, steps, mirrored):
        made = [Guarded(copy_to(at, step, mirrored), inside(step), inside(back(step))) for step in steps]
        for copy in made:
            copy.start()
        return made

    _, lane_18 = iotas(18)

    def put_z(at, s, source, sublane):
        lower = source[pl.ds(sublane, 18, stride=8), :]
        upper = source[pl.ds(144 + sublane, 18, stride=8), :]
        sent_z[at, s, 0:18, :] = jnp.where(lane_18 < 64, lower, roll(upper, 64))

    def take_z(at, s):
        rows = got_z[at, s]
        z_both[s, 0] = rows
        z_both[s, 1] = roll(rows, 64)

    def z_row(s, m):
        if m >= 36:
            return z_both[s, 0, m - 18 : m - 17, :]
        return z_both[s, m // 18, m % 18 : m % 18 + 1, :]

    def products(source):
        tiles = extended(tile_of(source))
        for v in range(49):
            grid_ext[8 * v : 8 * v + 8, :] = tiles[v]
        terms[...] = cell_terms(grid_ext[...], cell_matrix[0], cell_matrix[1], scales[0:1, :])

    def cell_sums(source, factor, extra):
        products(source)
        folded, x_high, y_high = local_fold(lambda v: terms[8 * v : 8 * v + 8, :])
        for g in range(36):
            part[8 * g : 8 * g + 8, :] = factor * folded[g] + extra(g)
        faces[0], faces[1] = factor * x_high, factor * y_high

    def put_level(at, xs, x_high, y_high):
        for s in range(2):
            k = 6 if s == 0 else 0
            sent_x[at, s] = xs[s]
            put_z(at, s, part, k)
            sent_z[at, s, 18:19, :] = x_high[k : k + 1]
            sent_z[at, s, 19:20, :] = y_high[k : k + 1]

    def start_sums(at, source, factor, extra, mirrored):
        cell_sums(source, factor, extra)
        x_high, y_high = faces[0], faces[1]
        xs, ys, edges = shared(tile_of(part), x_high, y_high)
        put_level(at, xs, x_high, y_high)
        for s in range(2):
            sent_y[at, s] = ys[s]
        for c in range(4):
            sent_e[at, c : c + 1, :] = edges[c]
        return start_copies(at, AROUND, mirrored)

    def finish_sums(at, made):
        for copy in made:
            copy.wait_recv()
        take_z(at, 0)
        take_z(at, 1)
        return absorb(
            tile_of(part),
            faces[0],
            faces[1],
            [got_x[at, s] for s in range(2)],
            [[got_xr[at, 2 * s + t : 2 * s + t + 1, :] for t in range(2)] for s in range(2)],
            [got_y[at, s] for s in range(2)],
            [[got_yr[at, 2 * s + t : 2 * s + t + 1, :] for t in range(2)] for s in range(2)],
            [got_e[at, t] for t in range(3)],
            z_row,
            low,
            high,
        )

    x_tile, y_tile = low_faces(tile_of(own))
    sent_x[0, 1] = x_tile
    sent_y[0, 1] = y_tile
    sent_e[0, 3:4, :] = column_to_row(own[0:8, :], 0)
    put_z(0, 1, own, 0)

    pl.semaphore_wait(barrier, n_greeted)
    ghosts = start_copies(0, BELOW, False)

    for load in loads[1:]:
        load.wait()
    three = to_cells(
        [
            jnp.concatenate([pad[m, pl.ds(c, 8, stride=18), :] for m in (1, 2, 3)], axis=0)
            for c in range(18)
        ],
        table[...],
    )
    for g in range(36):
        rows = slice(8 * g, 8 * g + 8)
        screen[rows, :] = three[g][16:24]
        vec[0, rows, :] = FILTER_SCALE * ((three[g][8:16] - FILTER_CENTER) * own[rows, :]) - three[g][0:8]
    padded_matrix[...] = jnp.zeros_like(padded_matrix)
    padded_matrix[0:343, 0:343] = raw_matrix[...]
    by_row, by_column = node_rows(400), node_rows(512)
    for h, piece in enumerate(split(padded_matrix[...])):
        rows_moved = jnp.dot(by_row, piece, preferred_element_type=F32).astype(BF16)
        cell_matrix[h] = lax.dot_general(
            rows_moved, by_column, (((1,), (1,)), ((), ())), preferred_element_type=F32
        ).astype(BF16)
    _, lane_64 = iotas(64)
    first_id = 6 * 49 * ((lane_64 & 63) >> 3) + 6 * (lane_64 & 7)
    matches = jnp.where(first_id == jnp.broadcast_to(ids[:, 0:1], (64, 128)), 1.0, 0.0).astype(F32)
    given = jnp.broadcast_to(given_scale[...], (8, 64))
    scales[...] = jnp.dot(given, matches, precision=lax.Precision.HIGHEST, preferred_element_type=F32)

    for copy in ghosts:
        copy.wait_recv()
    take_z(0, 0)
    compact = from_above(
        tile_of(own),
        got_x[0, 0],
        got_xr[0, 0:1, :],
        got_y[0, 0],
        got_yr[0, 0:1, :],
        got_e[0, 0, 0:1, :],
        got_e[0, 1, 0:1, :],
        lambda g: z_row(0, g),
        high,
    )
    for m in range(TILES):
        vec[1, 8 * m : 8 * m + 8, :] = compact[m]
    summing = start_sums(1, vec.at[1], 0.5 * FILTER_SCALE, tile_of(vec.at[0]), False)
    values = finish_sums(1, summing)
    weight = occupied[...]
    squares = [weight * value * value for value in values]
    for m in range(20):
        tile = squares[m]
        if m + 20 < TILES:
            tile = tile + roll(squares[m + 20], 64)
        dens[8 * m : 8 * m + 8, :] = tile

    mine = pl.multiple_of(80 * core, 8)
    other = pl.multiple_of(80 * (1 - core), 8)

    def band_copy(src, dst, at_send, at_recv, device):
        return pltpu.make_async_remote_copy(
            src_ref=src,
            dst_ref=dst,
            send_sem=band_send.at[at_send],
            recv_sem=band_recv.at[at_recv],
            device_id=device,
            device_id_type=MESH,
        )

    swap = band_copy(dens.at[pl.ds(other, 80), :], dens_in, 0, 0, partner)
    swap.start()
    for m in range(36):
        vec[0, 8 * m : 8 * m + 8, :] = values[m]
    swap.wait_recv()
    half[...] = dens[pl.ds(mine, 80), :] + dens_in[...]

    not_first, not_last = z_lo > 0, z_lo < ZLO - 1
    slot_first = jnp.maximum(z_lo - 1, 0)
    slot_last = jnp.minimum(z_lo, ZLO - 2)
    to_first = band_copy(half, half_in.at[slot_first], 1, 1 + slot_first, chip(0))
    to_last = band_copy(half, half_in.at[slot_last], 2, 1 + slot_last, chip(ZLO - 1))

    @pl.when(not_first)
    def _():
        to_first.start()

    @pl.when(not_last)
    def _():
        to_last.start()

    natural = from_cells([jnp.where(row < 6, vec[0, 8 * g : 8 * g + 8, :], 0.0) for g in range(36)], table[...])
    for c in range(18):
        nat_f[pl.ds(c, 8, stride=18), :] = natural[c]
    store = pltpu.make_async_copy(nat_f.at[pl.ds(0, 108), :], filtered_ref.at[:, 0, :], out_sem)
    store.start()

    B, W, Q, R1, W1 = 0, 1, 2, 3, 4

    def last_copy(at_send, e, device):
        return pltpu.make_async_remote_copy(
            src_ref=last_out,
            dst_ref=last_in.at[e],
            send_sem=last_send.at[at_send],
            recv_sem=last_recv.at[e],
            device_id=device,
            device_id_type=MESH,
        )

    def write_field(got, known):
        for e in range(1, 8):
            got = got + last_in[e]
        got = jnp.sum(got, axis=1, keepdims=True)
        c_b, c_w, c_q = combine(*[known[m : m + 1, 0:1] for m in range(3)], *[got[m : m + 1] for m in range(8)])
        field_ref[...] = c_b * nat[0, 0:108, :] + c_w * nat[1, 0:108, :] + c_q * nat[2, 0:108, :]

    @pl.when(is_end)
    def _():
        arrived = [band_copy(half, half_in.at[s], 1, 1 + s, partner) for s in range(ZLO - 1)]
        for copy in arrived:
            copy.wait_recv()
        total = half[...]
        for s in range(ZLO - 1):
            total = total + half_in[s]
        full_in[0] = total * (1.0 / STATES)
        again = band_copy(full_in.at[0], full_in.at[1], 3, 6, partner)
        again.start()
        again.wait_recv()
        both = (
            jnp.where(core == 0, full_in[0], full_in[1]),
            jnp.where(core == 0, full_in[1], full_in[0]),
        )
        for m in range(20):
            tile = both[m // 10][8 * (m % 10) : 8 * (m % 10) + 8]
            vec[B, 8 * m : 8 * m + 8, :] = jnp.where(lane < 64, tile, 0.0)
            if m + 20 < TILES:
                vec[B, 8 * (m + 20) : 8 * (m + 20) + 8, :] = jnp.where(lane < 64, roll(tile, 64), 0.0)

        def put(v, tiles):
            for m in range(TILES):
                vec[v, 8 * m : 8 * m + 8, :] = tiles[m]

        def screened(v):
            return lambda g: screen[8 * g : 8 * g + 8, :] * vec[v, 8 * g : 8 * g + 8, :]

        def onto_row(got):
            got = jnp.sum(got.reshape(36, 8, 128), axis=0)
            return jnp.sum(jnp.where(row < 6, got, 0.0), axis=0, keepdims=True)

        def dot_row(a, b):
            return onto_row(vec[a, 0:CORE_ROWS, :] * vec[b, 0:CORE_ROWS, :])

        def send_reduce(n, level, devices):
            made = [
                pltpu.make_async_remote_copy(
                    src_ref=red_out.at[n, level],
                    dst_ref=red_in.at[n, level, e],
                    send_sem=red_send.at[n, level, e],
                    recv_sem=red_recv.at[n, level, e],
                    device_id=device,
                    device_id_type=MESH,
                )
                for e, device in enumerate(devices)
            ]
            for copy in made:
                copy.start()
            return made

        def start_reduce(n, rows):
            tile = jnp.zeros((8, 128), F32)
            for m, values in enumerate(rows):
                tile = jnp.where(row == m, wide(values), tile)
            red_out[n, 0] = tile
            return send_reduce(n, 0, group_one)

        def take(n, level, made):
            for copy in made:
                copy.wait_recv()
            got = red_out[n, level]
            for e in range(7):
                got = got + red_in[n, level, e]
            return got

        def second_level(n, made):
            red_out[n, 1] = take(n, 0, made)
            return send_reduce(n, 1, group_two)

        def scalars(n, made, count):
            got = jnp.sum(take(n, 1, made), axis=1, keepdims=True)
            return [got[m : m + 1] for m in range(count)]

        def hand_on(n, v):
            natural = from_cells(
                [jnp.where(row < 6, vec[v, 8 * g : 8 * g + 8, :], 0.0) for g in range(36)], table[...]
            )
            for c in range(18):
                nat[n, pl.ds(c, 8, stride=18), :] = natural[c]
            return onward(nat.at[n, 0:112], nat.at[n, 0:112], n)

        def onward(src, dst, n):
            made = [
                band_copy(src, dst, 4 + 2 * n + s, 7 + n, chip(jnp.where(z_lo == 0, 1 + s, ZLO - 2 - s)))
                for s in range(2)
            ]
            for copy in made:
                copy.start()
            return made

        def energy_row(v):
            cells = jnp.sum((grid_ext[0:392, :] * terms[0:392, :]).reshape(49, 8, 128), axis=0)
            cells = jnp.sum(jnp.where(lane < 64, cells, 0.0), axis=0, keepdims=True)
            owned = vec[v, 0:CORE_ROWS, :]
            return cells + onto_row(screen[...] * owned * owned)

        sent = [again]
        made = start_sums(2, vec.at[B], 1.0, screened(B), True)
        red_a = start_reduce(0, [dot_row(B, B), energy_row(B)])
        sent += made + red_a + hand_on(0, B)
        put(W, finish_sums(2, made))
        red_b = second_level(0, red_a)
        made = start_sums(3, vec.at[W], 1.0, screened(W), True)
        sent += made + red_b + hand_on(1, W)
        put(Q, finish_sums(3, made))
        norm_0, image_0 = scalars(0, red_b, 2)
        alpha_0 = norm_0 / image_0
        factors[0] = jnp.where(row == 0, wide(alpha_0), jnp.where(row == 1, wide(norm_0), wide(image_0)))
        sent += onward(factors.at[0], factors.at[1], 3)

        vec[R1] = vec[B] - alpha_0 * vec[W]
        vec[W1] = vec[W] - alpha_0 * vec[Q]
        products(vec.at[W1])
        red_a = start_reduce(
            1,
            [
                dot_row(R1, R1),
                dot_row(R1, W1),
                dot_row(R1, W),
                dot_row(W1, W1),
                dot_row(W1, W),
                energy_row(W1),
                dot_row(W1, Q),
                dot_row(W, Q),
            ],
        )
        sent += hand_on(2, Q)
        last_out[...] = take(1, 0, red_a)
        last = [last_copy(e, e, device) for e, device in enumerate(group_two, 1)]
        for m in range(2):
            last += [last_copy(8 * (m + 1) + e, e, device) for e, device in enumerate(served[m])]
        for copy in last:
            copy.start()
        sent += red_a + last
        for copy in last[:7]:
            copy.wait_recv()
        write_field(last_out[...], factors[0])
        for copy in sent:
            copy.wait_send()

    @pl.when(jnp.logical_not(is_end))
    def _():
        for n in range(3):
            band_copy(nat.at[n, 0:112], nat.at[n, 0:112], 4, 7 + n, partner).wait_recv()
        band_copy(factors.at[0], factors.at[1], 4, 10, partner).wait_recv()
        for e in range(8):
            last_copy(e, e, partner).wait_recv()
        write_field(last_in[0], factors[1])

    swap.wait_send()

    @pl.when(not_first)
    def _():
        to_first.wait_send()

    @pl.when(not_last)
    def _():
        to_last.wait_send()

    for copy in ghosts + summing:
        copy.wait_send()
    store.wait()


def combine(alpha_0, norm_0, image_0, norm_1, rw, rv, ww, wv, waw, wav, vav):
    beta_1 = norm_1 / norm_0
    image_1 = rw + 2.0 * beta_1 * rv + beta_1 * beta_1 * image_0
    alpha_1 = norm_1 / image_1
    r_s = rw + beta_1 * rv
    s_s = ww + 2.0 * beta_1 * wv + beta_1 * beta_1 * (wv_self(alpha_0, wv, vav))
    r_as = ww + beta_1 * wv
    s_as = waw + 2.0 * beta_1 * wav + beta_1 * beta_1 * vav
    norm_2 = jnp.maximum(norm_1 - 2.0 * alpha_1 * r_s + alpha_1 * alpha_1 * s_s, 0.0)
    r2_ar2 = rw - 2.0 * alpha_1 * r_as + alpha_1 * alpha_1 * s_as
    r2_s = r_s - alpha_1 * s_s
    beta_2 = norm_2 / norm_1
    image_2 = r2_ar2 + 2.0 * beta_2 * r2_s + beta_2 * beta_2 * image_1
    alpha_2 = jnp.where(image_2 > 0.0, norm_2 / image_2, 0.0)
    grown = alpha_0 + alpha_1 * (1.0 + beta_1)
    c_b = grown + alpha_2 * (1.0 + beta_2 * (1.0 + beta_1))
    c_w = -alpha_1 * alpha_0 - alpha_2 * (grown + beta_2 * alpha_0)
    c_q = alpha_2 * alpha_1 * alpha_0
    return c_b, c_w, c_q


def wv_self(alpha_0, wv, vav):
    return wv + alpha_0 * vav


def per_device(states, previous, potential, screening, occupation, cell_scale, cell_matrix, connectivity):
    vmem = pl.BlockSpec(memory_space=pltpu.VMEM)
    anywhere = pl.BlockSpec(memory_space=pl.ANY)
    filtered, field = pl.pallas_call(
        kernel,
        out_shape=(jax.ShapeDtypeStruct((108, 1, 128), F32), jax.ShapeDtypeStruct((108, 128), F32)),
        in_specs=[anywhere] * 8,
        out_specs=(anywhere, vmem),
        scratch_shapes=[
            pltpu.VMEM((4, 144, 128), F32),
            pltpu.VMEM((343, 343), F32),
            pltpu.VMEM((64, 128), jnp.int32),
            pltpu.VMEM((1, 64), F32),
            pltpu.VMEM((1, 1), F32),
            pltpu.VMEM((384, 384), BF16),
            pltpu.VMEM((384, 384), F32),
            pltpu.VMEM((2, 400, 512), BF16),
            pltpu.VMEM((8, 128), F32),
            pltpu.VMEM((288, 128), F32),
            pltpu.VMEM((288, 128), F32),
            pltpu.VMEM((5, ROWS, 128), F32),
            pltpu.VMEM((512, 128), F32),
            pltpu.VMEM((400, 128), F32),
            pltpu.VMEM((288, 128), F32),
            pltpu.VMEM((2, 8, 128), F32),
            pltpu.VMEM((4, 2, 8, 128), F32),
            pltpu.VMEM((4, 2, 8, 128), F32),
            pltpu.VMEM((4, 2, 24, 128), F32),
            pltpu.VMEM((4, 8, 128), F32),
            pltpu.VMEM((4, 2, 8, 128), F32),
            pltpu.VMEM((4, 2, 8, 128), F32),
            pltpu.VMEM((4, 2, 24, 128), F32),
            pltpu.VMEM((4, 8, 128), F32),
            pltpu.VMEM((4, 8, 128), F32),
            pltpu.VMEM((4, 3, 8, 128), F32),
            pltpu.VMEM((2, 2, 24, 128), F32),
            pltpu.VMEM((160, 128), F32),
            pltpu.VMEM((80, 128), F32),
            pltpu.VMEM((80, 128), F32),
            pltpu.VMEM((5, 80, 128), F32),
            pltpu.VMEM((2, 80, 128), F32),
            pltpu.VMEM((2, 2, 8, 128), F32),
            pltpu.VMEM((2, 2, 7, 8, 128), F32),
            pltpu.VMEM((8, 128), F32),
            pltpu.VMEM((8, 8, 128), F32),
            pltpu.VMEM((3, 144, 128), F32),
            pltpu.VMEM((144, 128), F32),
            pltpu.VMEM((2, 8, 128), F32),
            pltpu.SemaphoreType.DMA((8,)),
            pltpu.SemaphoreType.DMA,
            pltpu.SemaphoreType.DMA((4, 26)),
            pltpu.SemaphoreType.DMA((4, 26)),
            pltpu.SemaphoreType.DMA((12,)),
            pltpu.SemaphoreType.DMA((11,)),
            pltpu.SemaphoreType.DMA((2, 2, 7)),
            pltpu.SemaphoreType.DMA((2, 2, 7)),
            pltpu.SemaphoreType.DMA((24,)),
            pltpu.SemaphoreType.DMA((8,)),
        ],
        compiler_params=pltpu.CompilerParams(collective_id=0, has_side_effects=True),
        name="step",
    )(
        states.reshape(108, 1, 128),
        previous.reshape(108, 1, 128),
        potential.reshape(108, 128),
        screening.reshape(108, 128),
        occupation.reshape(1, 1),
        cell_scale.reshape(1, 64),
        cell_matrix,
        connectivity.T,
    )
    return filtered.reshape(1, 13824), field.reshape(13824)


def solution(mesh):
    in_specs = (
        P("band", "dom"),
        P("band", "dom"),
        P("dom"),
        P("dom"),
        P("band"),
        P("dom"),
        P(),
        P(None, "dom"),
    )
    out_specs = (P("band", "dom"), P("dom"))
    return jax.shard_map(per_device, mesh=mesh, in_specs=in_specs, out_specs=out_specs, check_vma=False)
```

```python
import jax
import jax.numpy as jnp
from jax import lax
from jax.experimental import pallas as pl
from jax.experimental.pallas import tpu as pltpu
from jax.sharding import PartitionSpec as P

MESH = pl.DeviceIdType.MESH
F32 = jnp.float32
BF16 = jnp.bfloat16
STATES = 12
ZLO = 6
FILTER_CENTER = 2.0
FILTER_SCALE = 2.0 / 2.0


AROUND = [(x, y, z) for y in (1, -1, 0) for x in (1, -1, 0) for z in (1, -1, 0) if (x, y, z) != (0, 0, 0)]
BELOW = [d for d in AROUND if max(d) <= 0]
TILES = 38
CORE_ROWS = 288
ROWS = 8 * TILES


class Guarded:
    def __init__(self, copy, goes, comes):
        self.copy, self.goes, self.comes = copy, goes, comes

    def start(self):
        pl.when(self.goes)(self.copy.start)

    def wait_send(self):
        pl.when(self.goes)(self.copy.wait_send)

    def wait_recv(self):
        pl.when(self.comes)(self.copy.wait_recv)


def back(step):
    return tuple(-d for d in step)


def side(step):
    return 0 if step > 0 else 1

def roll(x, by, axis=1):
    by = by % x.shape[axis]
    return x if by == 0 else pltpu.roll(x, by, axis)


def iotas(rows=8, lanes=128):
    row = lax.broadcasted_iota(jnp.int32, (rows, lanes), 0)
    lane = lax.broadcasted_iota(jnp.int32, (rows, lanes), 1)
    return row, lane


def split(x):
    high = x.astype(BF16)
    return high, (x - high.astype(F32)).astype(BF16)


def column_table():
    row, lane = iotas(384, 384)
    g, cx = lane >> 3, lane & 7
    j = (g * 43) >> 8
    wanted = j * 48 + cx * 6 + (g - 6 * j)
    return jnp.where((row == wanted) & (lane < 288), 1.0, 0.0).astype(BF16)


def node_rows(rows):
    row, lane = iotas(rows, 384)
    k, v = row & 7, row >> 3
    return jnp.where((lane == 49 * k + v) & (k < 7) & (v < 49), 1.0, 0.0).astype(BF16)


def to_cells(tiles, table):
    n = tiles[0].shape[0]
    row, lane = iotas(n)
    group = lane >> 3
    chunks = []
    for cy in range(8):
        first, off = 288 * cy // 128, 288 * cy % 128
        parts = []
        for m in range(3):
            one = tiles[(first + m) % 18]
            if off:
                two = tiles[(first + m + 1) % 18]
                one = jnp.where(lane < 128 - off, roll(one, -off), roll(two, -off))
            parts.append(one)
        chunks.append(jnp.concatenate(parts, axis=1))
    stacked = jnp.concatenate(chunks, axis=0)
    high, low = split(stacked)
    both = jnp.dot(jnp.concatenate([high, low], axis=0), table, preferred_element_type=F32)
    moved = both[: 8 * n] + both[8 * n :]
    skewed = [
        [roll(moved[n * cy : n * cy + n, 128 * a : 128 * a + 128], 8 * cy) for a in range(3)]
        for cy in range(8)
    ]
    out = []
    for g in range(36):
        a, b = g // 16, g % 16
        got = jnp.where(group == b, skewed[0][a], 0.0)
        for cy in range(1, 8):
            got = jnp.where(group == (b + cy) % 16, skewed[cy][a], got)
        out.append(roll(got, -8 * b))
    return out


def split_exact(x):
    high, low = split(x)
    return high, low, (x - high.astype(F32) - low.astype(F32)).astype(BF16)


def from_cells(tiles, table):
    row, lane = iotas(8)
    group = lane >> 3
    placed = [roll(tiles[g], 8 * (g % 16)) for g in range(36)]
    rows = []
    for cy in range(8):
        parts = []
        for a in range(3):
            count = 16 if a < 2 else 4
            got = jnp.zeros((8, 128), F32)
            for b in range(count):
                got = jnp.where(group == (b + cy) % 16, placed[16 * a + b], got)
            parts.append(roll(got, -8 * cy))
        rows.append(jnp.concatenate(parts, axis=1))
    stacked = jnp.concatenate(rows, axis=0)
    both = lax.dot_general(
        jnp.concatenate(split_exact(stacked), axis=0), table, (((1,), (1,)), ((), ())), preferred_element_type=F32
    )
    moved = both[:64] + both[64:128] + both[128:]
    out = []
    for c in range(18):
        got = jnp.zeros((8, 128), F32)
        for cy in range(8):
            start = 288 * cy - 128 * c
            lo, hi = max(start, 0), min(start + 288, 128)
            if lo >= hi:
                continue
            off = start % 128
            for m in range(3):
                begin = start + 128 * m
                one_lo, one_hi = max(begin, lo), min(begin + 128, hi)
                if one_lo >= one_hi:
                    continue
                piece = roll(moved[8 * cy : 8 * cy + 8, 128 * m : 128 * m + 128], off)
                got = jnp.where((lane >= one_lo) & (lane < one_hi), piece, got)
        out.append(got)
    return out


def cell_terms(tiles, matrix_high, matrix_low, scale_row):
    high = tiles.astype(BF16).astype(F32)
    low = tiles - high
    _, lane = iotas(512)
    both = jnp.where(lane < 64, high, roll(low, 64)).astype(BF16)
    got = jnp.dot(matrix_high, both, preferred_element_type=F32)
    got = got + jnp.dot(matrix_low, both, preferred_element_type=F32)
    got = got + roll(got, 64)
    return got * scale_row


def local_fold(term):
    row, lane = iotas()
    cx, cy = lane & 7, lane >> 3
    upper_x = []
    for j in range(6):
        got = term(7 * j + 6)
        if j == 0:
            got = got + jnp.where(cy >= 1, roll(term(48), 8), 0.0)
        upper_x.append(got)
    x_tile = jnp.where(lane == 62, roll(term(48), -1), 0.0)
    for j in range(6):
        x_tile = jnp.where((cx == j) & (cy < 8), roll(upper_x[j], j - 7), x_tile)
    y_tile = jnp.zeros((8, 128), F32)
    for i in range(6):
        got = term(42 + i)
        if i == 0:
            got = got + jnp.where(cx >= 1, roll(term(48), 1), 0.0)
        y_tile = jnp.where(cy == i, roll(got, 8 * i - 56), y_tile)
    out = []
    for g in range(36):
        j, i = g // 6, g % 6
        got = term(7 * j + i)
        if j == 0:
            got = got + jnp.where(cy >= 1, roll(term(42 + i), 8), 0.0)
        if i == 0:
            got = got + jnp.where(cx >= 1, roll(upper_x[j], 1), 0.0)
        out.append(got)
    return out, x_tile, y_tile


def column_to_row(tile, at):
    row, lane = iotas()
    return jnp.sum(jnp.where(row == lane, jnp.broadcast_to(tile[:, at : at + 1], (8, 128)), 0.0), axis=0, keepdims=True)


def row_to_column(values):
    row, lane = iotas()
    return jnp.sum(jnp.where(row == lane, jnp.broadcast_to(values, (8, 128)), 0.0), axis=1, keepdims=True)


def wide(values):
    return jnp.broadcast_to(values, (8, 128))


def low_faces(field):
    row, lane = iotas()
    cx, cy = lane & 7, lane >> 3
    x_tile = jnp.zeros((8, 128), F32)
    y_tile = jnp.zeros((8, 128), F32)
    for j in range(6):
        x_tile = jnp.where((cx == j) & (cy < 8), roll(field(6 * j), j), x_tile)
    for i in range(6):
        y_tile = jnp.where(cy == i, roll(field(i), 8 * i), y_tile)
    return x_tile, y_tile


def from_above(field, x_tile, x_row, y_tile, y_row, edge, corner, z_row, high):
    row, lane = iotas()
    hx, hy, hz = high
    line = jnp.where(lane[0:1] == 6, roll(corner * hz, 6), edge)
    x_all = jnp.where(row == 6, wide(x_row * hz), x_tile)
    x_all = hx * jnp.where(lane == 62, wide(row_to_column(line) * hy), x_all)
    y_all = hy * jnp.where(row == 6, wide(y_row * hz), y_tile)
    core = [jnp.where(row == 6, wide(z_row(g) * hz), field(g)) for g in range(36)]
    return core + [x_all, y_all]


def extended(field):
    row, lane = iotas()
    cx, cy = lane & 7, lane >> 3
    x_all, y_all = field(36), field(37)
    out = [None] * 49
    for g in range(36):
        out[7 * (g // 6) + g % 6] = field(g)
    for j in range(6):
        out[7 * j + 6] = jnp.where(cx == 7, roll(x_all, 7 - j), roll(field(6 * j), -1))
    for i in range(6):
        out[42 + i] = jnp.where(cy == 7, roll(y_all, 56 - 8 * i), roll(field(i), -8))
    corner = jnp.where(cx == 7, roll(x_all, -1), roll(field(0), -9))
    corner = jnp.where(cy == 7, roll(y_all, 55), corner)
    out[48] = jnp.where(lane == 63, roll(x_all, 1), corner)
    return out


def shared(part, x_high, y_high):
    row, lane = iotas()
    x_low, y_low = low_faces(part)
    x_low = jnp.where(lane == 62, roll(y_high, 62), x_low)
    y_out = jnp.where(lane == 55, roll(x_high, -7), y_high)
    y_low = jnp.where(lane == 55, roll(x_high, 55), y_low)
    edges = [column_to_row(t, at) for t in (x_high, x_low) for at in (62, 0)]
    return (x_high, x_low), (y_out, y_low), edges


def absorb(part, x_high, y_high, xs, x_rows, ys, y_rows, edges, z_row, low, high):
    row, lane = iotas()
    cx, cy = lane & 7, lane >> 3
    hx, hy, hz = high
    lx, ly, lz = low

    def with_rows(tile, rows):
        return tile + jnp.where(row == 6, wide(rows[0]), jnp.where(row == 0, wide(rows[1] * lz), 0.0))

    x_up, x_down = with_rows(xs[0], x_rows[0]), with_rows(xs[1], x_rows[1]) * lx
    y_up, y_down = with_rows(ys[0], y_rows[0]), with_rows(ys[1], y_rows[1]) * ly
    lines = edges[0] + jnp.where(lane == 6, roll(edges[1], 6), jnp.where(lane == 0, roll(edges[2] * lz, -6), 0.0))
    columns = [wide(row_to_column(lines[c : c + 1])) for c in range(4)]
    up_row, down_row = row == 6, row == 0

    def vertical(up, down):
        return jnp.where(up_row, wide(up), jnp.where(down_row, wide(down * lz), 0.0))

    x_all = x_high + x_up + vertical(z_row(0, 36), z_row(1, 36))
    x_all = x_all + jnp.where(lane == 62, roll(y_up, 7) + columns[0], 0.0)
    x_all = x_all + jnp.where(lane == 0, roll(y_down, -55) + columns[1] * ly, 0.0)
    y_all = y_high + jnp.where(cy < 6, y_up, 0.0) + vertical(z_row(0, 37), z_row(1, 37))
    y_all = y_all + jnp.where(lane == 0, roll(x_down, -62) + columns[2] * lx, 0.0)
    top = jnp.where(up_row, hz, 1.0)
    x_all = x_all * (top * hx) * jnp.where(lane == 62, hy, 1.0)
    y_all = y_all * (top * hy)
    inside = jnp.where(lane < 64, top, 0.0)
    out = []
    for g in range(36):
        j, i = g // 6, g % 6
        got = part(g) + vertical(z_row(0, g), z_row(1, g))
        if i == 0:
            got = got + jnp.where((cx == 0) & (cy < 8), roll(x_down, -j), 0.0)
        if j == 0:
            got = got + jnp.where(cy == 0, roll(y_down, -8 * i), 0.0)
        if g == 0:
            got = got + jnp.where(lane == 0, columns[3] * (lx * ly), 0.0)
        out.append(jnp.where(lane < 64, got * inside, 0.0))
    return out + [x_all, y_all]


def kernel(
    states_ref, previous_ref, potential_ref, screening_ref, occupation_ref, scale_ref, matrix_ref, ids_ref,
    filtered_ref, field_ref,
    pad, raw_matrix, ids, given_scale, occupied, table, padded_matrix, cell_matrix, scales,
    own, screen, vec, grid_ext, terms, part, faces,
    sent_x, sent_y, sent_z, sent_e, got_x, got_y, got_z, got_xr, got_yr, got_e, z_both,
    dens, dens_in, half, half_in, full_in, red_out, red_in, last_out, last_in, nat, nat_f, factors,
    in_sem, out_sem, halo_send, halo_recv, band_send, band_recv, red_send, red_recv, last_send, last_recv,
):
    dom, band = lax.axis_index("dom"), lax.axis_index("band")
    px, py, pz = lax.rem(dom, 4), lax.rem(lax.div(dom, 4), 4), lax.div(dom, 16)
    z_lo, core = lax.div(band, 2), lax.rem(band, 2)
    z_hi = lax.rem(py, 2)
    across = 2 * (ZLO - 1 - z_lo) + core

    def place(x, y, z):
        return x + 4 * y + 16 * z

    def near(step, mirrored):
        x = lax.rem(px + (step[0] + 4), 4)
        y = lax.rem(py + (step[1] + 4), 4)
        z = lax.rem(pz + (step[2] + 4), 4)
        return (place(x, y, z), across if mirrored and step[1] else band)

    partner = (dom, 2 * z_lo + (1 - core))

    def chip(z):
        return (dom, 2 * z + core)

    y_at = lax.div(dom, 8)
    group_one, group_two = [], []
    for e in range(1, 8):
        x = lax.rem(px + e % 4, 4)
        y = py + 1 - 2 * z_hi if e // 4 else py
        group_one.append((place(x, y, pz), across if e // 4 else band))
    for e in range(1, 8):
        group_two.append((lax.rem(dom, 8) + 8 * lax.rem(y_at + e, 8), band))

    served = [
        [(device, 2 * jnp.where(z_lo == 0, 1 + s, ZLO - 2 - s) + core) for device in [dom] + [d for d, _ in group_two]]
        for s in range(2)
    ]
    serving = 2 * jnp.where(z_lo < ZLO // 2, 0, ZLO - 1) + core

    is_end = (z_lo == 0) | (z_lo == ZLO - 1)
    def inside(step):
        tests = []
        for at, d in zip((px, py, pz), step):
            if d:
                tests.append(at < 3 if d > 0 else at > 0)
        found = tests[0]
        for test in tests[1:]:
            found = found & test
        return found

    for got in (got_x, got_y, got_z, got_xr, got_yr, got_e):
        got[...] = jnp.zeros_like(got)
    barrier = pltpu.get_barrier_semaphore()

    def greet(device):
        pl.semaphore_signal(barrier, inc=1, device_id=device, device_id_type=MESH)

    for step in AROUND:
        pl.when(inside(step))(lambda step=step: greet(near(step, False)))
    others = [partner] + [chip(lax.rem(z_lo + e, ZLO)) for e in range(1, ZLO)]
    for device in others:
        greet(device)

    @pl.when(is_end)
    def _():
        for step in AROUND:
            if step[1]:
                pl.when(inside(step))(lambda step=step: greet(near(step, True)))
        for device in group_one + group_two + served[0][1:] + served[1][1:]:
            greet(device)

    @pl.when(jnp.logical_not(is_end))
    def _():
        for device, _ in group_two:
            greet((device, serving))

    def along(at):
        return 1 + lax.div(at + 3, 4) + lax.div(6 - at, 4)

    level = along(px) * along(pz)
    at_end = lax.div(z_lo, ZLO - 1) + lax.div(ZLO - 1 - z_lo, ZLO - 1)
    n_greeted = level * along(py) - 1 + len(others) + len(group_two)
    n_greeted = n_greeted + at_end * (level * (along(py) - 1) + len(group_one) + 2 * len(group_two))

    loads = [
        pltpu.make_async_copy(states_ref.at[:, 0, :], pad.at[0, pl.ds(0, 108), :], in_sem.at[0]),
        pltpu.make_async_copy(previous_ref.at[:, 0, :], pad.at[1, pl.ds(0, 108), :], in_sem.at[1]),
        pltpu.make_async_copy(potential_ref, pad.at[2, pl.ds(0, 108), :], in_sem.at[2]),
        pltpu.make_async_copy(screening_ref, pad.at[3, pl.ds(0, 108), :], in_sem.at[3]),
        pltpu.make_async_copy(matrix_ref, raw_matrix, in_sem.at[4]),
        pltpu.make_async_copy(ids_ref.at[:, pl.ds(0, 128)], ids, in_sem.at[5]),
        pltpu.make_async_copy(scale_ref, given_scale, in_sem.at[6]),
        pltpu.make_async_copy(occupation_ref, occupied, in_sem.at[7]),
    ]
    for load in loads:
        load.start()

    def flag(test):
        return jnp.where(test, 1.0, 0.0).astype(F32)

    high = (flag(px < 3), flag(py < 3), flag(pz < 3))
    low = (flag(px > 0), flag(py > 0), flag(pz > 0))
    row, lane = iotas()

    table[...] = column_table()
    for m in range(4):
        pad[m, 108:144, :] = jnp.zeros((36, 128), F32)
    grid_ext[...] = jnp.zeros_like(grid_ext)
    sent_z[...] = jnp.zeros_like(sent_z)
    loads[0].wait()
    first = to_cells([pad[0, pl.ds(c, 8, stride=18), :] for c in range(18)], table[...])
    for g in range(36):
        own[8 * g : 8 * g + 8, :] = first[g]

    def tile_of(source):
        return lambda g: source[8 * g : 8 * g + 8, :]

    def copy_to(at, step, mirrored):
        x, y, z = step
        s, t = side(-x), side(-y)
        if x and y:
            src = sent_e.at[at, pl.ds(2 * side(x) + side(y), 1)]
            dst = got_e.at[at, 0 if z == 0 else 1 + side(-z), pl.ds(2 * s + t, 1)]
        elif x:
            src, dst = sent_x.at[at, side(x)], got_x.at[at, s]
            if z:
                src = src.at[pl.ds(6 if z > 0 else 0, 1)]
                dst = got_xr.at[at, pl.ds(2 * s + side(-z), 1)]
        elif y:
            src, dst = sent_y.at[at, side(y)], got_y.at[at, t]
            if z:
                src = src.at[pl.ds(6 if z > 0 else 0, 1)]
                dst = got_yr.at[at, pl.ds(2 * t + side(-z), 1)]
        else:
            src, dst = sent_z.at[at, side(z)], got_z.at[at, side(-z)]
        e = AROUND.index(step)
        return pltpu.make_async_remote_copy(
            src_ref=src,
            dst_ref=dst,
            send_sem=halo_send.at[at, e],
            recv_sem=halo_recv.at[at, e],
            device_id=near(step, mirrored),
            device_id_type=MESH,
        )

    def start_copies(at, steps, mirrored):
        made = [Guarded(copy_to(at, step, mirrored), inside(step), inside(back(step))) for step in steps]
        for copy in made:
            copy.start()
        return made

    _, lane_18 = iotas(18)

    def put_z(at, s, source, sublane):
        lower = source[pl.ds(sublane, 18, stride=8), :]
        upper = source[pl.ds(144 + sublane, 18, stride=8), :]
        sent_z[at, s, 0:18, :] = jnp.where(lane_18 < 64, lower, roll(upper, 64))

    def take_z(at, s):
        rows = got_z[at, s]
        z_both[s, 0] = rows
        z_both[s, 1] = roll(rows, 64)

    def z_row(s, m):
        if m >= 36:
            return z_both[s, 0, m - 18 : m - 17, :]
        return z_both[s, m // 18, m % 18 : m % 18 + 1, :]

    def products(source):
        tiles = extended(tile_of(source))
        for v in range(49):
            grid_ext[8 * v : 8 * v + 8, :] = tiles[v]
        terms[...] = cell_terms(grid_ext[...], cell_matrix[0], cell_matrix[1], scales[0:1, :])

    def cell_sums(source, factor, extra):
        products(source)
        folded, x_high, y_high = local_fold(lambda v: terms[8 * v : 8 * v + 8, :])
        for g in range(36):
            part[8 * g : 8 * g + 8, :] = factor * folded[g] + extra(g)
        faces[0], faces[1] = factor * x_high, factor * y_high

    def put_level(at, xs, x_high, y_high):
        for s in range(2):
            k = 6 if s == 0 else 0
            sent_x[at, s] = xs[s]
            put_z(at, s, part, k)
            sent_z[at, s, 18:19, :] = x_high[k : k + 1]
            sent_z[at, s, 19:20, :] = y_high[k : k + 1]

    def start_sums(at, source, factor, extra, mirrored):
        cell_sums(source, factor, extra)
        x_high, y_high = faces[0], faces[1]
        xs, ys, edges = shared(tile_of(part), x_high, y_high)
        put_level(at, xs, x_high, y_high)
        for s in range(2):
            sent_y[at, s] = ys[s]
        for c in range(4):
            sent_e[at, c : c + 1, :] = edges[c]
        return start_copies(at, AROUND, mirrored)

    def finish_sums(at, made):
        for copy in made:
            copy.wait_recv()
        take_z(at, 0)
        take_z(at, 1)
        return absorb(
            tile_of(part),
            faces[0],
            faces[1],
            [got_x[at, s] for s in range(2)],
            [[got_xr[at, 2 * s + t : 2 * s + t + 1, :] for t in range(2)] for s in range(2)],
            [got_y[at, s] for s in range(2)],
            [[got_yr[at, 2 * s + t : 2 * s + t + 1, :] for t in range(2)] for s in range(2)],
            [got_e[at, t] for t in range(3)],
            z_row,
            low,
            high,
        )

    x_tile, y_tile = low_faces(tile_of(own))
    sent_x[0, 1] = x_tile
    sent_y[0, 1] = y_tile
    sent_e[0, 3:4, :] = column_to_row(own[0:8, :], 0)
    put_z(0, 1, own, 0)

    pl.semaphore_wait(barrier, n_greeted)
    ghosts = start_copies(0, BELOW, False)

    for load in loads[1:]:
        load.wait()
    three = to_cells(
        [
            jnp.concatenate([pad[m, pl.ds(c, 8, stride=18), :] for m in (1, 2, 3)], axis=0)
            for c in range(18)
        ],
        table[...],
    )
    for g in range(36):
        rows = slice(8 * g, 8 * g + 8)
        screen[rows, :] = three[g][16:24]
        vec[0, rows, :] = FILTER_SCALE * ((three[g][8:16] - FILTER_CENTER) * own[rows, :]) - three[g][0:8]
    padded_matrix[...] = jnp.zeros_like(padded_matrix)
    padded_matrix[0:343, 0:343] = raw_matrix[...]
    by_row, by_column = node_rows(400), node_rows(512)
    for h, piece in enumerate(split(padded_matrix[...])):
        rows_moved = jnp.dot(by_row, piece, preferred_element_type=F32).astype(BF16)
        cell_matrix[h] = lax.dot_general(
            rows_moved, by_column, (((1,), (1,)), ((), ())), preferred_element_type=F32
        ).astype(BF16)
    _, lane_64 = iotas(64)
    first_id = 6 * 49 * ((lane_64 & 63) >> 3) + 6 * (lane_64 & 7)
    matches = jnp.where(first_id == jnp.broadcast_to(ids[:, 0:1], (64, 128)), 1.0, 0.0).astype(F32)
    given = jnp.broadcast_to(given_scale[...], (8, 64))
    scales[...] = jnp.dot(given, matches, precision=lax.Precision.HIGHEST, preferred_element_type=F32)

    for copy in ghosts:
        copy.wait_recv()
    take_z(0, 0)
    compact = from_above(
        tile_of(own),
        got_x[0, 0],
        got_xr[0, 0:1, :],
        got_y[0, 0],
        got_yr[0, 0:1, :],
        got_e[0, 0, 0:1, :],
        got_e[0, 1, 0:1, :],
        lambda g: z_row(0, g),
        high,
    )
    for m in range(TILES):
        vec[1, 8 * m : 8 * m + 8, :] = compact[m]
    summing = start_sums(1, vec.at[1], 0.5 * FILTER_SCALE, tile_of(vec.at[0]), False)
    values = finish_sums(1, summing)
    weight = occupied[...]
    squares = [weight * value * value for value in values]
    two_faces = squares[36] + roll(squares[37], 64)
    for m in range(18):
        tile = squares[m] + roll(squares[m + 18], 64)
        if m < 7:
            tile = jnp.where(row == 7, wide(two_faces[m : m + 1]), tile)
        dens[8 * m : 8 * m + 8, :] = tile

    mine = pl.multiple_of(72 * core, 8)
    other = pl.multiple_of(72 * (1 - core), 8)

    def band_copy(src, dst, at_send, at_recv, device):
        return pltpu.make_async_remote_copy(
            src_ref=src,
            dst_ref=dst,
            send_sem=band_send.at[at_send],
            recv_sem=band_recv.at[at_recv],
            device_id=device,
            device_id_type=MESH,
        )

    swap = band_copy(dens.at[pl.ds(other, 72), :], dens_in, 0, 0, partner)
    swap.start()
    for m in range(36):
        vec[0, 8 * m : 8 * m + 8, :] = values[m]
    swap.wait_recv()
    half[...] = dens[pl.ds(mine, 72), :] + dens_in[...]

    not_first, not_last = z_lo > 0, z_lo < ZLO - 1
    slot_first = jnp.maximum(z_lo - 1, 0)
    slot_last = jnp.minimum(z_lo, ZLO - 2)
    to_first = band_copy(half, half_in.at[slot_first], 1, 1 + slot_first, chip(0))
    to_last = band_copy(half, half_in.at[slot_last], 2, 1 + slot_last, chip(ZLO - 1))

    @pl.when(not_first)
    def _():
        to_first.start()

    @pl.when(not_last)
    def _():
        to_last.start()

    natural = from_cells([jnp.where(row < 6, vec[0, 8 * g : 8 * g + 8, :], 0.0) for g in range(36)], table[...])
    for c in range(18):
        nat_f[pl.ds(c, 8, stride=18), :] = natural[c]
    store = pltpu.make_async_copy(nat_f.at[pl.ds(0, 108), :], filtered_ref, out_sem)
    store.start()

    B, W, Q, R1, W1 = 0, 1, 2, 3, 4

    def last_copy(at_send, e, device):
        return pltpu.make_async_remote_copy(
            src_ref=last_out,
            dst_ref=last_in.at[e],
            send_sem=last_send.at[at_send],
            recv_sem=last_recv.at[e],
            device_id=device,
            device_id_type=MESH,
        )

    def write_field(got, known):
        for e in range(1, 8):
            got = got + last_in[e]
        got = jnp.sum(got, axis=1, keepdims=True)
        c_b, c_w, c_q = combine(*[known[m : m + 1, 0:1] for m in range(3)], *[got[m : m + 1] for m in range(8)])
        field_ref[...] = c_b * nat[0, 0:108, :] + c_w * nat[1, 0:108, :] + c_q * nat[2, 0:108, :]

    @pl.when(is_end)
    def _():
        arrived = [band_copy(half, half_in.at[s], 1, 1 + s, partner) for s in range(ZLO - 1)]
        for copy in arrived:
            copy.wait_recv()
        total = half[...]
        for s in range(ZLO - 1):
            total = total + half_in[s]
        full_in[0] = total * (1.0 / STATES)
        again = band_copy(full_in.at[0], full_in.at[1], 3, 6, partner)
        again.start()
        again.wait_recv()
        both = (
            jnp.where(core == 0, full_in[0], full_in[1]),
            jnp.where(core == 0, full_in[1], full_in[0]),
        )
        two_faces = jnp.zeros((8, 128), F32)
        for m in range(18):
            tile = both[m // 9][8 * (m % 9) : 8 * (m % 9) + 8]
            if m < 7:
                two_faces = jnp.where(row == m, wide(tile[7:8]), two_faces)
            tile = jnp.where(row < 7, tile, 0.0)
            vec[B, 8 * m : 8 * m + 8, :] = jnp.where(lane < 64, tile, 0.0)
            vec[B, 8 * (m + 18) : 8 * (m + 18) + 8, :] = jnp.where(lane < 64, roll(tile, 64), 0.0)
        vec[B, 288:296, :] = jnp.where(lane < 64, two_faces, 0.0)
        vec[B, 296:304, :] = jnp.where(lane < 64, roll(two_faces, 64), 0.0)

        def put(v, tiles):
            for m in range(TILES):
                vec[v, 8 * m : 8 * m + 8, :] = tiles[m]

        def screened(v):
            return lambda g: screen[8 * g : 8 * g + 8, :] * vec[v, 8 * g : 8 * g + 8, :]

        def onto_row(got):
            got = jnp.sum(got.reshape(36, 8, 128), axis=0)
            return jnp.sum(jnp.where(row < 6, got, 0.0), axis=0, keepdims=True)

        def dot_row(a, b):
            return onto_row(vec[a, 0:CORE_ROWS, :] * vec[b, 0:CORE_ROWS, :])

        def send_reduce(n, level, devices):
            made = [
                pltpu.make_async_remote_copy(
                    src_ref=red_out.at[n, level],
                    dst_ref=red_in.at[n, level, e],
                    send_sem=red_send.at[n, level, e],
                    recv_sem=red_recv.at[n, level, e],
                    device_id=device,
                    device_id_type=MESH,
                )
                for e, device in enumerate(devices)
            ]
            for copy in made:
                copy.start()
            return made

        def start_reduce(n, rows):
            tile = jnp.zeros((8, 128), F32)
            for m, values in enumerate(rows):
                tile = jnp.where(row == m, wide(values), tile)
            red_out[n, 0] = tile
            return send_reduce(n, 0, group_one)

        def take(n, level, made):
            for copy in made:
                copy.wait_recv()
            got = red_out[n, level]
            for e in range(7):
                got = got + red_in[n, level, e]
            return got

        def second_level(n, made):
            red_out[n, 1] = take(n, 0, made)
            return send_reduce(n, 1, group_two)

        def scalars(n, made, count):
            got = jnp.sum(take(n, 1, made), axis=1, keepdims=True)
            return [got[m : m + 1] for m in range(count)]

        def hand_on(n, v):
            natural = from_cells(
                [jnp.where(row < 6, vec[v, 8 * g : 8 * g + 8, :], 0.0) for g in range(36)], table[...]
            )
            for c in range(18):
                nat[n, pl.ds(c, 8, stride=18), :] = natural[c]
            return onward(nat.at[n, 0:112], nat.at[n, 0:112], n)

        def onward(src, dst, n):
            made = [
                band_copy(src, dst, 4 + 2 * n + s, 7 + n, chip(jnp.where(z_lo == 0, 1 + s, ZLO - 2 - s)))
                for s in range(2)
            ]
            for copy in made:
                copy.start()
            return made

        def energy_row(v):
            cells = jnp.sum((grid_ext[0:392, :] * terms[0:392, :]).reshape(49, 8, 128), axis=0)
            cells = jnp.sum(jnp.where(lane < 64, cells, 0.0), axis=0, keepdims=True)
            owned = vec[v, 0:CORE_ROWS, :]
            return cells + onto_row(screen[...] * owned * owned)

        sent = [again]
        made = start_sums(2, vec.at[B], 1.0, screened(B), True)
        red_a = start_reduce(0, [dot_row(B, B), energy_row(B)])
        sent += made + red_a + hand_on(0, B)
        put(W, finish_sums(2, made))
        red_b = second_level(0, red_a)
        made = start_sums(3, vec.at[W], 1.0, screened(W), True)
        sent += made + red_b + hand_on(1, W)
        put(Q, finish_sums(3, made))
        norm_0, image_0 = scalars(0, red_b, 2)
        alpha_0 = norm_0 / image_0
        factors[0] = jnp.where(row == 0, wide(alpha_0), jnp.where(row == 1, wide(norm_0), wide(image_0)))
        sent += onward(factors.at[0], factors.at[1], 3)

        vec[R1] = vec[B] - alpha_0 * vec[W]
        vec[W1] = vec[W] - alpha_0 * vec[Q]
        products(vec.at[W1])
        red_a = start_reduce(
            1,
            [
                dot_row(R1, R1),
                dot_row(R1, W1),
                dot_row(R1, W),
                dot_row(W1, W1),
                dot_row(W1, W),
                energy_row(W1),
                dot_row(W1, Q),
                dot_row(W, Q),
            ],
        )
        sent += hand_on(2, Q)
        last_out[...] = take(1, 0, red_a)
        last = [last_copy(e, e, device) for e, device in enumerate(group_two, 1)]
        for m in range(2):
            last += [last_copy(8 * (m + 1) + e, e, device) for e, device in enumerate(served[m])]
        for copy in last:
            copy.start()
        sent += red_a + last
        for copy in last[:7]:
            copy.wait_recv()
        write_field(last_out[...], factors[0])
        for copy in sent:
            copy.wait_send()

    @pl.when(jnp.logical_not(is_end))
    def _():
        for n in range(3):
            band_copy(nat.at[n, 0:112], nat.at[n, 0:112], 4, 7 + n, partner).wait_recv()
        band_copy(factors.at[0], factors.at[1], 4, 10, partner).wait_recv()
        for e in range(8):
            last_copy(e, e, partner).wait_recv()
        write_field(last_in[0], factors[1])

    swap.wait_send()

    @pl.when(not_first)
    def _():
        to_first.wait_send()

    @pl.when(not_last)
    def _():
        to_last.wait_send()

    for copy in ghosts + summing:
        copy.wait_send()
    store.wait()


def combine(alpha_0, norm_0, image_0, norm_1, rw, rv, ww, wv, waw, wav, vav):
    beta_1 = norm_1 / norm_0
    image_1 = rw + 2.0 * beta_1 * rv + beta_1 * beta_1 * image_0
    alpha_1 = norm_1 / image_1
    r_s = rw + beta_1 * rv
    s_s = ww + 2.0 * beta_1 * wv + beta_1 * beta_1 * (wv_self(alpha_0, wv, vav))
    r_as = ww + beta_1 * wv
    s_as = waw + 2.0 * beta_1 * wav + beta_1 * beta_1 * vav
    norm_2 = jnp.maximum(norm_1 - 2.0 * alpha_1 * r_s + alpha_1 * alpha_1 * s_s, 0.0)
    r2_ar2 = rw - 2.0 * alpha_1 * r_as + alpha_1 * alpha_1 * s_as
    r2_s = r_s - alpha_1 * s_s
    beta_2 = norm_2 / norm_1
    image_2 = r2_ar2 + 2.0 * beta_2 * r2_s + beta_2 * beta_2 * image_1
    alpha_2 = jnp.where(image_2 > 0.0, norm_2 / image_2, 0.0)
    grown = alpha_0 + alpha_1 * (1.0 + beta_1)
    c_b = grown + alpha_2 * (1.0 + beta_2 * (1.0 + beta_1))
    c_w = -alpha_1 * alpha_0 - alpha_2 * (grown + beta_2 * alpha_0)
    c_q = alpha_2 * alpha_1 * alpha_0
    return c_b, c_w, c_q


def wv_self(alpha_0, wv, vav):
    return wv + alpha_0 * vav


def per_device(states, previous, potential, screening, occupation, cell_scale, cell_matrix, connectivity):
    vmem = pl.BlockSpec(memory_space=pltpu.VMEM)
    anywhere = pl.BlockSpec(memory_space=pl.ANY)
    filtered, field = pl.pallas_call(
        kernel,
        out_shape=(jax.ShapeDtypeStruct((108, 128), F32), jax.ShapeDtypeStruct((108, 128), F32)),
        in_specs=[anywhere] * 8,
        out_specs=(anywhere, vmem),
        scratch_shapes=[
            pltpu.VMEM((4, 144, 128), F32),
            pltpu.VMEM((343, 343), F32),
            pltpu.VMEM((64, 128), jnp.int32),
            pltpu.VMEM((1, 64), F32),
            pltpu.VMEM((1, 1), F32),
            pltpu.VMEM((384, 384), BF16),
            pltpu.VMEM((384, 384), F32),
            pltpu.VMEM((2, 400, 512), BF16),
            pltpu.VMEM((8, 128), F32),
            pltpu.VMEM((288, 128), F32),
            pltpu.VMEM((288, 128), F32),
            pltpu.VMEM((5, ROWS, 128), F32),
            pltpu.VMEM((512, 128), F32),
            pltpu.VMEM((400, 128), F32),
            pltpu.VMEM((288, 128), F32),
            pltpu.VMEM((2, 8, 128), F32),
            pltpu.VMEM((4, 2, 8, 128), F32),
            pltpu.VMEM((4, 2, 8, 128), F32),
            pltpu.VMEM((4, 2, 24, 128), F32),
            pltpu.VMEM((4, 8, 128), F32),
            pltpu.VMEM((4, 2, 8, 128), F32),
            pltpu.VMEM((4, 2, 8, 128), F32),
            pltpu.VMEM((4, 2, 24, 128), F32),
            pltpu.VMEM((4, 8, 128), F32),
            pltpu.VMEM((4, 8, 128), F32),
            pltpu.VMEM((4, 3, 8, 128), F32),
            pltpu.VMEM((2, 2, 24, 128), F32),
            pltpu.VMEM((144, 128), F32),
            pltpu.VMEM((72, 128), F32),
            pltpu.VMEM((72, 128), F32),
            pltpu.VMEM((5, 72, 128), F32),
            pltpu.VMEM((2, 72, 128), F32),
            pltpu.VMEM((2, 2, 8, 128), F32),
            pltpu.VMEM((2, 2, 7, 8, 128), F32),
            pltpu.VMEM((8, 128), F32),
            pltpu.VMEM((8, 8, 128), F32),
            pltpu.VMEM((3, 144, 128), F32),
            pltpu.VMEM((144, 128), F32),
            pltpu.VMEM((2, 8, 128), F32),
            pltpu.SemaphoreType.DMA((8,)),
            pltpu.SemaphoreType.DMA,
            pltpu.SemaphoreType.DMA((4, 26)),
            pltpu.SemaphoreType.DMA((4, 26)),
            pltpu.SemaphoreType.DMA((12,)),
            pltpu.SemaphoreType.DMA((11,)),
            pltpu.SemaphoreType.DMA((2, 2, 7)),
            pltpu.SemaphoreType.DMA((2, 2, 7)),
            pltpu.SemaphoreType.DMA((24,)),
            pltpu.SemaphoreType.DMA((8,)),
        ],
        compiler_params=pltpu.CompilerParams(collective_id=0, has_side_effects=True),
        name="step",
    )(
        states.reshape(108, 1, 128),
        previous.reshape(108, 1, 128),
        potential.reshape(108, 128),
        screening.reshape(108, 128),
        occupation.reshape(1, 1),
        cell_scale.reshape(1, 64),
        cell_matrix,
        connectivity.T,
    )
    flat = lax.optimization_barrier(filtered.reshape(13824))
    return flat.reshape(1, 13824), field.reshape(13824)


def solution(mesh):
    in_specs = (
        P("band", "dom"),
        P("band", "dom"),
        P("dom"),
        P("dom"),
        P("band"),
        P("dom"),
        P(),
        P(None, "dom"),
    )
    out_specs = (P("band", "dom"), P("dom"))
    return jax.shard_map(per_device, mesh=mesh, in_specs=in_specs, out_specs=out_specs, check_vma=False)
```

```python
import jax
import jax.numpy as jnp
from jax import lax
from jax.experimental import pallas as pl
from jax.experimental.pallas import tpu as pltpu
from jax.sharding import PartitionSpec as P

MESH = pl.DeviceIdType.MESH
F32 = jnp.float32
BF16 = jnp.bfloat16
STATES = 12
ZLO = 6
FILTER_CENTER = 2.0
FILTER_SCALE = 2.0 / 2.0


AROUND = [(x, y, z) for y in (1, -1, 0) for x in (1, -1, 0) for z in (1, -1, 0) if (x, y, z) != (0, 0, 0)]
BELOW = [d for d in AROUND if max(d) <= 0]
TILES = 38
CORE_ROWS = 288
ROWS = 8 * TILES


class Guarded:
    def __init__(self, copy, goes, comes):
        self.copy, self.goes, self.comes = copy, goes, comes

    def start(self):
        pl.when(self.goes)(self.copy.start)

    def wait_send(self):
        pl.when(self.goes)(self.copy.wait_send)

    def wait_recv(self):
        pl.when(self.comes)(self.copy.wait_recv)


def back(step):
    return tuple(-d for d in step)


def side(step):
    return 0 if step > 0 else 1

def roll(x, by, axis=1):
    by = by % x.shape[axis]
    return x if by == 0 else pltpu.roll(x, by, axis)


def iotas(rows=8, lanes=128):
    row = lax.broadcasted_iota(jnp.int32, (rows, lanes), 0)
    lane = lax.broadcasted_iota(jnp.int32, (rows, lanes), 1)
    return row, lane


def split(x):
    high = x.astype(BF16)
    return high, (x - high.astype(F32)).astype(BF16)


def column_table():
    row, lane = iotas(384, 384)
    g, cx = lane >> 3, lane & 7
    j = (g * 43) >> 8
    wanted = j * 48 + cx * 6 + (g - 6 * j)
    return jnp.where((row == wanted) & (lane < 288), 1.0, 0.0).astype(BF16)


def node_rows(rows):
    row, lane = iotas(rows, 384)
    k, v = row & 7, row >> 3
    return jnp.where((lane == 49 * k + v) & (k < 7) & (v < 49), 1.0, 0.0).astype(BF16)


def to_cells(tiles, table):
    n = tiles[0].shape[0]
    row, lane = iotas(n)
    group = lane >> 3
    chunks = []
    for cy in range(8):
        first, off = 288 * cy // 128, 288 * cy % 128
        parts = []
        for m in range(3):
            one = tiles[(first + m) % 18]
            if off:
                two = tiles[(first + m + 1) % 18]
                one = jnp.where(lane < 128 - off, roll(one, -off), roll(two, -off))
            parts.append(one)
        chunks.append(jnp.concatenate(parts, axis=1))
    stacked = jnp.concatenate(chunks, axis=0)
    high, low = split(stacked)
    both = jnp.dot(jnp.concatenate([high, low], axis=0), table, preferred_element_type=F32)
    moved = both[: 8 * n] + both[8 * n :]
    skewed = [
        [roll(moved[n * cy : n * cy + n, 128 * a : 128 * a + 128], 8 * cy) for a in range(3)]
        for cy in range(8)
    ]
    out = []
    for g in range(36):
        a, b = g // 16, g % 16
        got = jnp.where(group == b, skewed[0][a], 0.0)
        for cy in range(1, 8):
            got = jnp.where(group == (b + cy) % 16, skewed[cy][a], got)
        out.append(roll(got, -8 * b))
    return out


def split_exact(x):
    high, low = split(x)
    return high, low, (x - high.astype(F32) - low.astype(F32)).astype(BF16)


def from_cells(tiles, table):
    row, lane = iotas(8)
    group = lane >> 3
    placed = [roll(tiles[g], 8 * (g % 16)) for g in range(36)]
    rows = []
    for cy in range(8):
        parts = []
        for a in range(3):
            count = 16 if a < 2 else 4
            got = jnp.zeros((8, 128), F32)
            for b in range(count):
                got = jnp.where(group == (b + cy) % 16, placed[16 * a + b], got)
            parts.append(roll(got, -8 * cy))
        rows.append(jnp.concatenate(parts, axis=1))
    stacked = jnp.concatenate(rows, axis=0)
    both = lax.dot_general(
        jnp.concatenate(split_exact(stacked), axis=0), table, (((1,), (1,)), ((), ())), preferred_element_type=F32
    )
    moved = both[:64] + both[64:128] + both[128:]
    out = []
    for c in range(18):
        got = jnp.zeros((8, 128), F32)
        for cy in range(8):
            start = 288 * cy - 128 * c
            lo, hi = max(start, 0), min(start + 288, 128)
            if lo >= hi:
                continue
            off = start % 128
            for m in range(3):
                begin = start + 128 * m
                one_lo, one_hi = max(begin, lo), min(begin + 128, hi)
                if one_lo >= one_hi:
                    continue
                piece = roll(moved[8 * cy : 8 * cy + 8, 128 * m : 128 * m + 128], off)
                got = jnp.where((lane >= one_lo) & (lane < one_hi), piece, got)
        out.append(got)
    return out


def cell_terms(tiles, matrix_high, matrix_low, scale_row):
    high = tiles.astype(BF16).astype(F32)
    low = tiles - high
    _, lane = iotas(512)
    both = jnp.where(lane < 64, high, roll(low, 64)).astype(BF16)
    got = jnp.dot(matrix_high, both, preferred_element_type=F32)
    got = got + jnp.dot(matrix_low, both, preferred_element_type=F32)
    got = got + roll(got, 64)
    return got * scale_row


def local_fold(term):
    row, lane = iotas()
    cx, cy = lane & 7, lane >> 3
    upper_x = []
    for j in range(6):
        got = term(7 * j + 6)
        if j == 0:
            got = got + jnp.where(cy >= 1, roll(term(48), 8), 0.0)
        upper_x.append(got)
    x_tile = jnp.where(lane == 62, roll(term(48), -1), 0.0)
    for j in range(6):
        x_tile = jnp.where((cx == j) & (cy < 8), roll(upper_x[j], j - 7), x_tile)
    y_tile = jnp.zeros((8, 128), F32)
    for i in range(6):
        got = term(42 + i)
        if i == 0:
            got = got + jnp.where(cx >= 1, roll(term(48), 1), 0.0)
        y_tile = jnp.where(cy == i, roll(got, 8 * i - 56), y_tile)
    out = []
    for g in range(36):
        j, i = g // 6, g % 6
        got = term(7 * j + i)
        if j == 0:
            got = got + jnp.where(cy >= 1, roll(term(42 + i), 8), 0.0)
        if i == 0:
            got = got + jnp.where(cx >= 1, roll(upper_x[j], 1), 0.0)
        out.append(got)
    return out, x_tile, y_tile


def column_to_row(tile, at):
    row, lane = iotas()
    return jnp.sum(jnp.where(row == lane, jnp.broadcast_to(tile[:, at : at + 1], (8, 128)), 0.0), axis=0, keepdims=True)


def row_to_column(values):
    row, lane = iotas()
    return jnp.sum(jnp.where(row == lane, jnp.broadcast_to(values, (8, 128)), 0.0), axis=1, keepdims=True)


def wide(values):
    return jnp.broadcast_to(values, (8, 128))


def low_faces(field):
    row, lane = iotas()
    cx, cy = lane & 7, lane >> 3
    x_tile = jnp.zeros((8, 128), F32)
    y_tile = jnp.zeros((8, 128), F32)
    for j in range(6):
        x_tile = jnp.where((cx == j) & (cy < 8), roll(field(6 * j), j), x_tile)
    for i in range(6):
        y_tile = jnp.where(cy == i, roll(field(i), 8 * i), y_tile)
    return x_tile, y_tile


def from_above(field, x_tile, x_row, y_tile, y_row, edge, corner, z_row, high):
    row, lane = iotas()
    hx, hy, hz = high
    line = jnp.where(lane[0:1] == 6, roll(corner * hz, 6), edge)
    x_all = jnp.where(row == 6, wide(x_row * hz), x_tile)
    x_all = hx * jnp.where(lane == 62, wide(row_to_column(line) * hy), x_all)
    y_all = hy * jnp.where(row == 6, wide(y_row * hz), y_tile)
    core = [jnp.where(row == 6, wide(z_row(g) * hz), field(g)) for g in range(36)]
    return core + [x_all, y_all]


def extended(field):
    row, lane = iotas()
    cx, cy = lane & 7, lane >> 3
    x_all, y_all = field(36), field(37)
    out = [None] * 49
    for g in range(36):
        out[7 * (g // 6) + g % 6] = field(g)
    for j in range(6):
        out[7 * j + 6] = jnp.where(cx == 7, roll(x_all, 7 - j), roll(field(6 * j), -1))
    for i in range(6):
        out[42 + i] = jnp.where(cy == 7, roll(y_all, 56 - 8 * i), roll(field(i), -8))
    corner = jnp.where(cx == 7, roll(x_all, -1), roll(field(0), -9))
    corner = jnp.where(cy == 7, roll(y_all, 55), corner)
    out[48] = jnp.where(lane == 63, roll(x_all, 1), corner)
    return out


def shared(part, x_high, y_high):
    row, lane = iotas()
    x_low, y_low = low_faces(part)
    x_low = jnp.where(lane == 62, roll(y_high, 62), x_low)
    y_out = jnp.where(lane == 55, roll(x_high, -7), y_high)
    y_low = jnp.where(lane == 55, roll(x_high, 55), y_low)
    edges = [column_to_row(t, at) for t in (x_high, x_low) for at in (62, 0)]
    return (x_high, x_low), (y_out, y_low), edges


def absorb(part, x_high, y_high, xs, x_rows, ys, y_rows, edges, z_row, low, high):
    row, lane = iotas()
    cx, cy = lane & 7, lane >> 3
    hx, hy, hz = high
    lx, ly, lz = low

    def with_rows(tile, rows):
        return tile + jnp.where(row == 6, wide(rows[0]), jnp.where(row == 0, wide(rows[1] * lz), 0.0))

    x_up, x_down = with_rows(xs[0], x_rows[0]), with_rows(xs[1], x_rows[1]) * lx
    y_up, y_down = with_rows(ys[0], y_rows[0]), with_rows(ys[1], y_rows[1]) * ly
    lines = edges[0] + jnp.where(lane == 6, roll(edges[1], 6), jnp.where(lane == 0, roll(edges[2] * lz, -6), 0.0))
    columns = [wide(row_to_column(lines[c : c + 1])) for c in range(4)]
    up_row, down_row = row == 6, row == 0

    def vertical(up, down):
        return jnp.where(up_row, wide(up), jnp.where(down_row, wide(down * lz), 0.0))

    x_all = x_high + x_up + vertical(z_row(0, 36), z_row(1, 36))
    x_all = x_all + jnp.where(lane == 62, roll(y_up, 7) + columns[0], 0.0)
    x_all = x_all + jnp.where(lane == 0, roll(y_down, -55) + columns[1] * ly, 0.0)
    y_all = y_high + jnp.where(cy < 6, y_up, 0.0) + vertical(z_row(0, 37), z_row(1, 37))
    y_all = y_all + jnp.where(lane == 0, roll(x_down, -62) + columns[2] * lx, 0.0)
    top = jnp.where(up_row, hz, 1.0)
    x_all = x_all * (top * hx) * jnp.where(lane == 62, hy, 1.0)
    y_all = y_all * (top * hy)
    inside = jnp.where(lane < 64, top, 0.0)
    out = []
    for g in range(36):
        j, i = g // 6, g % 6
        got = part(g) + vertical(z_row(0, g), z_row(1, g))
        if i == 0:
            got = got + jnp.where((cx == 0) & (cy < 8), roll(x_down, -j), 0.0)
        if j == 0:
            got = got + jnp.where(cy == 0, roll(y_down, -8 * i), 0.0)
        if g == 0:
            got = got + jnp.where(lane == 0, columns[3] * (lx * ly), 0.0)
        out.append(jnp.where(lane < 64, got * inside, 0.0))
    return out + [x_all, y_all]


def kernel(
    states_ref, previous_ref, potential_ref, screening_ref, occupation_ref, scale_ref, matrix_ref, ids_ref,
    filtered_ref, field_ref,
    pad, raw_matrix, ids, given_scale, occupied, table, padded_matrix, cell_matrix, scales,
    own, screen, vec, grid_ext, terms, part, faces,
    sent_x, sent_y, sent_z, sent_e, got_x, got_y, got_z, got_xr, got_yr, got_e, z_both,
    dens, dens_in, half, half_in, full_in, red_out, red_in, last_out, last_in, nat, nat_f, factors,
    in_sem, out_sem, halo_send, halo_recv, band_send, band_recv, red_send, red_recv, last_send, last_recv,
):
    dom, band = lax.axis_index("dom"), lax.axis_index("band")
    px, py, pz = lax.rem(dom, 4), lax.rem(lax.div(dom, 4), 4), lax.div(dom, 16)
    z_lo, core = lax.div(band, 2), lax.rem(band, 2)
    z_hi = lax.rem(py, 2)
    across = 2 * (ZLO - 1 - z_lo) + core

    def place(x, y, z):
        return x + 4 * y + 16 * z

    def near(step, mirrored):
        x = lax.rem(px + (step[0] + 4), 4)
        y = lax.rem(py + (step[1] + 4), 4)
        z = lax.rem(pz + (step[2] + 4), 4)
        return (place(x, y, z), across if mirrored and step[1] else band)

    partner = (dom, 2 * z_lo + (1 - core))

    def chip(z):
        return (dom, 2 * z + core)

    y_at = lax.div(dom, 8)
    group_one, group_two = [], []
    for e in range(1, 8):
        x = lax.rem(px + e % 4, 4)
        y = py + 1 - 2 * z_hi if e // 4 else py
        group_one.append((place(x, y, pz), across if e // 4 else band))
    for e in range(1, 8):
        group_two.append((lax.rem(dom, 8) + 8 * lax.rem(y_at + e, 8), band))

    served = [
        [(device, 2 * jnp.where(z_lo == 0, 1 + s, ZLO - 2 - s) + core) for device in [dom] + [d for d, _ in group_two]]
        for s in range(2)
    ]
    serving = 2 * jnp.where(z_lo < ZLO // 2, 0, ZLO - 1) + core

    is_end = (z_lo == 0) | (z_lo == ZLO - 1)
    def inside(step):
        tests = []
        for at, d in zip((px, py, pz), step):
            if d:
                tests.append(at < 3 if d > 0 else at > 0)
        found = tests[0]
        for test in tests[1:]:
            found = found & test
        return found

    for got in (got_x, got_y, got_z, got_xr, got_yr, got_e):
        got[...] = jnp.zeros_like(got)
    barrier = pltpu.get_barrier_semaphore()

    def greet(device):
        pl.semaphore_signal(barrier, inc=1, device_id=device, device_id_type=MESH)

    for step in AROUND:
        pl.when(inside(step))(lambda step=step: greet(near(step, False)))
    others = [partner] + [chip(lax.rem(z_lo + e, ZLO)) for e in range(1, ZLO)]
    for device in others:
        greet(device)

    @pl.when(is_end)
    def _():
        for step in AROUND:
            if step[1]:
                pl.when(inside(step))(lambda step=step: greet(near(step, True)))
        for device in group_one + group_two + served[0][1:] + served[1][1:]:
            greet(device)

    @pl.when(jnp.logical_not(is_end))
    def _():
        for device, _ in group_two:
            greet((device, serving))

    def along(at):
        return 1 + lax.div(at + 3, 4) + lax.div(6 - at, 4)

    level = along(px) * along(pz)
    at_end = lax.div(z_lo, ZLO - 1) + lax.div(ZLO - 1 - z_lo, ZLO - 1)
    n_greeted = level * along(py) - 1 + len(others) + len(group_two)
    n_greeted = n_greeted + at_end * (level * (along(py) - 1) + len(group_one) + 2 * len(group_two))

    loads = [
        pltpu.make_async_copy(states_ref.at[:, 0, :], pad.at[0, pl.ds(0, 108), :], in_sem.at[0]),
        pltpu.make_async_copy(previous_ref.at[:, 0, :], pad.at[1, pl.ds(0, 108), :], in_sem.at[1]),
        pltpu.make_async_copy(potential_ref, pad.at[2, pl.ds(0, 108), :], in_sem.at[2]),
        pltpu.make_async_copy(screening_ref, pad.at[3, pl.ds(0, 108), :], in_sem.at[3]),
        pltpu.make_async_copy(matrix_ref, raw_matrix, in_sem.at[4]),
        pltpu.make_async_copy(ids_ref.at[:, pl.ds(0, 128)], ids, in_sem.at[5]),
        pltpu.make_async_copy(scale_ref, given_scale, in_sem.at[6]),
        pltpu.make_async_copy(occupation_ref, occupied, in_sem.at[7]),
    ]
    for load in loads:
        load.start()

    def flag(test):
        return jnp.where(test, 1.0, 0.0).astype(F32)

    high = (flag(px < 3), flag(py < 3), flag(pz < 3))
    low = (flag(px > 0), flag(py > 0), flag(pz > 0))
    row, lane = iotas()

    table[...] = column_table()
    for m in range(4):
        pad[m, 108:144, :] = jnp.zeros((36, 128), F32)
    grid_ext[...] = jnp.zeros_like(grid_ext)
    sent_z[...] = jnp.zeros_like(sent_z)
    loads[0].wait()
    first = to_cells([pad[0, pl.ds(c, 8, stride=18), :] for c in range(18)], table[...])
    for g in range(36):
        own[8 * g : 8 * g + 8, :] = first[g]

    def tile_of(source):
        return lambda g: source[8 * g : 8 * g + 8, :]

    def copy_to(at, step, mirrored):
        x, y, z = step
        s, t = side(-x), side(-y)
        if x and y:
            src = sent_e.at[at, pl.ds(2 * side(x) + side(y), 1)]
            dst = got_e.at[at, 0 if z == 0 else 1 + side(-z), pl.ds(2 * s + t, 1)]
        elif x:
            src, dst = sent_x.at[at, side(x)], got_x.at[at, s]
            if z:
                src = src.at[pl.ds(6 if z > 0 else 0, 1)]
                dst = got_xr.at[at, pl.ds(2 * s + side(-z), 1)]
        elif y:
            src, dst = sent_y.at[at, side(y)], got_y.at[at, t]
            if z:
                src = src.at[pl.ds(6 if z > 0 else 0, 1)]
                dst = got_yr.at[at, pl.ds(2 * t + side(-z), 1)]
        else:
            src, dst = sent_z.at[at, side(z)], got_z.at[at, side(-z)]
        e = AROUND.index(step)
        return pltpu.make_async_remote_copy(
            src_ref=src,
            dst_ref=dst,
            send_sem=halo_send.at[at, e],
            recv_sem=halo_recv.at[at, e],
            device_id=near(step, mirrored),
            device_id_type=MESH,
        )

    def start_copies(at, steps, mirrored):
        made = [Guarded(copy_to(at, step, mirrored), inside(step), inside(back(step))) for step in steps]
        for copy in made:
            copy.start()
        return made

    _, lane_18 = iotas(18)

    def put_z(at, s, source, sublane):
        lower = source[pl.ds(sublane, 18, stride=8), :]
        upper = source[pl.ds(144 + sublane, 18, stride=8), :]
        sent_z[at, s, 0:18, :] = jnp.where(lane_18 < 64, lower, roll(upper, 64))

    def take_z(at, s):
        rows = got_z[at, s]
        z_both[s, 0] = rows
        z_both[s, 1] = roll(rows, 64)

    def z_row(s, m):
        if m >= 36:
            return z_both[s, 0, m - 18 : m - 17, :]
        return z_both[s, m // 18, m % 18 : m % 18 + 1, :]

    def products(source):
        tiles = extended(tile_of(source))
        for v in range(49):
            grid_ext[8 * v : 8 * v + 8, :] = tiles[v]
        terms[...] = cell_terms(grid_ext[...], cell_matrix[0], cell_matrix[1], scales[0:1, :])

    def cell_sums(source, factor, extra, first):
        products(source)
        first()
        folded, x_high, y_high = local_fold(lambda v: terms[8 * v : 8 * v + 8, :])
        for g in range(36):
            part[8 * g : 8 * g + 8, :] = factor * folded[g] + extra(g)
        faces[0], faces[1] = factor * x_high, factor * y_high

    def put_level(at, xs, x_high, y_high):
        for s in range(2):
            k = 6 if s == 0 else 0
            sent_x[at, s] = xs[s]
            put_z(at, s, part, k)
            sent_z[at, s, 18:19, :] = x_high[k : k + 1]
            sent_z[at, s, 19:20, :] = y_high[k : k + 1]

    def start_sums(at, source, factor, extra, mirrored, first=lambda: None):
        cell_sums(source, factor, extra, first)
        x_high, y_high = faces[0], faces[1]
        xs, ys, edges = shared(tile_of(part), x_high, y_high)
        put_level(at, xs, x_high, y_high)
        for s in range(2):
            sent_y[at, s] = ys[s]
        for c in range(4):
            sent_e[at, c : c + 1, :] = edges[c]
        return start_copies(at, AROUND, mirrored)

    def finish_sums(at, made):
        for copy in made:
            copy.wait_recv()
        take_z(at, 0)
        take_z(at, 1)
        return absorb(
            tile_of(part),
            faces[0],
            faces[1],
            [got_x[at, s] for s in range(2)],
            [[got_xr[at, 2 * s + t : 2 * s + t + 1, :] for t in range(2)] for s in range(2)],
            [got_y[at, s] for s in range(2)],
            [[got_yr[at, 2 * s + t : 2 * s + t + 1, :] for t in range(2)] for s in range(2)],
            [got_e[at, t] for t in range(3)],
            z_row,
            low,
            high,
        )

    x_tile, y_tile = low_faces(tile_of(own))
    sent_x[0, 1] = x_tile
    sent_y[0, 1] = y_tile
    sent_e[0, 3:4, :] = column_to_row(own[0:8, :], 0)
    put_z(0, 1, own, 0)

    pl.semaphore_wait(barrier, n_greeted)
    ghosts = start_copies(0, BELOW, False)

    for load in loads[1:]:
        load.wait()
    three = to_cells(
        [
            jnp.concatenate([pad[m, pl.ds(c, 8, stride=18), :] for m in (1, 2, 3)], axis=0)
            for c in range(18)
        ],
        table[...],
    )
    for g in range(36):
        rows = slice(8 * g, 8 * g + 8)
        screen[rows, :] = three[g][16:24]
        vec[0, rows, :] = FILTER_SCALE * ((three[g][8:16] - FILTER_CENTER) * own[rows, :]) - three[g][0:8]
    padded_matrix[...] = jnp.zeros_like(padded_matrix)
    padded_matrix[0:343, 0:343] = raw_matrix[...]
    by_row, by_column = node_rows(400), node_rows(512)
    for h, piece in enumerate(split(padded_matrix[...])):
        rows_moved = jnp.dot(by_row, piece, preferred_element_type=F32).astype(BF16)
        cell_matrix[h] = lax.dot_general(
            rows_moved, by_column, (((1,), (1,)), ((), ())), preferred_element_type=F32
        ).astype(BF16)
    _, lane_64 = iotas(64)
    first_id = 6 * 49 * ((lane_64 & 63) >> 3) + 6 * (lane_64 & 7)
    matches = jnp.where(first_id == jnp.broadcast_to(ids[:, 0:1], (64, 128)), 1.0, 0.0).astype(F32)
    given = jnp.broadcast_to(given_scale[...], (8, 64))
    scales[...] = jnp.dot(given, matches, precision=lax.Precision.HIGHEST, preferred_element_type=F32)

    for copy in ghosts:
        copy.wait_recv()
    take_z(0, 0)
    compact = from_above(
        tile_of(own),
        got_x[0, 0],
        got_xr[0, 0:1, :],
        got_y[0, 0],
        got_yr[0, 0:1, :],
        got_e[0, 0, 0:1, :],
        got_e[0, 1, 0:1, :],
        lambda g: z_row(0, g),
        high,
    )
    for m in range(TILES):
        vec[1, 8 * m : 8 * m + 8, :] = compact[m]
    summing = start_sums(1, vec.at[1], 0.5 * FILTER_SCALE, tile_of(vec.at[0]), False)
    values = finish_sums(1, summing)
    weight = occupied[...]
    squares = [weight * value * value for value in values]
    two_faces = squares[36] + roll(squares[37], 64)
    for m in range(18):
        tile = squares[m] + roll(squares[m + 18], 64)
        if m < 7:
            tile = jnp.where(row == 7, wide(two_faces[m : m + 1]), tile)
        dens[8 * m : 8 * m + 8, :] = tile

    mine = pl.multiple_of(72 * core, 8)
    other = pl.multiple_of(72 * (1 - core), 8)

    def band_copy(src, dst, at_send, at_recv, device):
        return pltpu.make_async_remote_copy(
            src_ref=src,
            dst_ref=dst,
            send_sem=band_send.at[at_send],
            recv_sem=band_recv.at[at_recv],
            device_id=device,
            device_id_type=MESH,
        )

    swap = band_copy(dens.at[pl.ds(other, 72), :], dens_in, 0, 0, partner)
    swap.start()
    for m in range(36):
        vec[0, 8 * m : 8 * m + 8, :] = values[m]
    swap.wait_recv()
    half[...] = dens[pl.ds(mine, 72), :] + dens_in[...]

    not_first, not_last = z_lo > 0, z_lo < ZLO - 1
    slot_first = jnp.maximum(z_lo - 1, 0)
    slot_last = jnp.minimum(z_lo, ZLO - 2)
    to_first = band_copy(half, half_in.at[slot_first], 1, 1 + slot_first, chip(0))
    to_last = band_copy(half, half_in.at[slot_last], 2, 1 + slot_last, chip(ZLO - 1))

    @pl.when(not_first)
    def _():
        to_first.start()

    @pl.when(not_last)
    def _():
        to_last.start()

    natural = from_cells([jnp.where(row < 6, vec[0, 8 * g : 8 * g + 8, :], 0.0) for g in range(36)], table[...])
    for c in range(18):
        nat_f[pl.ds(c, 8, stride=18), :] = natural[c]
    store = pltpu.make_async_copy(nat_f.at[pl.ds(0, 108), :], filtered_ref.at[:, 0, :], out_sem)
    store.start()

    B, W, Q, R1, W1 = 0, 1, 2, 3, 4

    def last_copy(at_send, e, device):
        return pltpu.make_async_remote_copy(
            src_ref=last_out,
            dst_ref=last_in.at[e],
            send_sem=last_send.at[at_send],
            recv_sem=last_recv.at[e],
            device_id=device,
            device_id_type=MESH,
        )

    def write_field(got, known):
        for e in range(1, 8):
            got = got + last_in[e]
        got = jnp.sum(got, axis=1, keepdims=True)
        c_b, c_w, c_q = combine(*[known[m : m + 1, 0:1] for m in range(3)], *[got[m : m + 1] for m in range(8)])
        field_ref[...] = c_b * nat[0, 0:108, :] + c_w * nat[1, 0:108, :] + c_q * nat[2, 0:108, :]

    @pl.when(is_end)
    def _():
        arrived = [band_copy(half, half_in.at[s], 1, 1 + s, partner) for s in range(ZLO - 1)]
        for copy in arrived:
            copy.wait_recv()
        total = half[...]
        for s in range(ZLO - 1):
            total = total + half_in[s]
        full_in[0] = total * (1.0 / STATES)
        again = band_copy(full_in.at[0], full_in.at[1], 3, 6, partner)
        again.start()
        again.wait_recv()
        both = (
            jnp.where(core == 0, full_in[0], full_in[1]),
            jnp.where(core == 0, full_in[1], full_in[0]),
        )
        two_faces = jnp.zeros((8, 128), F32)
        for m in range(18):
            tile = both[m // 9][8 * (m % 9) : 8 * (m % 9) + 8]
            if m < 7:
                two_faces = jnp.where(row == m, wide(tile[7:8]), two_faces)
            tile = jnp.where(row < 7, tile, 0.0)
            vec[B, 8 * m : 8 * m + 8, :] = jnp.where(lane < 64, tile, 0.0)
            vec[B, 8 * (m + 18) : 8 * (m + 18) + 8, :] = jnp.where(lane < 64, roll(tile, 64), 0.0)
        vec[B, 288:296, :] = jnp.where(lane < 64, two_faces, 0.0)
        vec[B, 296:304, :] = jnp.where(lane < 64, roll(two_faces, 64), 0.0)

        def put(v, tiles):
            for m in range(TILES):
                vec[v, 8 * m : 8 * m + 8, :] = tiles[m]

        def screened(v):
            return lambda g: screen[8 * g : 8 * g + 8, :] * vec[v, 8 * g : 8 * g + 8, :]

        def onto_row(got):
            got = jnp.sum(got.reshape(36, 8, 128), axis=0)
            return jnp.sum(jnp.where(row < 6, got, 0.0), axis=0, keepdims=True)

        def dot_row(a, b):
            return onto_row(vec[a, 0:CORE_ROWS, :] * vec[b, 0:CORE_ROWS, :])

        def send_reduce(n, level, devices):
            made = [
                pltpu.make_async_remote_copy(
                    src_ref=red_out.at[n, level],
                    dst_ref=red_in.at[n, level, e],
                    send_sem=red_send.at[n, level, e],
                    recv_sem=red_recv.at[n, level, e],
                    device_id=device,
                    device_id_type=MESH,
                )
                for e, device in enumerate(devices)
            ]
            for copy in made:
                copy.start()
            return made

        def start_reduce(n, rows):
            tile = jnp.zeros((8, 128), F32)
            for m, values in enumerate(rows):
                tile = jnp.where(row == m, wide(values), tile)
            red_out[n, 0] = tile
            return send_reduce(n, 0, group_one)

        def take(n, level, made):
            for copy in made:
                copy.wait_recv()
            got = red_out[n, level]
            for e in range(7):
                got = got + red_in[n, level, e]
            return got

        def second_level(n, made):
            red_out[n, 1] = take(n, 0, made)
            return send_reduce(n, 1, group_two)

        def scalars(n, made, count):
            got = jnp.sum(take(n, 1, made), axis=1, keepdims=True)
            return [got[m : m + 1] for m in range(count)]

        def hand_on(n, v):
            natural = from_cells(
                [jnp.where(row < 6, vec[v, 8 * g : 8 * g + 8, :], 0.0) for g in range(36)], table[...]
            )
            for c in range(18):
                nat[n, pl.ds(c, 8, stride=18), :] = natural[c]
            return onward(nat.at[n, 0:112], nat.at[n, 0:112], n)

        def onward(src, dst, n):
            made = [
                band_copy(src, dst, 4 + 2 * n + s, 7 + n, chip(jnp.where(z_lo == 0, 1 + s, ZLO - 2 - s)))
                for s in range(2)
            ]
            for copy in made:
                copy.start()
            return made

        def energy_row(v):
            cells = jnp.sum((grid_ext[0:392, :] * terms[0:392, :]).reshape(49, 8, 128), axis=0)
            cells = jnp.sum(jnp.where(lane < 64, cells, 0.0), axis=0, keepdims=True)
            owned = vec[v, 0:CORE_ROWS, :]
            return cells + onto_row(screen[...] * owned * owned)

        sent = [again]
        red_a = []
        made = start_sums(
            2,
            vec.at[B],
            1.0,
            screened(B),
            True,
            lambda: red_a.extend(start_reduce(0, [dot_row(B, B), energy_row(B)])),
        )
        sent += made + red_a + hand_on(0, B)
        red_b = second_level(0, red_a)
        put(W, finish_sums(2, made))
        made = start_sums(3, vec.at[W], 1.0, screened(W), True)
        sent += made + red_b + hand_on(1, W)
        put(Q, finish_sums(3, made))
        norm_0, image_0 = scalars(0, red_b, 2)
        alpha_0 = norm_0 / image_0
        factors[0] = jnp.where(row == 0, wide(alpha_0), jnp.where(row == 1, wide(norm_0), wide(image_0)))
        sent += onward(factors.at[0], factors.at[1], 3)

        vec[R1] = vec[B] - alpha_0 * vec[W]
        vec[W1] = vec[W] - alpha_0 * vec[Q]
        products(vec.at[W1])
        red_a = start_reduce(
            1,
            [
                dot_row(R1, R1),
                dot_row(R1, W1),
                dot_row(R1, W),
                dot_row(W1, W1),
                dot_row(W1, W),
                energy_row(W1),
                dot_row(W1, Q),
                dot_row(W, Q),
            ],
        )
        sent += hand_on(2, Q)
        last_out[...] = take(1, 0, red_a)
        last = [last_copy(e, e, device) for e, device in enumerate(group_two, 1)]
        for m in range(2):
            last += [last_copy(8 * (m + 1) + e, e, device) for e, device in enumerate(served[m])]
        for copy in last:
            copy.start()
        sent += red_a + last
        for copy in last[:7]:
            copy.wait_recv()
        write_field(last_out[...], factors[0])
        for copy in sent:
            copy.wait_send()

    @pl.when(jnp.logical_not(is_end))
    def _():
        for n in range(3):
            band_copy(nat.at[n, 0:112], nat.at[n, 0:112], 4, 7 + n, partner).wait_recv()
        band_copy(factors.at[0], factors.at[1], 4, 10, partner).wait_recv()
        for e in range(8):
            last_copy(e, e, partner).wait_recv()
        write_field(last_in[0], factors[1])

    swap.wait_send()

    @pl.when(not_first)
    def _():
        to_first.wait_send()

    @pl.when(not_last)
    def _():
        to_last.wait_send()

    for copy in ghosts + summing:
        copy.wait_send()
    store.wait()


def combine(alpha_0, norm_0, image_0, norm_1, rw, rv, ww, wv, waw, wav, vav):
    beta_1 = norm_1 / norm_0
    image_1 = rw + 2.0 * beta_1 * rv + beta_1 * beta_1 * image_0
    alpha_1 = norm_1 / image_1
    r_s = rw + beta_1 * rv
    s_s = ww + 2.0 * beta_1 * wv + beta_1 * beta_1 * (wv_self(alpha_0, wv, vav))
    r_as = ww + beta_1 * wv
    s_as = waw + 2.0 * beta_1 * wav + beta_1 * beta_1 * vav
    norm_2 = jnp.maximum(norm_1 - 2.0 * alpha_1 * r_s + alpha_1 * alpha_1 * s_s, 0.0)
    r2_ar2 = rw - 2.0 * alpha_1 * r_as + alpha_1 * alpha_1 * s_as
    r2_s = r_s - alpha_1 * s_s
    beta_2 = norm_2 / norm_1
    image_2 = r2_ar2 + 2.0 * beta_2 * r2_s + beta_2 * beta_2 * image_1
    alpha_2 = jnp.where(image_2 > 0.0, norm_2 / image_2, 0.0)
    grown = alpha_0 + alpha_1 * (1.0 + beta_1)
    c_b = grown + alpha_2 * (1.0 + beta_2 * (1.0 + beta_1))
    c_w = -alpha_1 * alpha_0 - alpha_2 * (grown + beta_2 * alpha_0)
    c_q = alpha_2 * alpha_1 * alpha_0
    return c_b, c_w, c_q


def wv_self(alpha_0, wv, vav):
    return wv + alpha_0 * vav


def pass_on(filtered_in, field_in, filtered_out, field_out, filtered_here, field_here, sem):
    pairs = ((field_in, field_here, field_out), (filtered_in, filtered_here, filtered_out))
    taken = [pltpu.make_async_copy(a, b, sem.at[m]) for m, (a, b, _) in enumerate(pairs)]
    given = [pltpu.make_async_copy(b, c, sem.at[2 + m]) for m, (_, b, c) in enumerate(pairs)]
    for copy in taken:
        copy.start()
    for one, two in zip(taken, given):
        one.wait()
        two.start()
    for copy in given:
        copy.wait()


def per_device(states, previous, potential, screening, occupation, cell_scale, cell_matrix, connectivity):
    vmem = pl.BlockSpec(memory_space=pltpu.VMEM)
    anywhere = pl.BlockSpec(memory_space=pl.ANY)
    filtered, field = pl.pallas_call(
        kernel,
        out_shape=(jax.ShapeDtypeStruct((108, 1, 128), F32), jax.ShapeDtypeStruct((108, 128), F32)),
        in_specs=[anywhere] * 8,
        out_specs=(anywhere, vmem),
        scratch_shapes=[
            pltpu.VMEM((4, 144, 128), F32),
            pltpu.VMEM((343, 343), F32),
            pltpu.VMEM((64, 128), jnp.int32),
            pltpu.VMEM((1, 64), F32),
            pltpu.VMEM((1, 1), F32),
            pltpu.VMEM((384, 384), BF16),
            pltpu.VMEM((384, 384), F32),
            pltpu.VMEM((2, 400, 512), BF16),
            pltpu.VMEM((8, 128), F32),
            pltpu.VMEM((288, 128), F32),
            pltpu.VMEM((288, 128), F32),
            pltpu.VMEM((5, ROWS, 128), F32),
            pltpu.VMEM((512, 128), F32),
            pltpu.VMEM((400, 128), F32),
            pltpu.VMEM((288, 128), F32),
            pltpu.VMEM((2, 8, 128), F32),
            pltpu.VMEM((4, 2, 8, 128), F32),
            pltpu.VMEM((4, 2, 8, 128), F32),
            pltpu.VMEM((4, 2, 24, 128), F32),
            pltpu.VMEM((4, 8, 128), F32),
            pltpu.VMEM((4, 2, 8, 128), F32),
            pltpu.VMEM((4, 2, 8, 128), F32),
            pltpu.VMEM((4, 2, 24, 128), F32),
            pltpu.VMEM((4, 8, 128), F32),
            pltpu.VMEM((4, 8, 128), F32),
            pltpu.VMEM((4, 3, 8, 128), F32),
            pltpu.VMEM((2, 2, 24, 128), F32),
            pltpu.VMEM((144, 128), F32),
            pltpu.VMEM((72, 128), F32),
            pltpu.VMEM((72, 128), F32),
            pltpu.VMEM((5, 72, 128), F32),
            pltpu.VMEM((2, 72, 128), F32),
            pltpu.VMEM((2, 2, 8, 128), F32),
            pltpu.VMEM((2, 2, 7, 8, 128), F32),
            pltpu.VMEM((8, 128), F32),
            pltpu.VMEM((8, 8, 128), F32),
            pltpu.VMEM((3, 144, 128), F32),
            pltpu.VMEM((144, 128), F32),
            pltpu.VMEM((2, 8, 128), F32),
            pltpu.SemaphoreType.DMA((8,)),
            pltpu.SemaphoreType.DMA,
            pltpu.SemaphoreType.DMA((4, 26)),
            pltpu.SemaphoreType.DMA((4, 26)),
            pltpu.SemaphoreType.DMA((12,)),
            pltpu.SemaphoreType.DMA((11,)),
            pltpu.SemaphoreType.DMA((2, 2, 7)),
            pltpu.SemaphoreType.DMA((2, 2, 7)),
            pltpu.SemaphoreType.DMA((24,)),
            pltpu.SemaphoreType.DMA((8,)),
        ],
        compiler_params=pltpu.CompilerParams(collective_id=0, has_side_effects=True),
        name="step",
    )(
        states.reshape(108, 1, 128),
        previous.reshape(108, 1, 128),
        potential.reshape(108, 128),
        screening.reshape(108, 128),
        occupation.reshape(1, 1),
        cell_scale.reshape(1, 64),
        cell_matrix,
        connectivity.T,
    )
    filtered, field = pl.pallas_call(
        pass_on,
        out_shape=(jax.ShapeDtypeStruct((108, 1, 128), F32), jax.ShapeDtypeStruct((108, 128), F32)),
        in_specs=[anywhere] * 2,
        out_specs=(anywhere, anywhere),
        scratch_shapes=[
            pltpu.VMEM((108, 1, 128), F32),
            pltpu.VMEM((108, 128), F32),
            pltpu.SemaphoreType.DMA((4,)),
        ],
        name="pass_on",
    )(filtered, field)
    return filtered.reshape(1, 13824), field.reshape(13824)


def solution(mesh):
    in_specs = (
        P("band", "dom"),
        P("band", "dom"),
        P("dom"),
        P("dom"),
        P("band"),
        P("dom"),
        P(),
        P(None, "dom"),
    )
    out_specs = (P("band", "dom"), P("dom"))
    return jax.shard_map(per_device, mesh=mesh, in_specs=in_specs, out_specs=out_specs, check_vma=False)
```

```python
import jax
import jax.numpy as jnp
from jax import lax
from jax.experimental import pallas as pl
from jax.experimental.pallas import tpu as pltpu
from jax.sharding import PartitionSpec as P

MESH = pl.DeviceIdType.MESH
F32 = jnp.float32
BF16 = jnp.bfloat16
STATES = 12
ZLO = 6
FILTER_CENTER = 2.0
FILTER_SCALE = 2.0 / 2.0


AROUND = [(x, y, z) for y in (1, -1, 0) for x in (1, -1, 0) for z in (1, -1, 0) if (x, y, z) != (0, 0, 0)]
BELOW = [d for d in AROUND if max(d) <= 0]
TILES = 38
CORE_ROWS = 288
ROWS = 8 * TILES


class Guarded:
    def __init__(self, copy, goes, comes):
        self.copy, self.goes, self.comes = copy, goes, comes

    def start(self):
        pl.when(self.goes)(self.copy.start)

    def wait_send(self):
        pl.when(self.goes)(self.copy.wait_send)

    def wait_recv(self):
        pl.when(self.comes)(self.copy.wait_recv)


def back(step):
    return tuple(-d for d in step)


def side(step):
    return 0 if step > 0 else 1

def roll(x, by, axis=1):
    by = by % x.shape[axis]
    return x if by == 0 else pltpu.roll(x, by, axis)


def iotas(rows=8, lanes=128):
    row = lax.broadcasted_iota(jnp.int32, (rows, lanes), 0)
    lane = lax.broadcasted_iota(jnp.int32, (rows, lanes), 1)
    return row, lane


def split(x):
    high = x.astype(BF16)
    return high, (x - high.astype(F32)).astype(BF16)


def column_table():
    row, lane = iotas(384, 384)
    g, cx = lane >> 3, lane & 7
    j = (g * 43) >> 8
    wanted = j * 48 + cx * 6 + (g - 6 * j)
    return jnp.where((row == wanted) & (lane < 288), 1.0, 0.0).astype(BF16)


def node_rows(rows):
    row, lane = iotas(rows, 384)
    k, v = row & 7, row >> 3
    return jnp.where((lane == 49 * k + v) & (k < 7) & (v < 49), 1.0, 0.0).astype(BF16)


def to_cells(tiles, table):
    n = tiles[0].shape[0]
    row, lane = iotas(n)
    group = lane >> 3
    chunks = []
    for cy in range(8):
        first, off = 288 * cy // 128, 288 * cy % 128
        parts = []
        for m in range(3):
            one = tiles[(first + m) % 18]
            if off:
                two = tiles[(first + m + 1) % 18]
                one = jnp.where(lane < 128 - off, roll(one, -off), roll(two, -off))
            parts.append(one)
        chunks.append(jnp.concatenate(parts, axis=1))
    stacked = jnp.concatenate(chunks, axis=0)
    high, low = split(stacked)
    both = jnp.dot(jnp.concatenate([high, low], axis=0), table, preferred_element_type=F32)
    moved = both[: 8 * n] + both[8 * n :]
    skewed = [
        [roll(moved[n * cy : n * cy + n, 128 * a : 128 * a + 128], 8 * cy) for a in range(3)]
        for cy in range(8)
    ]
    out = []
    for g in range(36):
        a, b = g // 16, g % 16
        got = jnp.where(group == b, skewed[0][a], 0.0)
        for cy in range(1, 8):
            got = jnp.where(group == (b + cy) % 16, skewed[cy][a], got)
        out.append(roll(got, -8 * b))
    return out


def split_exact(x):
    high, low = split(x)
    return high, low, (x - high.astype(F32) - low.astype(F32)).astype(BF16)


def from_cells(tiles, table):
    row, lane = iotas(8)
    group = lane >> 3
    placed = [roll(tiles[g], 8 * (g % 16)) for g in range(36)]
    rows = []
    for cy in range(8):
        parts = []
        for a in range(3):
            count = 16 if a < 2 else 4
            got = jnp.zeros((8, 128), F32)
            for b in range(count):
                got = jnp.where(group == (b + cy) % 16, placed[16 * a + b], got)
            parts.append(roll(got, -8 * cy))
        rows.append(jnp.concatenate(parts, axis=1))
    stacked = jnp.concatenate(rows, axis=0)
    both = lax.dot_general(
        jnp.concatenate(split_exact(stacked), axis=0), table, (((1,), (1,)), ((), ())), preferred_element_type=F32
    )
    moved = both[:64] + both[64:128] + both[128:]
    out = []
    for c in range(18):
        got = jnp.zeros((8, 128), F32)
        for cy in range(8):
            start = 288 * cy - 128 * c
            lo, hi = max(start, 0), min(start + 288, 128)
            if lo >= hi:
                continue
            off = start % 128
            for m in range(3):
                begin = start + 128 * m
                one_lo, one_hi = max(begin, lo), min(begin + 128, hi)
                if one_lo >= one_hi:
                    continue
                piece = roll(moved[8 * cy : 8 * cy + 8, 128 * m : 128 * m + 128], off)
                got = jnp.where((lane >= one_lo) & (lane < one_hi), piece, got)
        out.append(got)
    return out


def cell_terms(tiles, matrix_high, matrix_low, scale_row):
    high = tiles.astype(BF16).astype(F32)
    low = tiles - high
    _, lane = iotas(512)
    both = jnp.where(lane < 64, high, roll(low, 64)).astype(BF16)
    got = jnp.dot(matrix_high, both, preferred_element_type=F32)
    got = got + jnp.dot(matrix_low, both, preferred_element_type=F32)
    got = got + roll(got, 64)
    return got * scale_row


def local_fold(term):
    row, lane = iotas()
    cx, cy = lane & 7, lane >> 3
    upper_x = []
    for j in range(6):
        got = term(7 * j + 6)
        if j == 0:
            got = got + jnp.where(cy >= 1, roll(term(48), 8), 0.0)
        upper_x.append(got)
    x_tile = jnp.where(lane == 62, roll(term(48), -1), 0.0)
    for j in range(6):
        x_tile = jnp.where((cx == j) & (cy < 8), roll(upper_x[j], j - 7), x_tile)
    y_tile = jnp.zeros((8, 128), F32)
    for i in range(6):
        got = term(42 + i)
        if i == 0:
            got = got + jnp.where(cx >= 1, roll(term(48), 1), 0.0)
        y_tile = jnp.where(cy == i, roll(got, 8 * i - 56), y_tile)
    out = []
    for g in range(36):
        j, i = g // 6, g % 6
        got = term(7 * j + i)
        if j == 0:
            got = got + jnp.where(cy >= 1, roll(term(42 + i), 8), 0.0)
        if i == 0:
            got = got + jnp.where(cx >= 1, roll(upper_x[j], 1), 0.0)
        out.append(got)
    return out, x_tile, y_tile


def column_to_row(tile, at):
    row, lane = iotas()
    return jnp.sum(jnp.where(row == lane, jnp.broadcast_to(tile[:, at : at + 1], (8, 128)), 0.0), axis=0, keepdims=True)


def row_to_column(values):
    row, lane = iotas()
    return jnp.sum(jnp.where(row == lane, jnp.broadcast_to(values, (8, 128)), 0.0), axis=1, keepdims=True)


def wide(values):
    return jnp.broadcast_to(values, (8, 128))


def low_faces(field):
    row, lane = iotas()
    cx, cy = lane & 7, lane >> 3
    x_tile = jnp.zeros((8, 128), F32)
    y_tile = jnp.zeros((8, 128), F32)
    for j in range(6):
        x_tile = jnp.where((cx == j) & (cy < 8), roll(field(6 * j), j), x_tile)
    for i in range(6):
        y_tile = jnp.where(cy == i, roll(field(i), 8 * i), y_tile)
    return x_tile, y_tile


def from_above(field, x_tile, x_row, y_tile, y_row, edge, corner, z_row, high):
    row, lane = iotas()
    hx, hy, hz = high
    line = jnp.where(lane[0:1] == 6, roll(corner * hz, 6), edge)
    x_all = jnp.where(row == 6, wide(x_row * hz), x_tile)
    x_all = hx * jnp.where(lane == 62, wide(row_to_column(line) * hy), x_all)
    y_all = hy * jnp.where(row == 6, wide(y_row * hz), y_tile)
    core = [jnp.where(row == 6, wide(z_row(g) * hz), field(g)) for g in range(36)]
    return core + [x_all, y_all]


def extended(field):
    row, lane = iotas()
    cx, cy = lane & 7, lane >> 3
    x_all, y_all = field(36), field(37)
    out = [None] * 49
    for g in range(36):
        out[7 * (g // 6) + g % 6] = field(g)
    for j in range(6):
        out[7 * j + 6] = jnp.where(cx == 7, roll(x_all, 7 - j), roll(field(6 * j), -1))
    for i in range(6):
        out[42 + i] = jnp.where(cy == 7, roll(y_all, 56 - 8 * i), roll(field(i), -8))
    corner = jnp.where(cx == 7, roll(x_all, -1), roll(field(0), -9))
    corner = jnp.where(cy == 7, roll(y_all, 55), corner)
    out[48] = jnp.where(lane == 63, roll(x_all, 1), corner)
    return out


def shared(part, x_high, y_high):
    row, lane = iotas()
    x_low, y_low = low_faces(part)
    x_low = jnp.where(lane == 62, roll(y_high, 62), x_low)
    y_out = jnp.where(lane == 55, roll(x_high, -7), y_high)
    y_low = jnp.where(lane == 55, roll(x_high, 55), y_low)
    edges = [column_to_row(t, at) for t in (x_high, x_low) for at in (62, 0)]
    return (x_high, x_low), (y_out, y_low), edges


def absorb(part, x_high, y_high, xs, x_rows, ys, y_rows, edges, z_row, low, high):
    row, lane = iotas()
    cx, cy = lane & 7, lane >> 3
    hx, hy, hz = high
    lx, ly, lz = low

    def with_rows(tile, rows):
        return tile + jnp.where(row == 6, wide(rows[0]), jnp.where(row == 0, wide(rows[1] * lz), 0.0))

    x_up, x_down = with_rows(xs[0], x_rows[0]), with_rows(xs[1], x_rows[1]) * lx
    y_up, y_down = with_rows(ys[0], y_rows[0]), with_rows(ys[1], y_rows[1]) * ly
    lines = edges[0] + jnp.where(lane == 6, roll(edges[1], 6), jnp.where(lane == 0, roll(edges[2] * lz, -6), 0.0))
    columns = [wide(row_to_column(lines[c : c + 1])) for c in range(4)]
    up_row, down_row = row == 6, row == 0

    def vertical(up, down):
        return jnp.where(up_row, wide(up), jnp.where(down_row, wide(down * lz), 0.0))

    x_all = x_high + x_up + vertical(z_row(0, 36), z_row(1, 36))
    x_all = x_all + jnp.where(lane == 62, roll(y_up, 7) + columns[0], 0.0)
    x_all = x_all + jnp.where(lane == 0, roll(y_down, -55) + columns[1] * ly, 0.0)
    y_all = y_high + jnp.where(cy < 6, y_up, 0.0) + vertical(z_row(0, 37), z_row(1, 37))
    y_all = y_all + jnp.where(lane == 0, roll(x_down, -62) + columns[2] * lx, 0.0)
    top = jnp.where(up_row, hz, 1.0)
    x_all = x_all * (top * hx) * jnp.where(lane == 62, hy, 1.0)
    y_all = y_all * (top * hy)
    inside = jnp.where(lane < 64, top, 0.0)
    out = []
    for g in range(36):
        j, i = g // 6, g % 6
        got = part(g) + vertical(z_row(0, g), z_row(1, g))
        if i == 0:
            got = got + jnp.where((cx == 0) & (cy < 8), roll(x_down, -j), 0.0)
        if j == 0:
            got = got + jnp.where(cy == 0, roll(y_down, -8 * i), 0.0)
        if g == 0:
            got = got + jnp.where(lane == 0, columns[3] * (lx * ly), 0.0)
        out.append(jnp.where(lane < 64, got * inside, 0.0))
    return out + [x_all, y_all]


def kernel(
    states_ref, previous_ref, potential_ref, screening_ref, occupation_ref, scale_ref, matrix_ref, ids_ref,
    filtered_ref, field_ref,
    pad, raw_matrix, ids, given_scale, occupied, table, padded_matrix, cell_matrix, scales,
    own, screen, vec, grid_ext, terms, part, faces,
    sent_x, sent_y, sent_z, sent_e, got_x, got_y, got_z, got_xr, got_yr, got_e, z_both,
    dens, dens_in, half, half_in, full_in, red_out, red_in, last_out, last_in, nat, nat_f, factors,
    in_sem, out_sem, halo_send, halo_recv, band_send, band_recv, red_send, red_recv, last_send, last_recv,
):
    dom, band = lax.axis_index("dom"), lax.axis_index("band")
    px, py, pz = lax.rem(dom, 4), lax.rem(lax.div(dom, 4), 4), lax.div(dom, 16)
    z_lo, core = lax.div(band, 2), lax.rem(band, 2)
    z_hi = lax.rem(py, 2)
    across = 2 * (ZLO - 1 - z_lo) + core

    def place(x, y, z):
        return x + 4 * y + 16 * z

    def near(step, mirrored):
        x = lax.rem(px + (step[0] + 4), 4)
        y = lax.rem(py + (step[1] + 4), 4)
        z = lax.rem(pz + (step[2] + 4), 4)
        return (place(x, y, z), across if mirrored and step[1] else band)

    partner = (dom, 2 * z_lo + (1 - core))

    def chip(z):
        return (dom, 2 * z + core)

    y_at = lax.div(dom, 8)
    group_one, group_two = [], []
    for e in range(1, 8):
        x = lax.rem(px + e % 4, 4)
        y = py + 1 - 2 * z_hi if e // 4 else py
        group_one.append((place(x, y, pz), across if e // 4 else band))
    for e in range(1, 8):
        group_two.append((lax.rem(dom, 8) + 8 * lax.rem(y_at + e, 8), band))

    served = [
        [(device, 2 * jnp.where(z_lo == 0, 1 + s, ZLO - 2 - s) + core) for device in [dom] + [d for d, _ in group_two]]
        for s in range(2)
    ]
    serving = 2 * jnp.where(z_lo < ZLO // 2, 0, ZLO - 1) + core

    is_end = (z_lo == 0) | (z_lo == ZLO - 1)
    def inside(step):
        tests = []
        for at, d in zip((px, py, pz), step):
            if d:
                tests.append(at < 3 if d > 0 else at > 0)
        found = tests[0]
        for test in tests[1:]:
            found = found & test
        return found

    for got in (got_x, got_y, got_z, got_xr, got_yr, got_e):
        got[...] = jnp.zeros_like(got)
    barrier = pltpu.get_barrier_semaphore()

    def greet(device):
        pl.semaphore_signal(barrier, inc=1, device_id=device, device_id_type=MESH)

    for step in AROUND:
        pl.when(inside(step))(lambda step=step: greet(near(step, False)))
    others = [partner] + [chip(lax.rem(z_lo + e, ZLO)) for e in range(1, ZLO)]
    for device in others:
        greet(device)

    @pl.when(is_end)
    def _():
        for step in AROUND:
            if step[1]:
                pl.when(inside(step))(lambda step=step: greet(near(step, True)))
        for device in group_one + group_two + served[0][1:] + served[1][1:]:
            greet(device)

    @pl.when(jnp.logical_not(is_end))
    def _():
        for device, _ in group_two:
            greet((device, serving))

    def along(at):
        return 1 + lax.div(at + 3, 4) + lax.div(6 - at, 4)

    level = along(px) * along(pz)
    at_end = lax.div(z_lo, ZLO - 1) + lax.div(ZLO - 1 - z_lo, ZLO - 1)
    n_greeted = level * along(py) - 1 + len(others) + len(group_two)
    n_greeted = n_greeted + at_end * (level * (along(py) - 1) + len(group_one) + 2 * len(group_two))

    loads = [
        pltpu.make_async_copy(states_ref.at[:, 0, :], pad.at[0, pl.ds(0, 108), :], in_sem.at[0]),
        pltpu.make_async_copy(previous_ref.at[:, 0, :], pad.at[1, pl.ds(0, 108), :], in_sem.at[1]),
        pltpu.make_async_copy(potential_ref, pad.at[2, pl.ds(0, 108), :], in_sem.at[2]),
        pltpu.make_async_copy(screening_ref, pad.at[3, pl.ds(0, 108), :], in_sem.at[3]),
        pltpu.make_async_copy(matrix_ref, raw_matrix, in_sem.at[4]),
        pltpu.make_async_copy(ids_ref.at[:, pl.ds(0, 128)], ids, in_sem.at[5]),
        pltpu.make_async_copy(scale_ref, given_scale, in_sem.at[6]),
        pltpu.make_async_copy(occupation_ref, occupied, in_sem.at[7]),
    ]
    for load in loads:
        load.start()

    def flag(test):
        return jnp.where(test, 1.0, 0.0).astype(F32)

    high = (flag(px < 3), flag(py < 3), flag(pz < 3))
    low = (flag(px > 0), flag(py > 0), flag(pz > 0))
    row, lane = iotas()

    table[...] = column_table()
    for m in range(4):
        pad[m, 108:144, :] = jnp.zeros((36, 128), F32)
    grid_ext[...] = jnp.zeros_like(grid_ext)
    sent_z[...] = jnp.zeros_like(sent_z)
    loads[0].wait()
    first = to_cells([pad[0, pl.ds(c, 8, stride=18), :] for c in range(18)], table[...])
    for g in range(36):
        own[8 * g : 8 * g + 8, :] = first[g]

    def tile_of(source):
        return lambda g: source[8 * g : 8 * g + 8, :]

    def copy_to(at, step, mirrored):
        x, y, z = step
        s, t = side(-x), side(-y)
        if x and y:
            src = sent_e.at[at, pl.ds(2 * side(x) + side(y), 1)]
            dst = got_e.at[at, 0 if z == 0 else 1 + side(-z), pl.ds(2 * s + t, 1)]
        elif x:
            src, dst = sent_x.at[at, side(x)], got_x.at[at, s]
            if z:
                src = src.at[pl.ds(6 if z > 0 else 0, 1)]
                dst = got_xr.at[at, pl.ds(2 * s + side(-z), 1)]
        elif y:
            src, dst = sent_y.at[at, side(y)], got_y.at[at, t]
            if z:
                src = src.at[pl.ds(6 if z > 0 else 0, 1)]
                dst = got_yr.at[at, pl.ds(2 * t + side(-z), 1)]
        else:
            src, dst = sent_z.at[at, side(z)], got_z.at[at, side(-z)]
        e = AROUND.index(step)
        return pltpu.make_async_remote_copy(
            src_ref=src,
            dst_ref=dst,
            send_sem=halo_send.at[at, e],
            recv_sem=halo_recv.at[at, e],
            device_id=near(step, mirrored),
            device_id_type=MESH,
        )

    def start_copies(at, steps, mirrored):
        made = [Guarded(copy_to(at, step, mirrored), inside(step), inside(back(step))) for step in steps]
        for copy in made:
            copy.start()
        return made

    _, lane_18 = iotas(18)

    def put_z(at, s, source, sublane):
        lower = source[pl.ds(sublane, 18, stride=8), :]
        upper = source[pl.ds(144 + sublane, 18, stride=8), :]
        sent_z[at, s, 0:18, :] = jnp.where(lane_18 < 64, lower, roll(upper, 64))

    def take_z(at, s):
        rows = got_z[at, s]
        z_both[s, 0] = rows
        z_both[s, 1] = roll(rows, 64)

    def z_row(s, m):
        if m >= 36:
            return z_both[s, 0, m - 18 : m - 17, :]
        return z_both[s, m // 18, m % 18 : m % 18 + 1, :]

    def products(source):
        tiles = extended(tile_of(source))
        for v in range(49):
            grid_ext[8 * v : 8 * v + 8, :] = tiles[v]
        terms[...] = cell_terms(grid_ext[...], cell_matrix[0], cell_matrix[1], scales[0:1, :])

    def cell_sums(source, factor, extra, first):
        products(source)
        first()
        folded, x_high, y_high = local_fold(lambda v: terms[8 * v : 8 * v + 8, :])
        for g in range(36):
            part[8 * g : 8 * g + 8, :] = factor * folded[g] + extra(g)
        faces[0], faces[1] = factor * x_high, factor * y_high

    def put_level(at, xs, x_high, y_high):
        for s in range(2):
            k = 6 if s == 0 else 0
            sent_x[at, s] = xs[s]
            put_z(at, s, part, k)
            sent_z[at, s, 18:19, :] = x_high[k : k + 1]
            sent_z[at, s, 19:20, :] = y_high[k : k + 1]

    def start_sums(at, source, factor, extra, mirrored, first=lambda: None):
        cell_sums(source, factor, extra, first)
        x_high, y_high = faces[0], faces[1]
        xs, ys, edges = shared(tile_of(part), x_high, y_high)
        put_level(at, xs, x_high, y_high)
        for s in range(2):
            sent_y[at, s] = ys[s]
        for c in range(4):
            sent_e[at, c : c + 1, :] = edges[c]
        return start_copies(at, AROUND, mirrored)

    def finish_sums(at, made):
        for copy in made:
            copy.wait_recv()
        take_z(at, 0)
        take_z(at, 1)
        return absorb(
            tile_of(part),
            faces[0],
            faces[1],
            [got_x[at, s] for s in range(2)],
            [[got_xr[at, 2 * s + t : 2 * s + t + 1, :] for t in range(2)] for s in range(2)],
            [got_y[at, s] for s in range(2)],
            [[got_yr[at, 2 * s + t : 2 * s + t + 1, :] for t in range(2)] for s in range(2)],
            [got_e[at, t] for t in range(3)],
            z_row,
            low,
            high,
        )

    x_tile, y_tile = low_faces(tile_of(own))
    sent_x[0, 1] = x_tile
    sent_y[0, 1] = y_tile
    sent_e[0, 3:4, :] = column_to_row(own[0:8, :], 0)
    put_z(0, 1, own, 0)

    pl.semaphore_wait(barrier, n_greeted)
    ghosts = start_copies(0, BELOW, False)

    for load in loads[1:]:
        load.wait()
    three = to_cells(
        [
            jnp.concatenate([pad[m, pl.ds(c, 8, stride=18), :] for m in (1, 2, 3)], axis=0)
            for c in range(18)
        ],
        table[...],
    )
    for g in range(36):
        rows = slice(8 * g, 8 * g + 8)
        screen[rows, :] = three[g][16:24]
        vec[0, rows, :] = FILTER_SCALE * ((three[g][8:16] - FILTER_CENTER) * own[rows, :]) - three[g][0:8]
    padded_matrix[...] = jnp.zeros_like(padded_matrix)
    padded_matrix[0:343, 0:343] = raw_matrix[...]
    by_row, by_column = node_rows(400), node_rows(512)
    for h, piece in enumerate(split(padded_matrix[...])):
        rows_moved = jnp.dot(by_row, piece, preferred_element_type=F32).astype(BF16)
        cell_matrix[h] = lax.dot_general(
            rows_moved, by_column, (((1,), (1,)), ((), ())), preferred_element_type=F32
        ).astype(BF16)
    _, lane_64 = iotas(64)
    first_id = 6 * 49 * ((lane_64 & 63) >> 3) + 6 * (lane_64 & 7)
    matches = jnp.where(first_id == jnp.broadcast_to(ids[:, 0:1], (64, 128)), 1.0, 0.0).astype(F32)
    given = jnp.broadcast_to(given_scale[...], (8, 64))
    scales[...] = jnp.dot(given, matches, precision=lax.Precision.HIGHEST, preferred_element_type=F32)

    for copy in ghosts:
        copy.wait_recv()
    take_z(0, 0)
    compact = from_above(
        tile_of(own),
        got_x[0, 0],
        got_xr[0, 0:1, :],
        got_y[0, 0],
        got_yr[0, 0:1, :],
        got_e[0, 0, 0:1, :],
        got_e[0, 1, 0:1, :],
        lambda g: z_row(0, g),
        high,
    )
    for m in range(TILES):
        vec[1, 8 * m : 8 * m + 8, :] = compact[m]
    summing = start_sums(1, vec.at[1], 0.5 * FILTER_SCALE, tile_of(vec.at[0]), False)
    values = finish_sums(1, summing)
    weight = occupied[...]
    squares = [weight * value * value for value in values]
    two_faces = squares[36] + roll(squares[37], 64)
    for m in range(18):
        tile = squares[m] + roll(squares[m + 18], 64)
        if m < 7:
            tile = jnp.where(row == 7, wide(two_faces[m : m + 1]), tile)
        dens[8 * m : 8 * m + 8, :] = tile

    mine = pl.multiple_of(72 * core, 8)
    other = pl.multiple_of(72 * (1 - core), 8)

    def band_copy(src, dst, at_send, at_recv, device):
        return pltpu.make_async_remote_copy(
            src_ref=src,
            dst_ref=dst,
            send_sem=band_send.at[at_send],
            recv_sem=band_recv.at[at_recv],
            device_id=device,
            device_id_type=MESH,
        )

    swap = band_copy(dens.at[pl.ds(other, 72), :], dens_in, 0, 0, partner)
    swap.start()
    for m in range(36):
        vec[0, 8 * m : 8 * m + 8, :] = values[m]
    swap.wait_recv()
    half[...] = dens[pl.ds(mine, 72), :] + dens_in[...]

    not_first, not_last = z_lo > 0, z_lo < ZLO - 1
    slot_first = jnp.maximum(z_lo - 1, 0)
    slot_last = jnp.minimum(z_lo, ZLO - 2)
    to_first = band_copy(half, half_in.at[slot_first], 1, 1 + slot_first, chip(0))
    to_last = band_copy(half, half_in.at[slot_last], 2, 1 + slot_last, chip(ZLO - 1))

    @pl.when(not_first)
    def _():
        to_first.start()

    @pl.when(not_last)
    def _():
        to_last.start()

    natural = from_cells([jnp.where(row < 6, vec[0, 8 * g : 8 * g + 8, :], 0.0) for g in range(36)], table[...])
    for c in range(18):
        nat_f[pl.ds(c, 8, stride=18), :] = natural[c]
    store = pltpu.make_async_copy(nat_f.at[pl.ds(0, 108), :], filtered_ref.at[:, 0, :], out_sem)
    store.start()

    B, W, Q, R1, W1 = 0, 1, 2, 3, 4

    def last_copy(at_send, e, device):
        return pltpu.make_async_remote_copy(
            src_ref=last_out,
            dst_ref=last_in.at[e],
            send_sem=last_send.at[at_send],
            recv_sem=last_recv.at[e],
            device_id=device,
            device_id_type=MESH,
        )

    def write_field(got, known):
        for e in range(1, 8):
            got = got + last_in[e]
        got = jnp.sum(got, axis=1, keepdims=True)
        c_b, c_w, c_q = combine(*[known[m : m + 1, 0:1] for m in range(3)], *[got[m : m + 1] for m in range(8)])
        field_ref[...] = c_b * nat[0, 0:108, :] + c_w * nat[1, 0:108, :] + c_q * nat[2, 0:108, :]

    @pl.when(is_end)
    def _():
        arrived = [band_copy(half, half_in.at[s], 1, 1 + s, partner) for s in range(ZLO - 1)]
        for copy in arrived:
            copy.wait_recv()
        total = half[...]
        for s in range(ZLO - 1):
            total = total + half_in[s]
        full_in[0] = total * (1.0 / STATES)
        again = band_copy(full_in.at[0], full_in.at[1], 3, 6, partner)
        again.start()
        again.wait_recv()
        both = (
            jnp.where(core == 0, full_in[0], full_in[1]),
            jnp.where(core == 0, full_in[1], full_in[0]),
        )
        two_faces = jnp.zeros((8, 128), F32)
        for m in range(18):
            tile = both[m // 9][8 * (m % 9) : 8 * (m % 9) + 8]
            if m < 7:
                two_faces = jnp.where(row == m, wide(tile[7:8]), two_faces)
            tile = jnp.where(row < 7, tile, 0.0)
            vec[B, 8 * m : 8 * m + 8, :] = jnp.where(lane < 64, tile, 0.0)
            vec[B, 8 * (m + 18) : 8 * (m + 18) + 8, :] = jnp.where(lane < 64, roll(tile, 64), 0.0)
        vec[B, 288:296, :] = jnp.where(lane < 64, two_faces, 0.0)
        vec[B, 296:304, :] = jnp.where(lane < 64, roll(two_faces, 64), 0.0)

        def put(v, tiles):
            for m in range(TILES):
                vec[v, 8 * m : 8 * m + 8, :] = tiles[m]

        def screened(v):
            return lambda g: screen[8 * g : 8 * g + 8, :] * vec[v, 8 * g : 8 * g + 8, :]

        def onto_row(got):
            got = jnp.sum(got.reshape(36, 8, 128), axis=0)
            return jnp.sum(jnp.where(row < 6, got, 0.0), axis=0, keepdims=True)

        def dot_row(a, b):
            return onto_row(vec[a, 0:CORE_ROWS, :] * vec[b, 0:CORE_ROWS, :])

        def send_reduce(n, level, devices):
            made = [
                pltpu.make_async_remote_copy(
                    src_ref=red_out.at[n, level],
                    dst_ref=red_in.at[n, level, e],
                    send_sem=red_send.at[n, level, e],
                    recv_sem=red_recv.at[n, level, e],
                    device_id=device,
                    device_id_type=MESH,
                )
                for e, device in enumerate(devices)
            ]
            for copy in made:
                copy.start()
            return made

        def start_reduce(n, rows):
            tile = jnp.zeros((8, 128), F32)
            for m, values in enumerate(rows):
                tile = jnp.where(row == m, wide(values), tile)
            red_out[n, 0] = tile
            return send_reduce(n, 0, group_one)

        def take(n, level, made):
            for copy in made:
                copy.wait_recv()
            got = red_out[n, level]
            for e in range(7):
                got = got + red_in[n, level, e]
            return got

        def second_level(n, made):
            red_out[n, 1] = take(n, 0, made)
            return send_reduce(n, 1, group_two)

        def scalars(n, made, count):
            got = jnp.sum(take(n, 1, made), axis=1, keepdims=True)
            return [got[m : m + 1] for m in range(count)]

        def hand_on(n, v):
            natural = from_cells(
                [jnp.where(row < 6, vec[v, 8 * g : 8 * g + 8, :], 0.0) for g in range(36)], table[...]
            )
            for c in range(18):
                nat[n, pl.ds(c, 8, stride=18), :] = natural[c]
            return onward(nat.at[n, 0:112], nat.at[n, 0:112], n)

        def onward(src, dst, n):
            made = [
                band_copy(src, dst, 4 + 2 * n + s, 7 + n, chip(jnp.where(z_lo == 0, 1 + s, ZLO - 2 - s)))
                for s in range(2)
            ]
            for copy in made:
                copy.start()
            return made

        def energy_row(v):
            cells = jnp.sum((grid_ext[0:392, :] * terms[0:392, :]).reshape(49, 8, 128), axis=0)
            cells = jnp.sum(jnp.where(lane < 64, cells, 0.0), axis=0, keepdims=True)
            owned = vec[v, 0:CORE_ROWS, :]
            return cells + onto_row(screen[...] * owned * owned)

        sent = [again]
        red_a = []
        made = start_sums(
            2,
            vec.at[B],
            1.0,
            screened(B),
            True,
            lambda: red_a.extend(start_reduce(0, [dot_row(B, B), energy_row(B)])),
        )
        sent += made + red_a + hand_on(0, B)
        red_b = second_level(0, red_a)
        put(W, finish_sums(2, made))
        made = start_sums(3, vec.at[W], 1.0, screened(W), True)
        sent += made + red_b + hand_on(1, W)
        put(Q, finish_sums(3, made))
        norm_0, image_0 = scalars(0, red_b, 2)
        alpha_0 = norm_0 / image_0
        factors[0] = jnp.where(row == 0, wide(alpha_0), jnp.where(row == 1, wide(norm_0), wide(image_0)))
        sent += onward(factors.at[0], factors.at[1], 3)

        vec[R1] = vec[B] - alpha_0 * vec[W]
        vec[W1] = vec[W] - alpha_0 * vec[Q]
        products(vec.at[W1])
        red_a = start_reduce(
            1,
            [
                dot_row(R1, R1),
                dot_row(R1, W1),
                dot_row(R1, W),
                dot_row(W1, W1),
                dot_row(W1, W),
                energy_row(W1),
                dot_row(W1, Q),
                dot_row(W, Q),
            ],
        )
        sent += hand_on(2, Q)
        last_out[...] = take(1, 0, red_a)
        last = [last_copy(e, e, device) for e, device in enumerate(group_two, 1)]
        for m in range(2):
            last += [last_copy(8 * (m + 1) + e, e, device) for e, device in enumerate(served[m])]
        for copy in last:
            copy.start()
        sent += red_a + last
        for copy in last[:7]:
            copy.wait_recv()
        write_field(last_out[...], factors[0])
        for copy in sent:
            copy.wait_send()

    @pl.when(jnp.logical_not(is_end))
    def _():
        for n in range(3):
            band_copy(nat.at[n, 0:112], nat.at[n, 0:112], 4, 7 + n, partner).wait_recv()
        band_copy(factors.at[0], factors.at[1], 4, 10, partner).wait_recv()
        for e in range(8):
            last_copy(e, e, partner).wait_recv()
        write_field(last_in[0], factors[1])

    swap.wait_send()

    @pl.when(not_first)
    def _():
        to_first.wait_send()

    @pl.when(not_last)
    def _():
        to_last.wait_send()

    for copy in ghosts + summing:
        copy.wait_send()
    store.wait()


def combine(alpha_0, norm_0, image_0, norm_1, rw, rv, ww, wv, waw, wav, vav):
    beta_1 = norm_1 / norm_0
    image_1 = rw + 2.0 * beta_1 * rv + beta_1 * beta_1 * image_0
    alpha_1 = norm_1 / image_1
    r_s = rw + beta_1 * rv
    s_s = ww + 2.0 * beta_1 * wv + beta_1 * beta_1 * (wv_self(alpha_0, wv, vav))
    r_as = ww + beta_1 * wv
    s_as = waw + 2.0 * beta_1 * wav + beta_1 * beta_1 * vav
    norm_2 = jnp.maximum(norm_1 - 2.0 * alpha_1 * r_s + alpha_1 * alpha_1 * s_s, 0.0)
    r2_ar2 = rw - 2.0 * alpha_1 * r_as + alpha_1 * alpha_1 * s_as
    r2_s = r_s - alpha_1 * s_s
    beta_2 = norm_2 / norm_1
    image_2 = r2_ar2 + 2.0 * beta_2 * r2_s + beta_2 * beta_2 * image_1
    alpha_2 = jnp.where(image_2 > 0.0, norm_2 / image_2, 0.0)
    grown = alpha_0 + alpha_1 * (1.0 + beta_1)
    c_b = grown + alpha_2 * (1.0 + beta_2 * (1.0 + beta_1))
    c_w = -alpha_1 * alpha_0 - alpha_2 * (grown + beta_2 * alpha_0)
    c_q = alpha_2 * alpha_1 * alpha_0
    return c_b, c_w, c_q


def wv_self(alpha_0, wv, vav):
    return wv + alpha_0 * vav


def per_device(states, previous, potential, screening, occupation, cell_scale, cell_matrix, connectivity):
    vmem = pl.BlockSpec(memory_space=pltpu.VMEM)
    anywhere = pl.BlockSpec(memory_space=pl.ANY)
    filtered, field = pl.pallas_call(
        kernel,
        out_shape=(pltpu.VMEM((108, 1, 128), F32), pltpu.VMEM((108, 128), F32)),
        in_specs=[anywhere] * 8,
        out_specs=(vmem, vmem),
        scratch_shapes=[
            pltpu.VMEM((4, 144, 128), F32),
            pltpu.VMEM((343, 343), F32),
            pltpu.VMEM((64, 128), jnp.int32),
            pltpu.VMEM((1, 64), F32),
            pltpu.VMEM((1, 1), F32),
            pltpu.VMEM((384, 384), BF16),
            pltpu.VMEM((384, 384), F32),
            pltpu.VMEM((2, 400, 512), BF16),
            pltpu.VMEM((8, 128), F32),
            pltpu.VMEM((288, 128), F32),
            pltpu.VMEM((288, 128), F32),
            pltpu.VMEM((5, ROWS, 128), F32),
            pltpu.VMEM((512, 128), F32),
            pltpu.VMEM((400, 128), F32),
            pltpu.VMEM((288, 128), F32),
            pltpu.VMEM((2, 8, 128), F32),
            pltpu.VMEM((4, 2, 8, 128), F32),
            pltpu.VMEM((4, 2, 8, 128), F32),
            pltpu.VMEM((4, 2, 24, 128), F32),
            pltpu.VMEM((4, 8, 128), F32),
            pltpu.VMEM((4, 2, 8, 128), F32),
            pltpu.VMEM((4, 2, 8, 128), F32),
            pltpu.VMEM((4, 2, 24, 128), F32),
            pltpu.VMEM((4, 8, 128), F32),
            pltpu.VMEM((4, 8, 128), F32),
            pltpu.VMEM((4, 3, 8, 128), F32),
            pltpu.VMEM((2, 2, 24, 128), F32),
            pltpu.VMEM((144, 128), F32),
            pltpu.VMEM((72, 128), F32),
            pltpu.VMEM((72, 128), F32),
            pltpu.VMEM((5, 72, 128), F32),
            pltpu.VMEM((2, 72, 128), F32),
            pltpu.VMEM((2, 2, 8, 128), F32),
            pltpu.VMEM((2, 2, 7, 8, 128), F32),
            pltpu.VMEM((8, 128), F32),
            pltpu.VMEM((8, 8, 128), F32),
            pltpu.VMEM((3, 144, 128), F32),
            pltpu.VMEM((144, 128), F32),
            pltpu.VMEM((2, 8, 128), F32),
            pltpu.SemaphoreType.DMA((8,)),
            pltpu.SemaphoreType.DMA,
            pltpu.SemaphoreType.DMA((4, 26)),
            pltpu.SemaphoreType.DMA((4, 26)),
            pltpu.SemaphoreType.DMA((12,)),
            pltpu.SemaphoreType.DMA((11,)),
            pltpu.SemaphoreType.DMA((2, 2, 7)),
            pltpu.SemaphoreType.DMA((2, 2, 7)),
            pltpu.SemaphoreType.DMA((24,)),
            pltpu.SemaphoreType.DMA((8,)),
        ],
        compiler_params=pltpu.CompilerParams(collective_id=0, has_side_effects=True),
        name="step",
    )(
        states.reshape(108, 1, 128),
        previous.reshape(108, 1, 128),
        potential.reshape(108, 128),
        screening.reshape(108, 128),
        occupation.reshape(1, 1),
        cell_scale.reshape(1, 64),
        cell_matrix,
        connectivity.T,
    )
    return filtered.reshape(1, 13824), field.reshape(13824)


def solution(mesh):
    in_specs = (
        P("band", "dom"),
        P("band", "dom"),
        P("dom"),
        P("dom"),
        P("band"),
        P("dom"),
        P(),
        P(None, "dom"),
    )
    out_specs = (P("band", "dom"), P("dom"))
    return jax.shard_map(per_device, mesh=mesh, in_specs=in_specs, out_specs=out_specs, check_vma=False)
```
